32 devices in a mesh: seq: 8 (over z, y), ff: 4 (over x, core).
Axes of the slice: x: 2, y: 2, z: 4, core: 2. Of those that a mesh axis runs over, the one named last changes fastest.
Arguments:
- tokens: bfloat16 [15360, 1024], P(('seq', 'ff')), may hold values from -6 to 6
- cotangent: bfloat16 [15360, 1024], P(('seq', 'ff')), may hold values from -6 to 6
- live_items: int32 [8], P('seq'), may hold values from 16 to 128, as said below
- qkv_weight: bfloat16 [1024, 3072], replicated, may hold values from -0.25 to 0.25
- out_weight: bfloat16 [1024, 1024], replicated, may hold values from -0.375 to 0.375
- up_weight: bfloat16 [1024, 2048], P(None, 'ff'), may hold values from -0.1875 to 0.1875
- down_weight: bfloat16 [2048, 1024], P('ff'), may hold values from -0.125 to 0.125
- gain_one: float32 [1024], replicated, may hold values from 0.5 to 1.5
- shift_one: float32 [1024], replicated, may hold values from -1 to 1
- gain_two: float32 [1024], replicated, may hold values from 0.5 to 1.5
- shift_two: float32 [1024], replicated, may hold values from -1 to 1
Outputs:
- layer_out: bfloat16 [15360, 1024], P(('seq', 'ff'))
- grad_tokens: bfloat16 [15360, 1024], P(('seq', 'ff'))
- grad_qkv_weight: float32 [1024, 3072], P('seq')
- grad_out_weight: float32 [1024, 1024], P('seq')
- grad_up_weight: float32 [1024, 2048], P('seq', 'ff')
- grad_down_weight: float32 [2048, 1024], P('ff', 'seq')
- grad_gain_one: float32 [1024], P('seq')
- grad_shift_one: float32 [1024], P('seq')
- grad_gain_two: float32 [1024], P('seq')
- grad_shift_two: float32 [1024], P('seq')
The draws below stay inside these ranges and needn't reach their ends.
Inputs may be any that keep to these rules, and one draw needn't show every extreme that they name: live_items of a group counts its live items, which stand at the front of the group's 4 * 32 items; in every draw some group is full.
All inputs are finite; a program needn't handle non-finite values.
Results may differ from the reference program's by a relative error of at most 0.015.
Values may be sent and summed in bfloat16 or wider, within the bound.
A program may use at most 192 MiB of HBM per device.

```python
import jax
import jax.numpy as jnp
from jax import lax

D = 1024
HEADS = 8
HEAD_DIM = 128
FF = 2048
ITEM_LEN = 15
ITEMS_DEV = 32
TOKENS = 15360
N_SEQ = 8
N_FF = 4


def draw_live_items(key, part):
    capacity = N_FF * ITEMS_DEV
    key_fill, key_full, key_pick = jax.random.split(key, 3)
    partial_fill = jax.random.randint(key_fill, (N_SEQ,), capacity // 8, capacity)
    full_mask = jax.random.randint(key_full, (N_SEQ,), 0, 2)
    forced = jax.random.randint(key_pick, (), 0, N_SEQ)
    position = jnp.arange(N_SEQ, dtype=jnp.int32)
    filled = jnp.where(full_mask == 1, capacity, partial_fill)
    return jnp.where(position == forced, capacity, filled).astype(jnp.int32)


def block_levels(key, extent, shards, least, high):
    level, own = 1.0, jax.random.fold_in(key, 6)
    for dim, parts in shards:
        heights = jnp.exp(jax.random.uniform(jax.random.fold_in(own, dim), (parts,), jnp.float32, least / len(shards), high / len(shards)))
        level = level * jnp.repeat(heights, extent[dim] // parts).reshape([-1 if axis == dim else 1 for axis in range(len(extent))])
    return level


def noise(rng, extent, scale, limit, cuts=(), held_as=jnp.bfloat16):
    entries = jax.random.normal(rng, extent, jnp.float32) * scale
    if len(cuts) > 0:
        entries = block_levels(rng, extent, cuts, -0.22, 0.18) * entries
    return jnp.clip(entries, min=-limit, max=limit).astype(held_as)


def setup_inputs(seed: int = 0) -> dict:
    arg_keys = jax.random.split(jax.random.key(seed), 12)
    return {
        "tokens": noise(arg_keys[0], (TOKENS, D), 1.0, 6.0, ((0, 32),)),
        "cotangent": noise(arg_keys[1], (TOKENS, D), 1.0, 6.0, ((0, 32),)),
        "live_items": draw_live_items(jax.random.fold_in(arg_keys[11], 71), 0),
        "qkv_weight": noise(arg_keys[3], (D, 3 * D), (D // 2) ** -0.5, 0.25),
        "out_weight": noise(arg_keys[4], (D, D), (D // 4) ** -0.5, 0.375),
        "up_weight": noise(arg_keys[5], (D, FF), D ** -0.5, 0.1875, ((1, 4),)),
        "down_weight": noise(arg_keys[6], (FF, D), FF ** -0.5, 0.125, ((0, 4),)),
        "gain_one": jnp.clip(1.0 + 0.1 * jax.random.normal(arg_keys[7], (D,), jnp.float32), 0.5, 1.5),
        "shift_one": noise(arg_keys[8], (D,), 0.2, 1.0, (), jnp.float32),
        "gain_two": jnp.clip(1.0 + 0.1 * jax.random.normal(arg_keys[9], (D,), jnp.float32), 0.5, 1.5),
        "shift_two": noise(arg_keys[10], (D,), 0.2, 1.0, (), jnp.float32),
    }


@jax.custom_vjp
def low(v):
    return lax.optimization_barrier(v.astype(jnp.bfloat16)).astype(jnp.float32)

@jax.custom_vjp
def low_back(v):
    return v

def low_keep(v):
    return (low(v), None)

def low_pass(kept, grad):
    return (grad,)

def back_keep(v):
    return (v, None)

def back_low(kept, grad):
    return (low(grad),)
low.defvjp(low_keep, low_pass)
low_back.defvjp(back_keep, back_low)

def layer_norm(content_matrix, gain, shift):
    centre = content_matrix - lax.optimization_barrier(jnp.mean(content_matrix, axis=-1, keepdims=True))
    spread = lax.optimization_barrier(jnp.mean(centre * centre, axis=-1, keepdims=True))
    return centre * lax.rsqrt(spread + 1e-05) * gain + shift

def matmul(left, right):
    return jnp.dot(left, right, precision=lax.Precision.HIGHEST)

def forward(weights, inputs, keep_mask):
    qkv_weight, out_weight, up_weight, down_weight, gain_one, shift_one, gain_two, shift_two = weights
    overall_count = inputs.shape[0]
    items = overall_count // ITEM_LEN
    normed = low(layer_norm(inputs, gain_one, shift_one))
    packed = low(low_back(matmul(normed, qkv_weight)))
    packed = packed.reshape(items, ITEM_LEN, 3, HEADS, HEAD_DIM)
    probe_matrix = packed[:, :, 0]
    lookup_matrix = packed[:, :, 1]
    content_matrix = packed[:, :, 2]
    scores = jnp.einsum('nqhd,nkhd->nhqk', probe_matrix, lookup_matrix, precision=lax.Precision.HIGHEST) * HEAD_DIM ** (-0.5)
    scores = low_back(scores)
    causal = jnp.tril(jnp.ones((ITEM_LEN, ITEM_LEN), dtype=bool))
    scores = jnp.where(causal, scores, -1e+30)
    attention_weights = low(jax.nn.softmax(scores, axis=-1))
    mixed_values = jnp.einsum('nhqk,nkhd->nqhd', attention_weights, content_matrix, precision=lax.Precision.HIGHEST)
    mixed_values = low(low_back(mixed_values.reshape(overall_count, HEADS * HEAD_DIM)))
    context_output = low_back(matmul(mixed_values, out_weight))
    middle = inputs + keep_mask * context_output
    normed_two = low(layer_norm(middle, gain_two, shift_two))
    activation_input = low_back(matmul(normed_two, up_weight))
    hidden = low(jax.nn.gelu(activation_input))
    branch = low_back(matmul(hidden, down_weight))
    return middle + keep_mask * branch

def reference(tokens, cotangent, live_items, qkv_weight, out_weight, up_weight, down_weight, gain_one, shift_one, gain_two, shift_two):
    weights = tuple((w.astype(jnp.float32) for w in (qkv_weight, out_weight, up_weight, down_weight, gain_one, shift_one, gain_two, shift_two)))
    group_rows = N_FF * ITEMS_DEV * ITEM_LEN
    inputs = tokens.astype(jnp.float32).reshape(N_SEQ, group_rows, D)
    cotangents = cotangent.astype(jnp.float32).reshape(N_SEQ, group_rows, D)
    item_index = (jnp.arange(group_rows, dtype=jnp.int32) // ITEM_LEN).astype(jnp.int32)

    def group_step(totals, pieces):
        block, block_cot, alive = pieces
        keep_mask = (item_index < alive).astype(jnp.float32)[:, None]
        result, pullback = jax.vjp(lambda w, v: forward(w, v, keep_mask), weights, block)
        grad_weights, grad_block = pullback(block_cot)
        totals = jax.tree.map(lambda a, b: a + b, totals, grad_weights)
        return (totals, (result.astype(jnp.bfloat16), grad_block.astype(jnp.bfloat16)))
    initial = tuple((jnp.zeros(w.shape, jnp.float32) for w in weights))
    totals, outputs = lax.scan(group_step, initial, (inputs, cotangents, live_items))
    layer_out = outputs[0].reshape(TOKENS, D)
    grad_tokens = outputs[1].reshape(TOKENS, D)
    return (layer_out, grad_tokens, totals[0], totals[1], totals[2], totals[3], totals[4], totals[5], totals[6], totals[7])
```

```python
import jax
import jax.numpy as jnp
from jax import lax
from jax.sharding import PartitionSpec as P

HEADS = 8
HEAD_DIM = 128
ITEM_LEN = 15
BF = jnp.bfloat16
F32 = jnp.float32


def layer_norm(content_matrix, gain, shift):
    centre = content_matrix - jnp.mean(content_matrix, axis=-1, keepdims=True)
    spread = jnp.mean(centre * centre, axis=-1, keepdims=True)
    return centre * lax.rsqrt(spread + 1e-05) * gain + shift


def tile_allowed(tile_rows):
    position = jnp.arange(tile_rows, dtype=jnp.int32)
    same_item = position[:, None] // ITEM_LEN == position[None, :] // ITEM_LEN
    return same_item & (position[None, :] <= position[:, None])


def dot(a, b):
    return jnp.dot(a, b, preferred_element_type=F32)


def tiles_of(x, tile):
    return x.reshape(-1, tile, HEAD_DIM)


def scores_of(q, k, allowed):
    s = jnp.einsum("tqd,tkd->tqk", q, k, preferred_element_type=F32) * HEAD_DIM ** (-0.5)
    return jnp.where(allowed, s, -1e30)


def attend_forward(packed, tile):
    allowed = tile_allowed(tile)
    width = HEADS * HEAD_DIM
    mixed, saved = [], []
    for h in range(HEADS):
        q, k, v = (tiles_of(packed[:, p * width + h * HEAD_DIM:][:, :HEAD_DIM], tile) for p in range(3))
        probs = jax.nn.softmax(scores_of(q, k, allowed), axis=-1)
        o = jnp.einsum("tqk,tkd->tqd", probs.astype(BF), v, preferred_element_type=F32)
        mixed.append(o.astype(BF).reshape(-1, HEAD_DIM))
        saved.append(probs)
    return jnp.concatenate(mixed, axis=1), saved


def attend_backward(packed, saved, grad_mixed, tile):
    width = HEADS * HEAD_DIM
    scale = HEAD_DIM ** (-0.5)
    parts = ([], [], [])
    for h in range(HEADS):
        q, k, v = (tiles_of(packed[:, p * width + h * HEAD_DIM:][:, :HEAD_DIM], tile) for p in range(3))
        o = tiles_of(grad_mixed[:, h * HEAD_DIM:][:, :HEAD_DIM], tile)
        probs = saved[h]
        dp = jnp.einsum("tqd,tkd->tqk", o, v, preferred_element_type=F32)
        gv = jnp.einsum("tqk,tqd->tkd", probs.astype(BF), o, preferred_element_type=F32)
        gs = (probs * (dp - jnp.sum(probs * dp, axis=-1, keepdims=True))).astype(BF)
        gq = jnp.einsum("tqk,tkd->tqd", gs, k, preferred_element_type=F32) * scale
        gk = jnp.einsum("tqk,tqd->tkd", gs, q, preferred_element_type=F32) * scale
        for part, g in zip(parts, (gq, gk, gv)):
            part.append(g.astype(BF).reshape(-1, HEAD_DIM))
    return jnp.concatenate(parts[0] + parts[1] + parts[2], axis=1)


def general(
    tokens, cotangent, live_items, qkv_weight, out_weight, up_weight, down_weight,
    gain_one, shift_one, gain_two, shift_two,
):
    rows = tokens.shape[0]
    items = rows // ITEM_LEN
    tile = ITEM_LEN * (16 if items % 16 == 0 else 1)
    place = lax.axis_index("ff") * items + jnp.arange(rows, dtype=jnp.int32) // ITEM_LEN
    keep = (place < live_items[0]).astype(F32)[:, None]
    up_all = lax.all_gather(up_weight, "ff", axis=1, tiled=True)
    down_all = lax.all_gather(down_weight, "ff", axis=0, tiled=True)
    inputs = tokens.astype(F32)
    normed, norm_one_pull = jax.vjp(layer_norm, inputs, gain_one, shift_one)
    normed = normed.astype(BF)
    packed = dot(normed, qkv_weight).astype(BF)
    mixed, saved = attend_forward(packed, tile)
    middle = inputs + keep * dot(mixed, out_weight)
    normed_two, norm_two_pull = jax.vjp(layer_norm, middle, gain_two, shift_two)
    normed_two = normed_two.astype(BF)
    grad_out = cotangent.astype(F32)
    grad_branch = (keep * grad_out).astype(BF)
    pre = dot(normed_two, up_all)
    hidden = jax.nn.gelu(pre).astype(BF)
    layer_out = (middle + keep * dot(hidden, down_all)).astype(BF)
    grad_hidden = dot(grad_branch, down_all.T)
    grad_pre = jax.vjp(jax.nn.gelu, pre)[1](grad_hidden)[0].astype(BF)
    grad_down = dot(hidden.T, grad_branch).astype(BF)
    grad_up = dot(normed_two.T, grad_pre).astype(BF)
    grad_middle_norm, grad_gain_two, grad_shift_two = norm_two_pull(dot(grad_pre, up_all.T))
    grad_middle = grad_out + grad_middle_norm
    grad_attended = (keep * grad_middle).astype(BF)
    grad_out_weight = dot(mixed.T, grad_attended).astype(BF)
    grad_mixed = dot(grad_attended, out_weight.T).astype(BF)
    grad_packed = attend_backward(packed, saved, grad_mixed, tile)
    grad_qkv = dot(normed.T, grad_packed).astype(BF)
    grad_inputs, grad_gain_one, grad_shift_one = norm_one_pull(dot(grad_packed, qkv_weight.T))
    grad_tokens = (grad_middle + grad_inputs).astype(BF)

    def scatter(x, axis, dim):
        return lax.psum_scatter(x, axis, scatter_dimension=dim, tiled=True)

    grad_up = scatter(scatter(grad_up, "ff", 1), "seq", 0).astype(F32)
    grad_down = scatter(scatter(grad_down, "ff", 0), "seq", 1).astype(F32)
    shared = [
        lax.psum(scatter(g, "seq", 0), "ff").astype(F32)
        for g in (grad_qkv, grad_out_weight, grad_gain_one, grad_shift_one, grad_gain_two, grad_shift_two)
    ]
    return (layer_out, grad_tokens, shared[0], shared[1], grad_up, grad_down, *shared[2:])


IN_SPECS = (
    P(("seq", "ff"), None), P(("seq", "ff"), None), P("seq"), P(), P(), P(None, "ff"), P("ff", None),
    P(), P(), P(), P(),
)
OUT_SPECS = (
    P(("seq", "ff"), None), P(("seq", "ff"), None), P("seq", None), P("seq", None), P("seq", "ff"),
    P("ff", "seq"), P("seq"), P("seq"), P("seq"), P("seq"),
)


def solution(mesh):
    return jax.shard_map(general, mesh=mesh, in_specs=IN_SPECS, out_specs=OUT_SPECS, check_vma=False)
```

```python
import jax
import jax.numpy as jnp
from jax import lax
from jax.experimental import pallas as pl
from jax.experimental.pallas import tpu as pltpu
from jax.sharding import PartitionSpec as P

HEADS = 8
HEAD_DIM = 128
ITEM_LEN = 15
BF = jnp.bfloat16
F32 = jnp.float32


def layer_norm(content_matrix, gain, shift):
    centre = content_matrix - jnp.mean(content_matrix, axis=-1, keepdims=True)
    spread = jnp.mean(centre * centre, axis=-1, keepdims=True)
    return centre * lax.rsqrt(spread + 1e-05) * gain + shift


def tile_allowed(tile_rows):
    position = jnp.arange(tile_rows, dtype=jnp.int32)
    same_item = position[:, None] // ITEM_LEN == position[None, :] // ITEM_LEN
    return same_item & (position[None, :] <= position[:, None])


def dot(a, b):
    return jnp.dot(a, b, preferred_element_type=F32)


def tiles_of(x, tile):
    return x.reshape(-1, tile, HEAD_DIM)


def scores_of(q, k, allowed):
    s = jnp.einsum("tqd,tkd->tqk", q, k, preferred_element_type=F32) * HEAD_DIM ** (-0.5)
    return jnp.where(allowed, s, -1e30)


def attend_forward(packed, tile):
    allowed = tile_allowed(tile)
    width = HEADS * HEAD_DIM
    mixed, saved = [], []
    for h in range(HEADS):
        q, k, v = (tiles_of(packed[:, p * width + h * HEAD_DIM:][:, :HEAD_DIM], tile) for p in range(3))
        probs = jax.nn.softmax(scores_of(q, k, allowed), axis=-1)
        o = jnp.einsum("tqk,tkd->tqd", probs.astype(BF), v, preferred_element_type=F32)
        mixed.append(o.astype(BF).reshape(-1, HEAD_DIM))
        saved.append(probs)
    return jnp.concatenate(mixed, axis=1), saved


def attend_backward(packed, saved, grad_mixed, tile):
    width = HEADS * HEAD_DIM
    scale = HEAD_DIM ** (-0.5)
    parts = ([], [], [])
    for h in range(HEADS):
        q, k, v = (tiles_of(packed[:, p * width + h * HEAD_DIM:][:, :HEAD_DIM], tile) for p in range(3))
        o = tiles_of(grad_mixed[:, h * HEAD_DIM:][:, :HEAD_DIM], tile)
        probs = saved[h]
        dp = jnp.einsum("tqd,tkd->tqk", o, v, preferred_element_type=F32)
        gv = jnp.einsum("tqk,tqd->tkd", probs.astype(BF), o, preferred_element_type=F32)
        gs = (probs * (dp - jnp.sum(probs * dp, axis=-1, keepdims=True))).astype(BF)
        gq = jnp.einsum("tqk,tkd->tqd", gs, k, preferred_element_type=F32) * scale
        gk = jnp.einsum("tqk,tqd->tkd", gs, q, preferred_element_type=F32) * scale
        for part, g in zip(parts, (gq, gk, gv)):
            part.append(g.astype(BF).reshape(-1, HEAD_DIM))
    return jnp.concatenate(parts[0] + parts[1] + parts[2], axis=1)


def general(
    tokens, cotangent, live_items, qkv_weight, out_weight, up_weight, down_weight,
    gain_one, shift_one, gain_two, shift_two,
):
    rows = tokens.shape[0]
    items = rows // ITEM_LEN
    tile = ITEM_LEN * (16 if items % 16 == 0 else 1)
    place = lax.axis_index("ff") * items + jnp.arange(rows, dtype=jnp.int32) // ITEM_LEN
    keep = (place < live_items[0]).astype(F32)[:, None]
    up_all = lax.all_gather(up_weight, "ff", axis=1, tiled=True)
    down_all = lax.all_gather(down_weight, "ff", axis=0, tiled=True)
    inputs = tokens.astype(F32)
    normed, norm_one_pull = jax.vjp(layer_norm, inputs, gain_one, shift_one)
    normed = normed.astype(BF)
    packed = dot(normed, qkv_weight).astype(BF)
    mixed, saved = attend_forward(packed, tile)
    middle = inputs + keep * dot(mixed, out_weight)
    normed_two, norm_two_pull = jax.vjp(layer_norm, middle, gain_two, shift_two)
    normed_two = normed_two.astype(BF)
    grad_out = cotangent.astype(F32)
    grad_branch = (keep * grad_out).astype(BF)
    pre = dot(normed_two, up_all)
    hidden = jax.nn.gelu(pre).astype(BF)
    layer_out = (middle + keep * dot(hidden, down_all)).astype(BF)
    grad_hidden = dot(grad_branch, down_all.T)
    grad_pre = jax.vjp(jax.nn.gelu, pre)[1](grad_hidden)[0].astype(BF)
    grad_down = dot(hidden.T, grad_branch).astype(BF)
    grad_up = dot(normed_two.T, grad_pre).astype(BF)
    grad_middle_norm, grad_gain_two, grad_shift_two = norm_two_pull(dot(grad_pre, up_all.T))
    grad_middle = grad_out + grad_middle_norm
    grad_attended = (keep * grad_middle).astype(BF)
    grad_out_weight = dot(mixed.T, grad_attended).astype(BF)
    grad_mixed = dot(grad_attended, out_weight.T).astype(BF)
    grad_packed = attend_backward(packed, saved, grad_mixed, tile)
    grad_qkv = dot(normed.T, grad_packed).astype(BF)
    grad_inputs, grad_gain_one, grad_shift_one = norm_one_pull(dot(grad_packed, qkv_weight.T))
    grad_tokens = (grad_middle + grad_inputs).astype(BF)

    def scatter(x, axis, dim):
        return lax.psum_scatter(x, axis, scatter_dimension=dim, tiled=True)

    grad_up = scatter(scatter(grad_up, "ff", 1), "seq", 0).astype(F32)
    grad_down = scatter(scatter(grad_down, "ff", 0), "seq", 1).astype(F32)
    shared = [
        lax.psum(scatter(g, "seq", 0), "ff").astype(F32)
        for g in (grad_qkv, grad_out_weight, grad_gain_one, grad_shift_one, grad_gain_two, grad_shift_two)
    ]
    return (layer_out, grad_tokens, shared[0], shared[1], grad_up, grad_down, *shared[2:])


MESH = pl.DeviceIdType.MESH
ROWS, PAD, D, FF, SHARD = 480, 512, 1024, 2048, 512
TILE = 240
WIDE = 256
STEP = 32
UP0, UP1, DN0, DN1, OUT, QS, KS, VS = range(8)
ORDER = {
    UP0: "lyxh", UP1: "ylxh", DN0: "lxyh", DN1: "xylh", OUT: "xylh", QS: "xlyh", KS: "yxlh", VS: "lyxh",
}
EYES = "xhly"
M_UPC, M_DNC = 0, 1
M_WX, M_WL, M_WCX, M_WCL = 2, 6, 10, 14
M_GBT, M_N2T, M_MXT, M_N1T, M_GA = 18, 19, 20, 21, 22
M_HID, M_GPR = 23, 25
M_PK = 27
M_RED = 33
M_AGC, M_AGX, M_AGF = 73, 77, 81
M_VEC = 85
N_MSG = 90


def dot_nt(a, b):
    return lax.dot_general(a, b, (((1,), (1,)), ((), ())), preferred_element_type=F32)


def layer_kernel(
    tok_h, cot_h, live, wq_h, wo_h, up_h, dn_h, g1, s1, g2, s2,
    lo_h, gt_h, gqkv_h, gout_h, gup_o, gdn_o, gg1_o, gs1_o, gg2_o, gs2_o,
    wq, wo, upa, dna, tok, gb, nb, mx, pk, pks, xgb, xn2, xmx, xn1, probs, mask, mid, gm, facc,
    hids, gprs, ga, gas, gw, r0, r1, r2, r3, vsum, vbuf, vrecv, ssem, rsem, lsem,
):
    s, f = lax.axis_index("seq"), lax.axis_index("ff")
    bit = {"h": s // 4, "l": (s // 2) % 2, "y": s % 2, "x": f // 2, "c": f % 2}
    mate = {
        "h": (s + 4 - 8 * bit["h"], f), "l": (s + 2 - 4 * bit["l"], f), "y": (s + 1 - 2 * bit["y"], f),
        "x": (s, f + 2 - 4 * bit["x"]), "c": (s, f + 1 - 2 * bit["c"]),
    }
    x, c = bit["x"], bit["c"]

    def at(base, size, unit=128):
        return pl.ds(pl.multiple_of(base, unit), size)

    def local(i, src, dst):
        return pltpu.make_async_copy(src, dst, lsem.at[i])

    loads = {
        0: (tok_h, tok), 1: (cot_h, gb.at[0:ROWS]), 2: (wq_h, wq), 3: (wo_h, wo), 4: (up_h, upa.at[:, 0:SHARD]),
        5: (dn_h, dna.at[0:SHARD]), 6: (cot_h, nb.at[0:ROWS]), 7: (wq_h, wq),
        8: (nb.at[0:ROWS], lo_h), 9: (tok, gt_h), 10: (gm.at[0:128], gout_h),
        11: (facc.at[0:128], gqkv_h.at[:, 0:D]), 12: (facc.at[128:256], gqkv_h.at[:, D:2 * D]),
        13: (facc.at[256:384], gqkv_h.at[:, 2 * D:3 * D]),
    }

    def load(i):
        local(i, *loads[i]).start()

    def loaded(i):
        local(i, *loads[i]).wait()

    def remote(i, to, src, dst):
        return pltpu.make_async_remote_copy(
            src_ref=src, dst_ref=dst, send_sem=ssem.at[i], recv_sem=rsem.at[i], device_id=mate[to], device_id_type=MESH
        )

    def quarter(k, own, slot, whole):
        half = bit["l"] if own else 1 - bit["l"]
        if k < 2:
            rows = at(half * 512 + k * 256, 256)
            return (up_h.at[rows, :] if whole else upa.at[rows, slot * SHARD:(slot + 1) * SHARD])
        start = half * 256 + (k - 2) * 128
        return dn_h.at[at(start, 128), :] if whole else dna.at[at(slot * SHARD + start, 128), :]

    def weight_x(k):
        half_mate = quarter(k, True, 2, True)
        return remote(M_WX + k, "x", half_mate, quarter(k, True, 2, False))

    def weight_l(k):
        ref = quarter(k, True, 2, False)
        return remote(M_WL + k, "l", ref, ref)

    def weight_cx(k):
        return remote(M_WCX + k, "c", quarter(k, True, 2, False), quarter(k, True, 3, False))

    def weight_cl(k):
        return remote(M_WCL + k, "c", quarter(k, False, 2, False), quarter(k, False, 3, False))

    def relay_x(k):
        weight_x(k).wait()
        weight_l(k).start()
        weight_cx(k).start()

    def relay_l(k):
        weight_l(k).wait()
        weight_cl(k).start()

    def weight_c(which):
        if which == 0:
            return remote(M_UPC, "c", up_h, upa.at[:, SHARD:2 * SHARD])
        return remote(M_DNC, "c", dn_h, dna.at[SHARD:2 * SHARD])

    def turned(i, ref):
        return remote(i, "c", ref.at[:, 0:PAD], ref.at[:, PAD:2 * PAD])

    def own_hid(slot):
        return wq.at[0:PAD, at(slot * SHARD, SHARD)]

    def own_gpr(slot):
        return wq.at[PAD:2 * PAD, at(slot * SHARD, SHARD)]

    def hid_copy(g):
        return remote(M_HID + g, "c", own_hid(2 * g + 1), hids.at[:, at(g * SHARD, SHARD)])

    def gpr_copy(g):
        return remote(M_GPR + g, "c", own_gpr(2 * g + 1), gprs.at[:, at(g * SHARD, SHARD)])

    def ga_copy():
        return remote(M_GA, "c", ga.at[:, at((1 - c) * 512, 512)], gas)

    def pk_copy(n, xb, part):
        return remote(
            M_PK + n * 3 + part, "c", pk.at[:, at(part * D + (1 - c) * 512 + xb * WIDE, WIDE)],
            pks.at[:, at(part * 512 + xb * WIDE, WIDE)],
        )

    landing = (r0, r1, r2, r3)

    def bits_of(p):
        if p < OUT:
            return {**bit, "x": 0}
        return bit

    def chosen(p, k, mine, xb=None):
        own, order, index = bits_of(p), ORDER[p], []
        for e in EYES:
            if e in order[:k]:
                index.append(own[e])
            elif e == order[k]:
                index.append(own[e] if mine else 1 - own[e])
            elif e == "x" and xb is not None:
                index.append(xb)
            else:
                index.append(slice(None))
        return index

    def red(p, k, xb=None, part=0):
        dst = landing[k].at[p] if xb is None else landing[k].at[p, xb]
        return remote(
            M_RED + p * 5 + (k + 1 if k else part), ORDER[p][k], gw.at[(p, *chosen(p, k, False, xb))], dst
        )

    def add(p, k, xb=None):
        index = chosen(p, k, True, xb)
        free = [n for n, e in enumerate(index) if isinstance(e, slice)]
        count = len(free)

        def body(i, _):
            place = [(i // (1 << (count - 1 - n))) % 2 for n in range(count)]
            full = list(index)
            for n, e in zip(free, place):
                full[n] = e
            lead = (p, *place) if xb is None else (p, xb, *place)
            gw[(p, *full)] = (gw[(p, *full)].astype(F32) + landing[k][lead].astype(F32)).astype(BF)
            return 0

        lax.fori_loop(0, 1 << count, body, 0)

    def first(p, xb, part):
        if ORDER[p][0] != "x":
            red(p, 0, xb, part).start()
        elif isinstance(xb, int):
            if xb == 1:
                red(p, 0).start()
        elif part == 0:
            red(p, 0).start()

    def first_done(p, xb, part):
        red(p, 0, xb, part).wait()
        add(p, 0, xb)

    def done(p, k):
        red(p, k).wait()
        add(p, k)

    def step(p, k):
        done(p, k)
        red(p, k + 1).start()

    def result(p):
        red(p, 3).wait()
        own = bits_of(p)
        return gw[(p, *(own[e] for e in EYES))].astype(F32) + r3[p].astype(F32)

    def quarters(q, n):
        return xgb.at[q * 128:(q + 1) * 128, at(n * WIDE, WIDE)]

    own_quarter = 2 * c + x

    def gather_c(q):
        return remote(M_AGC + q, "c", quarters(q, own_quarter), quarters(q, own_quarter))

    def gather_x(q):
        return remote(M_AGX + q, "x", quarters(q, own_quarter), quarters(q, own_quarter))

    def gather_f(q):
        other = 2 * c + 1 - x
        return remote(M_AGF + q, "c", quarters(q, other), quarters(q, other))

    limit = (live[0] - f * (ROWS // 15)) * 15

    def keep_of(r):
        rows = r * STEP + lax.broadcasted_iota(jnp.int32, (STEP, 1), 0)
        return jnp.where(rows < limit, 1.0, 0.0).astype(F32)

    def block(r):
        return pl.ds(pl.multiple_of(r * STEP, STEP), STEP)

    def centred(v):
        centre = v - jnp.mean(v, axis=-1, keepdims=True)
        rstd = lax.rsqrt(jnp.mean(centre * centre, axis=-1, keepdims=True) + 1e-05)
        return centre * rstd, rstd

    def turn(src, dst):
        def body(j, _):
            cols = at(j * 128, 128)
            dst[cols, 0:PAD] = src[:, cols].T
            return 0

        lax.fori_loop(0, D // 128, body, 0)

    for i in range(6):
        load(i)
    barrier = pltpu.get_barrier_semaphore()
    for e in "xylhc":
        pl.semaphore_signal(barrier, inc=1, device_id=mate[e], device_id_type=MESH)
    for ref in (gb, nb, mx, ga):
        ref[ROWS:PAD, :] = jnp.zeros((PAD - ROWS, D), BF)
    pk[ROWS:PAD, :] = jnp.zeros((PAD - ROWS, 3 * D), BF)
    vsum[...] = jnp.zeros(vsum.shape, F32)
    qi = lax.broadcasted_iota(jnp.int32, (TILE, TILE), 0)
    ki = lax.broadcasted_iota(jnp.int32, (TILE, TILE), 1)
    mask[...] = jnp.where((ki <= qi) & (ki >= qi - lax.rem(qi, 15)), 0.0, -1e30).astype(F32)

    loaded(0)

    def norm_one(r, _):
        xhat, _r = centred(tok[block(r), :].astype(F32))
        nb[block(r), :] = (xhat * g1[...] + s1[...]).astype(BF)
        return 0

    lax.fori_loop(0, ROWS // STEP, norm_one, 0)
    pl.semaphore_wait(barrier, 5)
    for k in range(4):
        weight_x(k).start()
    weight_c(0).start()
    weight_c(1).start()

    loaded(2)

    def qkv(n, _):
        cols = at(n * 512, 512)
        pk[0:ROWS, cols] = jnp.dot(nb[0:ROWS, :], wq[:, cols], preferred_element_type=F32).astype(BF)
        return 0

    lax.fori_loop(0, 6, qkv, 0)
    turn(nb, xn1)
    turned(M_N1T, xn1).start()

    loaded(1)

    def mask_cot(r, _):
        gb[block(r), :] = (keep_of(r) * gb[block(r), :].astype(F32)).astype(BF)
        return 0

    lax.fori_loop(0, ROWS // STEP, mask_cot, 0)
    turn(gb, xgb)
    turned(M_GBT, xgb).start()

    def attend(h, _):
        cols = [at(part * D + h * 128, 128) for part in range(3)]
        for t in range(2):
            rows = slice(t * TILE, (t + 1) * TILE)
            sc = dot_nt(pk[rows, cols[0]], pk[rows, cols[1]]) * (128 ** -0.5) + mask[...]
            w = jnp.exp(sc - jnp.max(sc, axis=-1, keepdims=True))
            p = (w * (1.0 / jnp.sum(w, axis=-1, keepdims=True))).astype(BF)
            probs[h * 2 + t] = p
            mx[rows, at(h * 128, 128)] = jnp.dot(p, pk[rows, cols[2]], preferred_element_type=F32).astype(BF)
        return 0

    lax.fori_loop(0, 8, attend, 0)
    relay_x(0)
    turn(mx, xmx)
    turned(M_MXT, xmx).start()

    loaded(3)

    def project(n, _):
        cols = at(n * 512, 512)
        facc[:, cols] = jnp.dot(mx[0:ROWS, :], wo[:, cols], preferred_element_type=F32)
        return 0

    lax.fori_loop(0, 2, project, 0)

    def norm_two(r, _):
        m = tok[block(r), :].astype(F32) + keep_of(r) * facc[block(r), :]
        mid[block(r), :] = m
        xhat, _r = centred(m)
        nb[block(r), :] = (xhat * g2[...] + s2[...]).astype(BF)
        return 0

    lax.fori_loop(0, ROWS // STEP, norm_two, 0)
    relay_x(1)
    turn(nb, xn2)
    turned(M_N2T, xn2).start()

    loaded(4)
    loaded(5)
    weight_c(0).wait()
    weight_c(1).wait()
    wq[ROWS:PAD, 0:FF] = jnp.zeros((PAD - ROWS, FF), BF)
    wq[PAD + ROWS:2 * PAD, 0:FF] = jnp.zeros((PAD - ROWS, FF), BF)

    def shard(j):
        cols = at(j * SHARD, SHARD)
        pre = jnp.dot(nb[0:ROWS, :], upa[:, cols], preferred_element_type=F32)
        sq = pre * pre
        t = jnp.tanh(0.7978845608028654 * pre * (1.0 + 0.044715 * sq))
        half = 0.5 * (1.0 + t)
        wq[0:ROWS, cols] = (pre * half).astype(BF)
        slope = half + 0.5 * pre * (1.0 - t * t) * (0.7978845608028654 * (1.0 + 0.134145 * sq))
        gh = dot_nt(gb[0:ROWS, :], dna[cols, :])
        wq[PAD:PAD + ROWS, cols] = (gh * slope).astype(BF)

    def group(g, _):
        @pl.when(g == 1)
        def _():
            for k in range(4):
                weight_cx(k).wait()
                weight_cl(k).wait()

        def one(n, _):
            shard(2 * g + 1 - n)

            @pl.when(n == 0)
            def _():
                hid_copy(g).start()
                gpr_copy(g).start()

                @pl.when(g == 0)
                def _():
                    relay_x(2)
                    relay_l(0)
                    relay_l(1)

            return 0

        lax.fori_loop(0, 2, one, 0)

        @pl.when(g == 0)
        def _():
            relay_x(3)
            relay_l(2)
            turned(M_N2T, xn2).wait()
            turned(M_GBT, xgb).wait()

        hid_copy(g).wait()
        gpr_copy(g).wait()
        mine, theirs = at(2 * g * SHARD, SHARD), at(g * SHARD, SHARD)

        def sums(n, _):
            rows = at(n * 512, 512)
            for lhs, top, low, p in ((xn2, PAD, gprs, UP0), (xgb, 0, hids, DN0)):
                rhs = jnp.concatenate([wq[top:top + PAD, mine], low[:, theirs]], axis=0)
                total = jnp.dot(lhs[rows, :], rhs, preferred_element_type=F32).astype(BF)
                for half in range(2):
                    gw[p + half, g, n] = total[:, half * WIDE:(half + 1) * WIDE].reshape(2, 2, 128, WIDE)
            return 0

        lax.fori_loop(0, 2, sums, 0)

        @pl.when(g == 0)
        def _():
            for p in (UP0, UP1, DN0, DN1):
                first(p, 0, 0)
            relay_l(3)

        @pl.when(g == 1)
        def _():
            for p in (DN1, UP0, UP1, DN0):
                first(p, 1, 1)

        return 0

    lax.fori_loop(0, 2, group, 0)
    load(6)

    def back_up(n, _):
        cols = at(n * 512, 512)
        facc[:, cols] = dot_nt(wq[PAD:PAD + ROWS, 0:FF], upa[cols, :])
        return 0

    lax.fori_loop(0, 2, back_up, 0)
    for p in (UP0, UP1, DN0):
        first_done(p, 0, 0)
    loaded(6)

    def row_sum(v):
        total = v[0:8]
        for n in range(1, STEP // 8):
            total = total + v[n * 8:(n + 1) * 8]
        return total

    def norm_back(v, gn, gain, n):
        xhat, rstd = centred(v)
        vsum[n] += row_sum(gn * xhat)
        vsum[n + 1] += row_sum(gn)
        e = gn * gain
        return rstd * (e - jnp.mean(e, axis=-1, keepdims=True) - xhat * jnp.mean(e * xhat, axis=-1, keepdims=True))

    def norm_two_back(r, _):
        total = nb[block(r), :].astype(F32) + norm_back(mid[block(r), :], facc[block(r), :], g2[...], 2)
        gm[block(r), :] = total
        ga[block(r), :] = (keep_of(r) * total).astype(BF)
        return 0

    lax.fori_loop(0, ROWS // STEP, norm_two_back, 0)
    ga_copy().start()

    def back_out(n, _):
        cols = at(n * 512, 512)
        mx[0:ROWS, cols] = dot_nt(ga[0:ROWS, :], wo[cols, :]).astype(BF)
        return 0

    turned(M_MXT, xmx).wait()
    lax.fori_loop(0, 2, back_out, 0)
    ga_copy().wait()

    def out_sums(n, _):
        rows = at(n * 512, 512)
        rhs = jnp.concatenate([ga[:, at(c * 512, 512)], gas[...]], axis=0)
        total = jnp.dot(xmx[rows, :], rhs, preferred_element_type=F32).astype(BF)
        for half in range(2):
            gw[OUT, half, n] = total[:, half * WIDE:(half + 1) * WIDE].reshape(2, 2, 128, WIDE)
        return 0

    lax.fori_loop(0, 2, out_sums, 0)
    red(OUT, 0).start()
    for p in (UP0, UP1, DN0):
        first_done(p, 1, 1)
        red(p, 1).start()
    turned(M_N1T, xn1).wait()

    def head_back(h):
        cols = [at(part * D + h * 128, 128) for part in range(3)]
        for t in range(2):
            rows = slice(t * TILE, (t + 1) * TILE)
            q, k, v = (pk[rows, col] for col in cols)
            o = mx[rows, at(h * 128, 128)]
            pb = probs[h * 2 + t]
            p = pb.astype(F32)
            dp = dot_nt(o, v)
            gs = (p * (dp - jnp.sum(p * dp, axis=-1, keepdims=True))).astype(BF)
            gv = lax.dot_general(pb, o, (((0,), (0,)), ((), ())), preferred_element_type=F32)
            gq = jnp.dot(gs, k, preferred_element_type=F32) * (128 ** -0.5)
            gk = lax.dot_general(gs, q, (((0,), (0,)), ((), ())), preferred_element_type=F32) * (128 ** -0.5)
            for col, g in zip(cols, (gq, gk, gv)):
                pk[rows, col] = g.astype(BF)

    def pair(i, _):
        cb = lax.rem(i + 1 + c, 2)
        later = i // 2
        xb = lax.rem(later + 1 + x, 2)

        def one(n, _):
            head_back(cb * 4 + xb * 2 + n)
            return 0

        lax.fori_loop(0, 2, one, 0)

        for n in range(2):
            xn = 1 - x if n == 0 else x

            @pl.when(i == 2 * n)
            def _():
                for part in range(3):
                    pk_copy(n, xn, part).start()

        def qkv_sums():
            def body(n, _):
                rows = at(n * 512, 512)
                rhs = jnp.concatenate(
                    [
                        jnp.concatenate([pk[:, at(part * D + c * 512 + xb * WIDE, WIDE)] for part in range(3)], axis=1),
                        jnp.concatenate([pks[:, at(part * 512 + xb * WIDE, WIDE)] for part in range(3)], axis=1),
                    ],
                    axis=0,
                )
                total = jnp.dot(xn1[rows, :], rhs, preferred_element_type=F32).astype(BF)
                for part in range(3):
                    gw[QS + part, xb, n] = total[:, part * WIDE:(part + 1) * WIDE].reshape(2, 2, 128, WIDE)
                return 0

            lax.fori_loop(0, 2, body, 0)

        @pl.when(i % 2 == 1)
        def _():
            for n in range(2):
                xn = 1 - x if n == 0 else x

                @pl.when(later == n)
                def _():
                    for part in range(3):
                        pk_copy(n, xn, part).wait()

            qkv_sums()

        @pl.when(i == 1)
        def _():
            for p in (QS, KS, VS):
                first(p, 1 - x, 0)
            step(DN1, 0)

        @pl.when(i == 3)
        def _():
            for p in (QS, KS, VS):
                first(p, x, 1)

        return 0

    lax.fori_loop(0, 4, pair, 0)
    for p in (UP0, UP1, DN0):
        step(p, 1)
    step(OUT, 0)

    def down(n, _):
        cols = at(n * 512, 512)
        facc[:, cols] = jnp.dot(wq[0:ROWS, 0:FF], dna[:, cols], preferred_element_type=F32)
        return 0

    lax.fori_loop(0, 2, down, 0)
    load(7)

    def finish_out(r, _):
        nb[block(r), :] = (mid[block(r), :] + keep_of(r) * facc[block(r), :]).astype(BF)
        return 0

    lax.fori_loop(0, ROWS // STEP, finish_out, 0)
    load(8)
    step(DN1, 1)
    for p in (KS, VS):
        first_done(p, 1 - x, 0)
    step(QS, 0)
    loaded(7)

    def back_qkv(n, _):
        cols = at(n * 512, 512)
        facc[:, cols] = dot_nt(pk[0:ROWS, :], wq[cols, :])
        return 0

    lax.fori_loop(0, 2, back_qkv, 0)

    def norm_one_back(r, _):
        total = gm[block(r), :] + norm_back(tok[block(r), :].astype(F32), facc[block(r), :], g1[...], 0)
        tok[block(r), :] = total.astype(BF)
        return 0

    lax.fori_loop(0, ROWS // STEP, norm_one_back, 0)
    load(9)

    vbuf[0] = jnp.concatenate(
        [jnp.sum(vsum[n], axis=0, keepdims=True) for n in range(4)] + [jnp.zeros((4, D), F32)], axis=0
    )

    def vec(n):
        return remote(M_VEC + n, "cxylh"[n], vbuf.at[n], vrecv.at[n])

    def vec_step(n):
        vec(n).wait()
        vbuf[n + 1] = vbuf[n] + vrecv[n]
        if n < 4:
            vec(n + 1).start()

    vec(0).start()
    for p in (KS, VS):
        first_done(p, x, 1)
        red(p, 1).start()
    vec_step(0)
    for p in (UP0, UP1, DN0, DN1):
        step(p, 2)
    step(OUT, 1)
    step(QS, 1)
    vec_step(1)
    step(KS, 1)
    step(VS, 1)
    step(OUT, 2)
    vec_step(2)
    for half in range(2):
        gup_o[:, half * WIDE:(half + 1) * WIDE] = result(UP0 + half)
    for half in range(2):
        gdn_o[half * WIDE:(half + 1) * WIDE, :] = result(DN0 + half).T
    vec_step(3)

    def share(p):
        quarters(p - OUT, own_quarter)[...] = result(p).astype(BF)
        gather_c(p - OUT).start()
        gather_x(p - OUT).start()

    def pass_on(p):
        gather_x(p - OUT).wait()
        gather_f(p - OUT).start()

    def write(p, dst, base):
        gather_c(p - OUT).wait()
        gather_f(p - OUT).wait()
        q = p - OUT
        dst[base:base + 128, :] = xgb[q * 128:(q + 1) * 128, :].astype(F32)

    share(OUT)
    step(QS, 2)
    step(KS, 2)
    step(VS, 2)
    vec_step(4)
    pass_on(OUT)
    for n, ref in enumerate((gg1_o, gs1_o, gg2_o, gs2_o)):
        ref[...] = vbuf[5, n:n + 1, at(s * 128, 128)]
    share(QS)
    share(KS)
    share(VS)
    write(OUT, gm, 0)
    load(10)
    pass_on(QS)
    pass_on(KS)
    pass_on(VS)
    for n, p in enumerate((QS, KS, VS)):
        write(p, facc, 128 * n)
        load(11 + n)
    for i in range(8, 14):
        loaded(i)


def fused(
    tokens, cotangent, live_items, qkv_weight, out_weight, up_weight, down_weight,
    gain_one, shift_one, gain_two, shift_two,
):
    rows_of = [v.reshape(1, D) for v in (gain_one, shift_one, gain_two, shift_two)]
    hbm, vmem = pl.BlockSpec(memory_space=pl.ANY), pl.BlockSpec(memory_space=pltpu.VMEM)
    shape = jax.ShapeDtypeStruct
    outs = pl.pallas_call(
        layer_kernel,
        name="layer",
        out_shape=(
            shape((ROWS, D), BF), shape((ROWS, D), BF), shape((128, 3 * D), F32), shape((128, D), F32),
            shape((128, SHARD), F32), shape((SHARD, 128), F32),
            shape((1, 128), F32), shape((1, 128), F32), shape((1, 128), F32), shape((1, 128), F32),
        ),
        in_specs=[hbm, hbm, pl.BlockSpec(memory_space=pltpu.SMEM), hbm, hbm, hbm, hbm, vmem, vmem, vmem, vmem],
        out_specs=[hbm] * 4 + [vmem] * 6,
        scratch_shapes=[
            pltpu.VMEM((D, 3 * D), BF), pltpu.VMEM((D, D), BF), pltpu.VMEM((D, FF), BF), pltpu.VMEM((FF, D), BF),
            pltpu.VMEM((ROWS, D), BF), pltpu.VMEM((PAD, D), BF), pltpu.VMEM((PAD, D), BF), pltpu.VMEM((PAD, D), BF),
            pltpu.VMEM((PAD, 3 * D), BF), pltpu.VMEM((PAD, 3 * 512), BF),
            pltpu.VMEM((D, 2 * PAD), BF), pltpu.VMEM((D, 2 * PAD), BF), pltpu.VMEM((D, 2 * PAD), BF),
            pltpu.VMEM((D, 2 * PAD), BF),
            pltpu.VMEM((16, TILE, TILE), BF), pltpu.VMEM((TILE, TILE), F32),
            pltpu.VMEM((ROWS, D), F32), pltpu.VMEM((ROWS, D), F32), pltpu.VMEM((ROWS, D), F32),
            pltpu.VMEM((PAD, 2 * SHARD), BF), pltpu.VMEM((PAD, 2 * SHARD), BF),
            pltpu.VMEM((PAD, D), BF), pltpu.VMEM((PAD, 512), BF),
            pltpu.VMEM((8, 2, 2, 2, 2, 128, WIDE), BF),
            pltpu.VMEM((8, 2, 2, 2, 128, WIDE), BF), pltpu.VMEM((8, 2, 2, 128, WIDE), BF),
            pltpu.VMEM((8, 2, 128, WIDE), BF), pltpu.VMEM((8, 128, WIDE), BF),
            pltpu.VMEM((4, 8, D), F32), pltpu.VMEM((6, 8, D), F32), pltpu.VMEM((5, 8, D), F32),
            pltpu.SemaphoreType.DMA((N_MSG,)), pltpu.SemaphoreType.DMA((N_MSG,)), pltpu.SemaphoreType.DMA((14,)),
        ],
        compiler_params=pltpu.CompilerParams(
            collective_id=0, has_side_effects=True, vmem_limit_bytes=67_043_328
        ),
    )(tokens, cotangent, live_items, qkv_weight, out_weight, up_weight, down_weight, *rows_of)
    return (*outs[:6], *(v.reshape(128) for v in outs[6:]))


IN_SPECS = (
    P(("seq", "ff"), None), P(("seq", "ff"), None), P("seq"), P(), P(), P(None, "ff"), P("ff", None),
    P(), P(), P(), P(),
)
OUT_SPECS = (
    P(("seq", "ff"), None), P(("seq", "ff"), None), P("seq", None), P("seq", None), P("seq", "ff"),
    P("ff", "seq"), P("seq"), P("seq"), P("seq"), P("seq"),
)


def solution(mesh):
    body = fused if (mesh.shape["seq"], mesh.shape["ff"]) == (8, 4) else general
    return jax.shard_map(body, mesh=mesh, in_specs=IN_SPECS, out_specs=OUT_SPECS, check_vma=False)
```

```python
import jax
import jax.numpy as jnp
from jax import lax
from jax.experimental import pallas as pl
from jax.experimental.pallas import tpu as pltpu
from jax.sharding import PartitionSpec as P

HEADS = 8
HEAD_DIM = 128
ITEM_LEN = 15
BF = jnp.bfloat16
F32 = jnp.float32


def layer_norm(content_matrix, gain, shift):
    centre = content_matrix - jnp.mean(content_matrix, axis=-1, keepdims=True)
    spread = jnp.mean(centre * centre, axis=-1, keepdims=True)
    return centre * lax.rsqrt(spread + 1e-05) * gain + shift


def tile_allowed(tile_rows):
    position = jnp.arange(tile_rows, dtype=jnp.int32)
    same_item = position[:, None] // ITEM_LEN == position[None, :] // ITEM_LEN
    return same_item & (position[None, :] <= position[:, None])


def dot(a, b):
    return jnp.dot(a, b, preferred_element_type=F32)


def tiles_of(x, tile):
    return x.reshape(-1, tile, HEAD_DIM)


def scores_of(q, k, allowed):
    s = jnp.einsum("tqd,tkd->tqk", q, k, preferred_element_type=F32) * HEAD_DIM ** (-0.5)
    return jnp.where(allowed, s, -1e30)


def attend_forward(packed, tile):
    allowed = tile_allowed(tile)
    width = HEADS * HEAD_DIM
    mixed, saved = [], []
    for h in range(HEADS):
        q, k, v = (tiles_of(packed[:, p * width + h * HEAD_DIM:][:, :HEAD_DIM], tile) for p in range(3))
        probs = jax.nn.softmax(scores_of(q, k, allowed), axis=-1)
        o = jnp.einsum("tqk,tkd->tqd", probs.astype(BF), v, preferred_element_type=F32)
        mixed.append(o.astype(BF).reshape(-1, HEAD_DIM))
        saved.append(probs)
    return jnp.concatenate(mixed, axis=1), saved


def attend_backward(packed, saved, grad_mixed, tile):
    width = HEADS * HEAD_DIM
    scale = HEAD_DIM ** (-0.5)
    parts = ([], [], [])
    for h in range(HEADS):
        q, k, v = (tiles_of(packed[:, p * width + h * HEAD_DIM:][:, :HEAD_DIM], tile) for p in range(3))
        o = tiles_of(grad_mixed[:, h * HEAD_DIM:][:, :HEAD_DIM], tile)
        probs = saved[h]
        dp = jnp.einsum("tqd,tkd->tqk", o, v, preferred_element_type=F32)
        gv = jnp.einsum("tqk,tqd->tkd", probs.astype(BF), o, preferred_element_type=F32)
        gs = (probs * (dp - jnp.sum(probs * dp, axis=-1, keepdims=True))).astype(BF)
        gq = jnp.einsum("tqk,tkd->tqd", gs, k, preferred_element_type=F32) * scale
        gk = jnp.einsum("tqk,tqd->tkd", gs, q, preferred_element_type=F32) * scale
        for part, g in zip(parts, (gq, gk, gv)):
            part.append(g.astype(BF).reshape(-1, HEAD_DIM))
    return jnp.concatenate(parts[0] + parts[1] + parts[2], axis=1)


def general(
    tokens, cotangent, live_items, qkv_weight, out_weight, up_weight, down_weight,
    gain_one, shift_one, gain_two, shift_two,
):
    rows = tokens.shape[0]
    items = rows // ITEM_LEN
    tile = ITEM_LEN * (16 if items % 16 == 0 else 1)
    place = lax.axis_index("ff") * items + jnp.arange(rows, dtype=jnp.int32) // ITEM_LEN
    keep = (place < live_items[0]).astype(F32)[:, None]
    up_all = lax.all_gather(up_weight, "ff", axis=1, tiled=True)
    down_all = lax.all_gather(down_weight, "ff", axis=0, tiled=True)
    inputs = tokens.astype(F32)
    normed, norm_one_pull = jax.vjp(layer_norm, inputs, gain_one, shift_one)
    normed = normed.astype(BF)
    packed = dot(normed, qkv_weight).astype(BF)
    mixed, saved = attend_forward(packed, tile)
    middle = inputs + keep * dot(mixed, out_weight)
    normed_two, norm_two_pull = jax.vjp(layer_norm, middle, gain_two, shift_two)
    normed_two = normed_two.astype(BF)
    grad_out = cotangent.astype(F32)
    grad_branch = (keep * grad_out).astype(BF)
    pre = dot(normed_two, up_all)
    hidden = jax.nn.gelu(pre).astype(BF)
    layer_out = (middle + keep * dot(hidden, down_all)).astype(BF)
    grad_hidden = dot(grad_branch, down_all.T)
    grad_pre = jax.vjp(jax.nn.gelu, pre)[1](grad_hidden)[0].astype(BF)
    grad_down = dot(hidden.T, grad_branch).astype(BF)
    grad_up = dot(normed_two.T, grad_pre).astype(BF)
    grad_middle_norm, grad_gain_two, grad_shift_two = norm_two_pull(dot(grad_pre, up_all.T))
    grad_middle = grad_out + grad_middle_norm
    grad_attended = (keep * grad_middle).astype(BF)
    grad_out_weight = dot(mixed.T, grad_attended).astype(BF)
    grad_mixed = dot(grad_attended, out_weight.T).astype(BF)
    grad_packed = attend_backward(packed, saved, grad_mixed, tile)
    grad_qkv = dot(normed.T, grad_packed).astype(BF)
    grad_inputs, grad_gain_one, grad_shift_one = norm_one_pull(dot(grad_packed, qkv_weight.T))
    grad_tokens = (grad_middle + grad_inputs).astype(BF)

    def scatter(x, axis, dim):
        return lax.psum_scatter(x, axis, scatter_dimension=dim, tiled=True)

    grad_up = scatter(scatter(grad_up, "ff", 1), "seq", 0).astype(F32)
    grad_down = scatter(scatter(grad_down, "ff", 0), "seq", 1).astype(F32)
    shared = [
        lax.psum(scatter(g, "seq", 0), "ff").astype(F32)
        for g in (grad_qkv, grad_out_weight, grad_gain_one, grad_shift_one, grad_gain_two, grad_shift_two)
    ]
    return (layer_out, grad_tokens, shared[0], shared[1], grad_up, grad_down, *shared[2:])


MESH = pl.DeviceIdType.MESH
ROWS, PAD, D, FF, SHARD = 480, 512, 1024, 2048, 512
TILE = 240
WIDE = 256
STEP = 96
UP0, UP1, DN0, DN1, OUT, QS, KS, VS = range(8)
ORDER = {
    UP0: "lyxh", UP1: "ylxh", DN0: "lxyh", DN1: "xylh", OUT: "xylh", QS: "xlyh", KS: "yxlh", VS: "lyxh",
}
EYES = "xhly"
M_UPC, M_DNC = 0, 1
M_W = 2
M_GBT, M_N2T, M_MXT, M_N1T, M_GA = 42, 43, 44, 45, 46
M_HID, M_GPR = 47, 49
M_PK = 51
M_RED = 57
M_AGC, M_AGX, M_AGF = 97, 101, 105
M_VEC = 109
N_MSG = 114
WAYS = ("X", "Y", "L", "P", "Q")
SCHED = {
    ("qkv", 5): (
        ("X", 0),
    ),
    ("att", 0): (
        ("X", 1),
    ),
    ("att", 2): (
        ("Y", 0), ("L", 0), ("X", 2),
    ),
    "mxt": (
        ("Y", 1), ("L", 1),
    ),
    "proj": (
        ("X", 3), ("P", 0), ("Q", 0),
    ),
    "n2t": (
        ("Y", 2), ("L", 2),
    ),
    ("sh", 0): (
        ("P", 1), ("Q", 1),
    ),
    ("sum", 0): (
        ("Y", 3), ("L", 3),
    ),
    ("sum", 2): (
        ("P", 2), ("Q", 2),
    ),
    "weights": (
        ("P", 3), ("Q", 3),
    ),
    ("sum", 5): (
        ("R", UP0, 0, 0), ("R", UP1, 0, 0),
    ),
    "ln2b": (
        ("R", DN0, 0, 0),
    ),
    "osum": (
        ("R", UP1, 0, 1),
    ),
    ("pr", 0): (
        ("R", UP0, 0, 1),
    ),
    ("qs", 0): (
        ("R", DN1, 0, 0),
    ),
    ("pr", 2): (
        ("R", DN0, 0, 1),
    ),
    ("pr", 3): (
        ("R", UP0, 1, 0),
    ),
    ("dwn", 0): (
        ("R", UP1, 1, 0),
    ),
    ("dwn", 1): (
        ("R", KS, 0, 0),
    ),
    "fin": (
        ("R", OUT, 0, 0),
    ),
    ("gn1", 0): (
        ("R", VS, 0, 0),
    ),
    ("gn1", 1): (
        ("R", DN1, 1, 0),
    ),
    "tail": (
        ("V", 0), ("R", VS, 0, 1), ("R", KS, 0, 1), ("R", DN1, 2, 0), ("R", QS, 0, 0), ("R", OUT, 1, 0),
        ("R", DN1, 3, 0), ("R", DN0, 1, 0), ("R", UP0, 2, 0), ("R", QS, 1, 0), ("R", VS, 1, 0), ("R", UP1, 2, 0),
        ("R", OUT, 2, 0), ("V", 1), ("R", DN0, 2, 0), ("R", UP0, 3, 0), ("R", QS, 2, 0), ("V", 2), ("R", UP1, 3, 0),
        ("R", KS, 1, 0), ("R", OUT, 3, 0), ("R", VS, 2, 0), ("R", DN0, 3, 0), ("G", 0), ("V", 3), ("R", QS, 3, 0),
        ("R", KS, 2, 0), ("G", 1), ("R", VS, 3, 0), ("V", 4), ("G", 3), ("R", KS, 3, 0), ("G", 2),
    ),
}


def dot_nt(a, b):
    return lax.dot_general(a, b, (((1,), (1,)), ((), ())), preferred_element_type=F32)


def layer_kernel(
    tok_h, cot_h, live, wq_h, wo_h, up_h, dn_h, g1, s1, g2, s2,
    lo_h, gt_h, gq_h, gup_o, gdn_o, gg1_o, gs1_o, gg2_o, gs2_o,
    wq, wo, upa, dna, tok, gb, nb, mx, pk, pks, xgb, xn2, xmx, xn1, probs, mask, mid, gm, facc,
    hids, gprs, ga, gas, gw, r0, r1, r2, r3, vsum, vbuf, vrecv, ssem, rsem, lsem,
):
    s, f = lax.axis_index("seq"), lax.axis_index("ff")
    bit = {"h": s // 4, "l": (s // 2) % 2, "y": s % 2, "x": f // 2, "c": f % 2}
    mate = {
        "h": (s + 4 - 8 * bit["h"], f), "l": (s + 2 - 4 * bit["l"], f), "y": (s + 1 - 2 * bit["y"], f),
        "x": (s, f + 2 - 4 * bit["x"]), "c": (s, f + 1 - 2 * bit["c"]),
    }
    x, c = bit["x"], bit["c"]

    def at(base, size, unit=128):
        return pl.ds(pl.multiple_of(base, unit), size)

    def local(i, src, dst):
        return pltpu.make_async_copy(src, dst, lsem.at[i])

    loads = {
        0: (tok_h, tok), 1: (cot_h, gb.at[0:ROWS]), 2: (wq_h, wq), 3: (wo_h, wo), 4: (up_h, upa.at[:, 0:SHARD]),
        5: (dn_h, dna.at[0:SHARD]), 6: (cot_h, nb.at[0:ROWS]), 7: (wq_h, wq),
        8: (nb.at[0:ROWS], lo_h), 9: (tok, gt_h), 10: (xgb.at[0:512], gq_h),
    }

    def load(i):
        local(i, *loads[i]).start()

    def loaded(i):
        local(i, *loads[i]).wait()

    def remote(i, to, src, dst):
        return pltpu.make_async_remote_copy(
            src_ref=src, dst_ref=dst, send_sem=ssem.at[i], recv_sem=rsem.at[i], device_id=mate[to], device_id_type=MESH
        )

    def region(k, way, slot):
        yb = bit["y"] if way in ("X", "L") else 1 - bit["y"]
        lb = bit["l"] if way in ("X", "Y") else 1 - bit["l"]
        size = 128 if k < 2 else 64
        start = (2 * yb + lb) * (2 * size) + (k % 2) * size
        if way in ("P", "Q"):
            size //= 2
            start = start + (size if way == "Q" else 0)
        rows = at(start, size, 32)
        if slot is None:
            return up_h.at[rows, :] if k < 2 else dn_h.at[rows, :]
        if k < 2:
            return upa.at[rows, slot * SHARD:(slot + 1) * SHARD]
        return dna.at[at(slot * SHARD + start, size, 32), :]

    def onward(k, way):
        yb = bit["y"] if way == "Q" else 1 - bit["y"]
        lb = bit["l"] if way == "P" else 1 - bit["l"]
        size = 64 if k < 2 else 32
        start = (2 * yb + lb) * (4 * size) + (k % 2) * (2 * size) + (size if way == "Q" else 0)
        if k < 2:
            return upa.at[at(start, size, 32), 2 * SHARD:3 * SHARD]
        return dna.at[at(2 * SHARD + start, size, 32), :]

    def weight(k, way):
        i = M_W + k * 10 + WAYS.index(way)
        if way == "X":
            return remote(i, "x", region(k, "X", None), region(k, "X", 2))
        if way in ("Y", "L"):
            return remote(i, way.lower(), region(k, "X", 2), region(k, "X", 2))
        return remote(i, "l" if way == "P" else "y", onward(k, way), onward(k, way))

    def weight_mate(k, way):
        return remote(M_W + k * 10 + 5 + WAYS.index(way), "c", region(k, way, 2), region(k, way, 3))

    def relay(way, k):
        weight(k, way).wait()
        if way == "X":
            weight(k, "Y").start()
            weight(k, "L").start()
        elif way == "Y":
            weight(k, "P").start()
        elif way == "L":
            weight(k, "Q").start()
        weight_mate(k, way).start()

    def weight_c(which):
        if which == 0:
            return remote(M_UPC, "c", up_h, upa.at[:, SHARD:2 * SHARD])
        return remote(M_DNC, "c", dn_h, dna.at[SHARD:2 * SHARD])

    def turned(i, ref):
        return remote(i, "c", ref.at[:, 0:PAD], ref.at[:, PAD:2 * PAD])

    def own_hid(slot):
        return wq.at[0:PAD, at(slot * SHARD, SHARD)]

    def own_gpr(slot):
        return wq.at[PAD:2 * PAD, at(slot * SHARD, SHARD)]

    def hid_copy(g):
        return remote(M_HID + g, "c", own_hid(2 * g + 1), hids.at[:, at(g * SHARD, SHARD)])

    def gpr_copy(g):
        return remote(M_GPR + g, "c", own_gpr(2 * g + 1), gprs.at[:, at(g * SHARD, SHARD)])

    def ga_copy():
        return remote(M_GA, "c", ga.at[:, at((1 - c) * 512, 512)], gas)

    def pk_copy(n, xb, part):
        return remote(
            M_PK + n * 3 + part, "c", pk.at[:, at(part * D + (1 - c) * 512 + xb * WIDE, WIDE)],
            pks.at[:, at(part * 512 + xb * WIDE, WIDE)],
        )

    landing = (r0, r1, r2, r3)

    def bits_of(p):
        if p < OUT:
            return {**bit, "x": 0}
        return bit

    def chosen(p, k, mine, xb=None):
        own, order, index = bits_of(p), ORDER[p], []
        for e in EYES:
            if e in order[:k]:
                index.append(own[e])
            elif e == order[k]:
                index.append(own[e] if mine else 1 - own[e])
            elif e == "x" and xb is not None:
                index.append(xb)
            else:
                index.append(slice(None))
        return index

    def red(p, k, xb=None, part=0):
        dst = landing[k].at[p] if xb is None else landing[k].at[p, xb]
        return remote(
            M_RED + p * 5 + (k + 1 if k else part), ORDER[p][k], gw.at[(p, *chosen(p, k, False, xb))], dst
        )

    def add(p, k, xb=None):
        index = chosen(p, k, True, xb)
        free = [n for n, e in enumerate(index) if isinstance(e, slice)]
        count = len(free)

        def body(i, _):
            place = [(i // (1 << (count - 1 - n))) % 2 for n in range(count)]
            full = list(index)
            for n, e in zip(free, place):
                full[n] = e
            lead = (p, *place) if xb is None else (p, xb, *place)
            gw[(p, *full)] = (gw[(p, *full)].astype(F32) + landing[k][lead].astype(F32)).astype(BF)
            return 0

        lax.fori_loop(0, 1 << count, body, 0)

    parts_done = {}

    def first(p, xb, part):
        if ORDER[p][0] != "x":
            red(p, 0, xb, part).start()
        elif (part == 1) == (p < OUT):
            red(p, 0).start()

    def reduced(p, k, part):
        if k == 0 and ORDER[p][0] != "x" and p != OUT:
            xb = part if p < OUT else (1 - x if part == 0 else x)
            red(p, 0, xb, part).wait()
            add(p, 0, xb)
            parts_done[p] = parts_done.get(p, 0) + 1
            if parts_done[p] == 2:
                red(p, 1).start()
        elif k < 3:
            red(p, k).wait()
            add(p, k)
            red(p, k + 1).start()
        else:
            red(p, 3).wait()
            own = bits_of(p)
            total = gw[(p, *(own[e] for e in EYES))].astype(F32) + r3[p].astype(F32)
            if p in (UP0, UP1):
                half = p - UP0
                gup_o[:, half * WIDE:(half + 1) * WIDE] = total
            elif p in (DN0, DN1):
                half = p - DN0
                gdn_o[half * WIDE:(half + 1) * WIDE, :] = total.T
            else:
                quarters(p - OUT, own_quarter)[...] = total.astype(BF)
                gather_c(p - OUT).start()
                gather_x(p - OUT).start()

    def quarters(q, n):
        return xgb.at[q * 128:(q + 1) * 128, at(n * WIDE, WIDE)]

    own_quarter = 2 * c + x

    def gather_c(q):
        return remote(M_AGC + q, "c", quarters(q, own_quarter), quarters(q, own_quarter))

    def gather_x(q):
        return remote(M_AGX + q, "x", quarters(q, own_quarter), quarters(q, own_quarter))

    def gather_f(q):
        other = 2 * c + 1 - x
        return remote(M_AGF + q, "c", quarters(q, other), quarters(q, other))

    def vec(n):
        return remote(M_VEC + n, "cxylh"[n], vbuf.at[n], vrecv.at[n])

    def vec_step(n):
        vec(n).wait()
        vbuf[n + 1] = vbuf[n] + vrecv[n]
        if n < 4:
            vec(n + 1).start()

    def handle(event):
        kind = event[0]
        if kind == "R":
            reduced(*event[1:])
        elif kind == "G":
            gather_x(event[1]).wait()
            gather_f(event[1]).start()
        elif kind == "V":
            vec_step(event[1])
        else:
            relay(kind, event[1])

    def poll(name):
        for event in SCHED.get(name, ()):
            handle(event)

    def poll_at(name, i, count):
        for n in range(count):
            if (name, n) in SCHED:
                @pl.when(i == n)
                def _():
                    for event in SCHED[(name, n)]:
                        handle(event)

    limit = (live[0] - f * (ROWS // 15)) * 15

    def keep_of(r):
        rows = r * STEP + lax.broadcasted_iota(jnp.int32, (STEP, 1), 0)
        return jnp.where(rows < limit, 1.0, 0.0).astype(F32)

    def block(r):
        return pl.ds(pl.multiple_of(r * STEP, STEP), STEP)

    def centred(v):
        centre = v - jnp.mean(v, axis=-1, keepdims=True)
        rstd = lax.rsqrt(jnp.mean(centre * centre, axis=-1, keepdims=True) + 1e-05)
        return centre * rstd, rstd

    def turn(src, dst):
        def body(j, _):
            cols = at(j * 128, 128)
            dst[cols, 0:PAD] = src[:, cols].T
            return 0

        lax.fori_loop(0, D // 128, body, 0)

    load(0)
    load(2)
    barrier = pltpu.get_barrier_semaphore()
    for e in "xylhc":
        pl.semaphore_signal(barrier, inc=1, device_id=mate[e], device_id_type=MESH)
    for i in (1, 3, 4, 5):
        load(i)
    qi = lax.broadcasted_iota(jnp.int32, (TILE, TILE), 0)
    ki = lax.broadcasted_iota(jnp.int32, (TILE, TILE), 1)
    mask[...] = jnp.where((ki <= qi) & (ki >= qi - lax.rem(qi, 15)), 0.0, -1e30).astype(F32)
    nb[ROWS:PAD, :] = jnp.zeros((PAD - ROWS, D), BF)
    pl.semaphore_wait(barrier, 5)
    for k in range(4):
        weight(k, "X").start()
    weight_c(0).start()
    weight_c(1).start()
    for ref in (gb, mx, ga):
        ref[ROWS:PAD, :] = jnp.zeros((PAD - ROWS, D), BF)
    pk[ROWS:PAD, :] = jnp.zeros((PAD - ROWS, 3 * D), BF)
    vsum[...] = jnp.zeros(vsum.shape, F32)
    loaded(0)

    def norm_one(r, _):
        xhat, _r = centred(tok[block(r), :].astype(F32))
        nb[block(r), :] = (xhat * g1[...] + s1[...]).astype(BF)
        return 0

    lax.fori_loop(0, ROWS // STEP, norm_one, 0)
    poll("ln1")
    loaded(2)

    def qkv(n, _):
        cols = at(n * 512, 512)
        pk[0:ROWS, cols] = jnp.dot(nb[0:ROWS, :], wq[:, cols], preferred_element_type=F32).astype(BF)
        poll_at("qkv", n, 6)
        return 0

    lax.fori_loop(0, 6, qkv, 0)
    turn(nb, xn1)
    turned(M_N1T, xn1).start()
    poll("n1t")
    loaded(1)

    def mask_cot(r, _):
        gb[block(r), :] = (keep_of(r) * gb[block(r), :].astype(F32)).astype(BF)
        return 0

    lax.fori_loop(0, ROWS // STEP, mask_cot, 0)
    turn(gb, xgb)
    turned(M_GBT, xgb).start()
    poll("gbt")

    def attend(i, _):
        for h, t in ((i * 2 + n, t) for n in range(2) for t in range(2)):
            cols = [at(part * D + h * 128, 128) for part in range(3)]
            rows = slice(t * TILE, (t + 1) * TILE)
            sc = dot_nt(pk[rows, cols[0]], pk[rows, cols[1]]) * (128 ** -0.5) + mask[...]
            w = jnp.exp(sc - jnp.max(sc, axis=-1, keepdims=True))
            p = (w * (1.0 / jnp.sum(w, axis=-1, keepdims=True))).astype(BF)
            probs[h * 2 + t] = p
            mx[rows, at(h * 128, 128)] = jnp.dot(p, pk[rows, cols[2]], preferred_element_type=F32).astype(BF)
        poll_at("att", i, 4)
        return 0

    lax.fori_loop(0, 4, attend, 0)
    turn(mx, xmx)
    turned(M_MXT, xmx).start()
    poll("mxt")
    loaded(3)

    def project(n, _):
        cols = at(n * 512, 512)
        facc[:, cols] = jnp.dot(mx[0:ROWS, :], wo[:, cols], preferred_element_type=F32)
        return 0

    lax.fori_loop(0, 2, project, 0)
    poll("proj")

    def norm_two(r, _):
        m = tok[block(r), :].astype(F32) + keep_of(r) * facc[block(r), :]
        mid[block(r), :] = m
        xhat, _r = centred(m)
        nb[block(r), :] = (xhat * g2[...] + s2[...]).astype(BF)
        return 0

    lax.fori_loop(0, ROWS // STEP, norm_two, 0)
    poll("ln2")
    turn(nb, xn2)
    turned(M_N2T, xn2).start()
    poll("n2t")

    loaded(4)
    loaded(5)
    wq[ROWS:PAD, 0:FF] = jnp.zeros((PAD - ROWS, FF), BF)
    wq[PAD + ROWS:2 * PAD, 0:FF] = jnp.zeros((PAD - ROWS, FF), BF)

    def shard(j):
        cols = at(j * SHARD, SHARD)
        pre = jnp.dot(nb[0:ROWS, :], upa[:, cols], preferred_element_type=F32)
        sq = pre * pre
        t = jnp.tanh(0.7978845608028654 * pre * (1.0 + 0.044715 * sq))
        half = 0.5 * (1.0 + t)
        wq[0:ROWS, cols] = (pre * half).astype(BF)
        slope = half + 0.5 * pre * (1.0 - t * t) * (0.7978845608028654 * (1.0 + 0.134145 * sq))
        gh = dot_nt(gb[0:ROWS, :], dna[cols, :])
        wq[PAD:PAD + ROWS, cols] = (gh * slope).astype(BF)

    def group(g, _):
        @pl.when(g == 0)
        def _():
            weight_c(0).wait()
            weight_c(1).wait()

        @pl.when(g == 1)
        def _():
            poll("weights")
            for k in range(4):
                for way in WAYS:
                    weight_mate(k, way).wait()

        def one(n, _):
            shard(2 * g + 1 - n)

            @pl.when(n == 0)
            def _():
                hid_copy(g).start()
                gpr_copy(g).start()

            poll_at("sh", 2 * g + n, 4)
            return 0

        lax.fori_loop(0, 2, one, 0)

        @pl.when(g == 0)
        def _():
            turned(M_N2T, xn2).wait()
            turned(M_GBT, xgb).wait()

        hid_copy(g).wait()
        gpr_copy(g).wait()
        mine, theirs = at(2 * g * SHARD, SHARD), at(g * SHARD, SHARD)

        def sums(i, _):
            n = lax.rem(i, 2)
            rows = at(n * 512, 512)
            for m, lhs, top, low, p in ((0, xn2, PAD, gprs, UP0), (1, xgb, 0, hids, DN0)):
                @pl.when(i // 2 == m)
                def _():
                    rhs = jnp.concatenate([wq[top:top + PAD, mine], low[:, theirs]], axis=0)
                    total = jnp.dot(lhs[rows, :], rhs, preferred_element_type=F32).astype(BF)
                    for half in range(2):
                        gw[p + half, g, n] = total[:, half * WIDE:(half + 1) * WIDE].reshape(2, 2, 128, WIDE)

                    for part in range(2):
                        @pl.when((n == 1) & (g == part))
                        def _():
                            for half in range(2):
                                first(p + half, part, part)

            poll_at("sum", 4 * g + i, 8)
            return 0

        lax.fori_loop(0, 4, sums, 0)
        return 0

    lax.fori_loop(0, 2, group, 0)
    load(6)

    def back_up(n, _):
        cols = at(n * 512, 512)
        facc[:, cols] = dot_nt(wq[PAD:PAD + ROWS, 0:FF], upa[cols, :])
        poll_at("bup", n, 2)
        return 0

    lax.fori_loop(0, 2, back_up, 0)
    loaded(6)

    def row_sum(v):
        total = v[0:8]
        for n in range(1, STEP // 8):
            total = total + v[n * 8:(n + 1) * 8]
        return total

    def norm_back(v, gn, gain, n):
        xhat, rstd = centred(v)
        vsum[n] += row_sum(gn * xhat)
        vsum[n + 1] += row_sum(gn)
        e = gn * gain
        return rstd * (e - jnp.mean(e, axis=-1, keepdims=True) - xhat * jnp.mean(e * xhat, axis=-1, keepdims=True))

    def norm_two_back(r, _):
        total = nb[block(r), :].astype(F32) + norm_back(mid[block(r), :], facc[block(r), :], g2[...], 2)
        gm[block(r), :] = total
        ga[block(r), :] = (keep_of(r) * total).astype(BF)
        return 0

    lax.fori_loop(0, ROWS // STEP, norm_two_back, 0)
    ga_copy().start()
    poll("ln2b")

    def back_out(n, _):
        cols = at(n * 512, 512)
        mx[0:ROWS, cols] = dot_nt(ga[0:ROWS, :], wo[cols, :]).astype(BF)
        return 0

    turned(M_MXT, xmx).wait()
    lax.fori_loop(0, 2, back_out, 0)
    poll("bout")
    ga_copy().wait()

    def out_sums(n, _):
        rows = at(n * 512, 512)
        rhs = jnp.concatenate([ga[:, at(c * 512, 512)], gas[...]], axis=0)
        total = jnp.dot(xmx[rows, :], rhs, preferred_element_type=F32).astype(BF)
        for half in range(2):
            gw[OUT, half, n] = total[:, half * WIDE:(half + 1) * WIDE].reshape(2, 2, 128, WIDE)
        return 0

    lax.fori_loop(0, 2, out_sums, 0)
    red(OUT, 0).start()
    poll("osum")
    turned(M_N1T, xn1).wait()

    def heads_back(h0):
        for h, t in ((h0 + n, t) for n in range(2) for t in range(2)):
            cols = [at(part * D + h * 128, 128) for part in range(3)]
            rows = slice(t * TILE, (t + 1) * TILE)
            q, k, v = (pk[rows, col] for col in cols)
            o = mx[rows, at(h * 128, 128)]
            pb = probs[h * 2 + t]
            p = pb.astype(F32)
            dp = dot_nt(o, v)
            gs = (p * (dp - jnp.sum(p * dp, axis=-1, keepdims=True))).astype(BF)
            gv = lax.dot_general(pb, o, (((0,), (0,)), ((), ())), preferred_element_type=F32)
            gq = jnp.dot(gs, k, preferred_element_type=F32) * (128 ** -0.5)
            gk = lax.dot_general(gs, q, (((0,), (0,)), ((), ())), preferred_element_type=F32) * (128 ** -0.5)
            for col, g in zip(cols, (gq, gk, gv)):
                pk[rows, col] = g.astype(BF)

    def pair(i, _):
        cb = lax.rem(i + 1 + c, 2)
        later = i // 2
        xb = lax.rem(later + 1 + x, 2)
        heads_back(cb * 4 + xb * 2)
        for n in range(2):
            @pl.when(i == 2 * n)
            def _():
                for part in range(3):
                    pk_copy(n, 1 - x if n == 0 else x, part).start()

        poll_at("pr", i, 4)

        @pl.when(i % 2 == 1)
        def _():
            for n in range(2):
                @pl.when(later == n)
                def _():
                    for part in range(3):
                        pk_copy(n, 1 - x if n == 0 else x, part).wait()

            def body(n, _):
                rows = at(n * 512, 512)
                rhs = jnp.concatenate(
                    [
                        jnp.concatenate([pk[:, at(part * D + c * 512 + xb * WIDE, WIDE)] for part in range(3)], axis=1),
                        jnp.concatenate([pks[:, at(part * 512 + xb * WIDE, WIDE)] for part in range(3)], axis=1),
                    ],
                    axis=0,
                )
                total = jnp.dot(xn1[rows, :], rhs, preferred_element_type=F32).astype(BF)
                for part in range(3):
                    gw[QS + part, xb, n] = total[:, part * WIDE:(part + 1) * WIDE].reshape(2, 2, 128, WIDE)
                return 0

            lax.fori_loop(0, 2, body, 0)
            for n in range(2):
                @pl.when(later == n)
                def _():
                    for p in (QS, KS, VS):
                        first(p, 1 - x if n == 0 else x, n)
                    poll(("qs", n))

        return 0

    lax.fori_loop(0, 4, pair, 0)

    def down(n, _):
        cols = at(n * 512, 512)
        facc[:, cols] = jnp.dot(wq[0:ROWS, 0:FF], dna[:, cols], preferred_element_type=F32)
        poll_at("dwn", n, 2)
        return 0

    lax.fori_loop(0, 2, down, 0)
    load(7)

    def finish_out(r, _):
        nb[block(r), :] = (mid[block(r), :] + keep_of(r) * facc[block(r), :]).astype(BF)
        return 0

    lax.fori_loop(0, ROWS // STEP, finish_out, 0)
    load(8)
    poll("fin")
    loaded(7)

    def back_qkv(n, _):
        cols = at(n * 512, 512)
        facc[:, cols] = dot_nt(pk[0:ROWS, :], wq[cols, :])
        poll_at("gn1", n, 2)
        return 0

    lax.fori_loop(0, 2, back_qkv, 0)

    def norm_one_back(r, _):
        total = gm[block(r), :] + norm_back(tok[block(r), :].astype(F32), facc[block(r), :], g1[...], 0)
        tok[block(r), :] = total.astype(BF)
        return 0

    lax.fori_loop(0, ROWS // STEP, norm_one_back, 0)
    load(9)
    vbuf[0] = jnp.concatenate(
        [jnp.sum(vsum[n], axis=0, keepdims=True) for n in range(4)] + [jnp.zeros((4, D), F32)], axis=0
    )
    vec(0).start()
    poll("ln1b")
    poll("tail")
    for n, ref in enumerate((gg1_o, gs1_o, gg2_o, gs2_o)):
        ref[...] = vbuf[5, n:n + 1, at(s * 128, 128)]
    for p in (OUT, QS, KS, VS):
        gather_c(p - OUT).wait()
        gather_f(p - OUT).wait()
    load(10)
    for i in (8, 9, 10):
        loaded(i)


def result_kernel(lo, gt, gq, gup, gdn, gg1, gs1, gg2, gs2, lo_o, gt_o, gqkv_o, gout_o, gup_o, gdn_o, gg1_o, gs1_o, gg2_o, gs2_o, lov, gtv, gqv, gqkv, gout, sem):
    ins = [pltpu.make_async_copy(a, b, sem.at[n]) for n, (a, b) in enumerate(((lo, lov), (gt, gtv), (gq, gqv)))]
    for copy in ins:
        copy.start()
    gup_o[...] = gup[...]
    gdn_o[...] = gdn[...]
    for a, b in ((gg1, gg1_o), (gs1, gs1_o), (gg2, gg2_o), (gs2, gs2_o)):
        b[...] = a[...].reshape(128)
    outs = [pltpu.make_async_copy(a, b, sem.at[3 + n]) for n, (a, b) in enumerate(((lov, lo_o), (gtv, gt_o), (gout, gout_o), (gqkv, gqkv_o)))]
    for n in range(2):
        ins[n].wait()
        outs[n].start()
    ins[2].wait()
    gout[...] = gqv[0:128, :].astype(F32)
    outs[2].start()
    for n in range(3):
        gqkv[:, n * D:(n + 1) * D] = gqv[(n + 1) * 128:(n + 2) * 128, :].astype(F32)
    outs[3].start()
    for copy in outs:
        copy.wait()


def fused(
    tokens, cotangent, live_items, qkv_weight, out_weight, up_weight, down_weight,
    gain_one, shift_one, gain_two, shift_two,
):
    rows_of = [v.reshape(1, D) for v in (gain_one, shift_one, gain_two, shift_two)]
    hbm, vmem = pl.BlockSpec(memory_space=pl.ANY), pl.BlockSpec(memory_space=pltpu.VMEM)
    shape = jax.ShapeDtypeStruct
    outs = pl.pallas_call(
        layer_kernel,
        name="layer",
        out_shape=(
            shape((ROWS, D), BF), shape((ROWS, D), BF), shape((512, D), BF),
            shape((128, SHARD), F32), shape((SHARD, 128), F32),
            shape((1, 128), F32), shape((1, 128), F32), shape((1, 128), F32), shape((1, 128), F32),
        ),
        in_specs=[hbm, hbm, pl.BlockSpec(memory_space=pltpu.SMEM), hbm, hbm, hbm, hbm, vmem, vmem, vmem, vmem],
        out_specs=[hbm] * 3 + [vmem] * 6,
        scratch_shapes=[
            pltpu.VMEM((D, 3 * D), BF), pltpu.VMEM((D, D), BF), pltpu.VMEM((D, FF), BF), pltpu.VMEM((FF, D), BF),
            pltpu.VMEM((ROWS, D), BF), pltpu.VMEM((PAD, D), BF), pltpu.VMEM((PAD, D), BF), pltpu.VMEM((PAD, D), BF),
            pltpu.VMEM((PAD, 3 * D), BF), pltpu.VMEM((PAD, 3 * 512), BF),
            pltpu.VMEM((D, 2 * PAD), BF), pltpu.VMEM((D, 2 * PAD), BF), pltpu.VMEM((D, 2 * PAD), BF),
            pltpu.VMEM((D, 2 * PAD), BF),
            pltpu.VMEM((16, TILE, TILE), BF), pltpu.VMEM((TILE, TILE), F32),
            pltpu.VMEM((ROWS, D), F32), pltpu.VMEM((ROWS, D), F32), pltpu.VMEM((ROWS, D), F32),
            pltpu.VMEM((PAD, 2 * SHARD), BF), pltpu.VMEM((PAD, 2 * SHARD), BF),
            pltpu.VMEM((PAD, D), BF), pltpu.VMEM((PAD, 512), BF),
            pltpu.VMEM((8, 2, 2, 2, 2, 128, WIDE), BF),
            pltpu.VMEM((8, 2, 2, 2, 128, WIDE), BF), pltpu.VMEM((8, 2, 2, 128, WIDE), BF),
            pltpu.VMEM((8, 2, 128, WIDE), BF), pltpu.VMEM((8, 128, WIDE), BF),
            pltpu.VMEM((4, 8, D), F32), pltpu.VMEM((6, 8, D), F32), pltpu.VMEM((5, 8, D), F32),
            pltpu.SemaphoreType.DMA((N_MSG,)), pltpu.SemaphoreType.DMA((N_MSG,)), pltpu.SemaphoreType.DMA((14,)),
        ],
        compiler_params=pltpu.CompilerParams(
            collective_id=0, has_side_effects=True, vmem_limit_bytes=67_043_328
        ),
    )(tokens, cotangent, live_items, qkv_weight, out_weight, up_weight, down_weight, *rows_of)
    return pl.pallas_call(
        result_kernel,
        name="results",
        out_shape=(
            shape((ROWS, D), BF), shape((ROWS, D), BF), shape((128, 3 * D), F32), shape((128, D), F32),
            shape((128, SHARD), F32), shape((SHARD, 128), F32),
            shape((128,), F32), shape((128,), F32), shape((128,), F32), shape((128,), F32),
        ),
        in_specs=[hbm] * 3 + [vmem] * 6,
        out_specs=[hbm] * 4 + [vmem] * 6,
        scratch_shapes=[
            pltpu.VMEM((ROWS, D), BF), pltpu.VMEM((ROWS, D), BF), pltpu.VMEM((512, D), BF),
            pltpu.VMEM((128, 3 * D), F32), pltpu.VMEM((128, D), F32), pltpu.SemaphoreType.DMA((7,)),
        ],
    )(*outs)


IN_SPECS = (
    P(("seq", "ff"), None), P(("seq", "ff"), None), P("seq"), P(), P(), P(None, "ff"), P("ff", None),
    P(), P(), P(), P(),
)
OUT_SPECS = (
    P(("seq", "ff"), None), P(("seq", "ff"), None), P("seq", None), P("seq", None), P("seq", "ff"),
    P("ff", "seq"), P("seq"), P("seq"), P("seq"), P("seq"),
)


def solution(mesh):
    body = fused if (mesh.shape["seq"], mesh.shape["ff"]) == (8, 4) else general
    return jax.shard_map(body, mesh=mesh, in_specs=IN_SPECS, out_specs=OUT_SPECS, check_vma=False)
```

```python
import jax
import jax.numpy as jnp
from jax import lax
from jax.experimental import pallas as pl
from jax.experimental.pallas import tpu as pltpu
from jax.sharding import PartitionSpec as P

HEADS = 8
HEAD_DIM = 128
ITEM_LEN = 15
BF = jnp.bfloat16
F32 = jnp.float32


def layer_norm(content_matrix, gain, shift):
    centre = content_matrix - jnp.mean(content_matrix, axis=-1, keepdims=True)
    spread = jnp.mean(centre * centre, axis=-1, keepdims=True)
    return centre * lax.rsqrt(spread + 1e-05) * gain + shift


def tile_allowed(tile_rows):
    position = jnp.arange(tile_rows, dtype=jnp.int32)
    same_item = position[:, None] // ITEM_LEN == position[None, :] // ITEM_LEN
    return same_item & (position[None, :] <= position[:, None])


def dot(a, b):
    return jnp.dot(a, b, preferred_element_type=F32)


def tiles_of(x, tile):
    return x.reshape(-1, tile, HEAD_DIM)


def scores_of(q, k, allowed):
    s = jnp.einsum("tqd,tkd->tqk", q, k, preferred_element_type=F32) * HEAD_DIM ** (-0.5)
    return jnp.where(allowed, s, -1e30)


def attend_forward(packed, tile):
    allowed = tile_allowed(tile)
    width = HEADS * HEAD_DIM
    mixed, saved = [], []
    for h in range(HEADS):
        q, k, v = (tiles_of(packed[:, p * width + h * HEAD_DIM:][:, :HEAD_DIM], tile) for p in range(3))
        probs = jax.nn.softmax(scores_of(q, k, allowed), axis=-1)
        o = jnp.einsum("tqk,tkd->tqd", probs.astype(BF), v, preferred_element_type=F32)
        mixed.append(o.astype(BF).reshape(-1, HEAD_DIM))
        saved.append(probs)
    return jnp.concatenate(mixed, axis=1), saved


def attend_backward(packed, saved, grad_mixed, tile):
    width = HEADS * HEAD_DIM
    scale = HEAD_DIM ** (-0.5)
    parts = ([], [], [])
    for h in range(HEADS):
        q, k, v = (tiles_of(packed[:, p * width + h * HEAD_DIM:][:, :HEAD_DIM], tile) for p in range(3))
        o = tiles_of(grad_mixed[:, h * HEAD_DIM:][:, :HEAD_DIM], tile)
        probs = saved[h]
        dp = jnp.einsum("tqd,tkd->tqk", o, v, preferred_element_type=F32)
        gv = jnp.einsum("tqk,tqd->tkd", probs.astype(BF), o, preferred_element_type=F32)
        gs = (probs * (dp - jnp.sum(probs * dp, axis=-1, keepdims=True))).astype(BF)
        gq = jnp.einsum("tqk,tkd->tqd", gs, k, preferred_element_type=F32) * scale
        gk = jnp.einsum("tqk,tqd->tkd", gs, q, preferred_element_type=F32) * scale
        for part, g in zip(parts, (gq, gk, gv)):
            part.append(g.astype(BF).reshape(-1, HEAD_DIM))
    return jnp.concatenate(parts[0] + parts[1] + parts[2], axis=1)


def general(
    tokens, cotangent, live_items, qkv_weight, out_weight, up_weight, down_weight,
    gain_one, shift_one, gain_two, shift_two,
):
    rows = tokens.shape[0]
    items = rows // ITEM_LEN
    tile = ITEM_LEN * (16 if items % 16 == 0 else 1)
    place = lax.axis_index("ff") * items + jnp.arange(rows, dtype=jnp.int32) // ITEM_LEN
    keep = (place < live_items[0]).astype(F32)[:, None]
    up_all = lax.all_gather(up_weight, "ff", axis=1, tiled=True)
    down_all = lax.all_gather(down_weight, "ff", axis=0, tiled=True)
    inputs = tokens.astype(F32)
    normed, norm_one_pull = jax.vjp(layer_norm, inputs, gain_one, shift_one)
    normed = normed.astype(BF)
    packed = dot(normed, qkv_weight).astype(BF)
    mixed, saved = attend_forward(packed, tile)
    middle = inputs + keep * dot(mixed, out_weight)
    normed_two, norm_two_pull = jax.vjp(layer_norm, middle, gain_two, shift_two)
    normed_two = normed_two.astype(BF)
    grad_out = cotangent.astype(F32)
    grad_branch = (keep * grad_out).astype(BF)
    pre = dot(normed_two, up_all)
    hidden = jax.nn.gelu(pre).astype(BF)
    layer_out = (middle + keep * dot(hidden, down_all)).astype(BF)
    grad_hidden = dot(grad_branch, down_all.T)
    grad_pre = jax.vjp(jax.nn.gelu, pre)[1](grad_hidden)[0].astype(BF)
    grad_down = dot(hidden.T, grad_branch).astype(BF)
    grad_up = dot(normed_two.T, grad_pre).astype(BF)
    grad_middle_norm, grad_gain_two, grad_shift_two = norm_two_pull(dot(grad_pre, up_all.T))
    grad_middle = grad_out + grad_middle_norm
    grad_attended = (keep * grad_middle).astype(BF)
    grad_out_weight = dot(mixed.T, grad_attended).astype(BF)
    grad_mixed = dot(grad_attended, out_weight.T).astype(BF)
    grad_packed = attend_backward(packed, saved, grad_mixed, tile)
    grad_qkv = dot(normed.T, grad_packed).astype(BF)
    grad_inputs, grad_gain_one, grad_shift_one = norm_one_pull(dot(grad_packed, qkv_weight.T))
    grad_tokens = (grad_middle + grad_inputs).astype(BF)

    def scatter(x, axis, dim):
        return lax.psum_scatter(x, axis, scatter_dimension=dim, tiled=True)

    grad_up = scatter(scatter(grad_up, "ff", 1), "seq", 0).astype(F32)
    grad_down = scatter(scatter(grad_down, "ff", 0), "seq", 1).astype(F32)
    shared = [
        lax.psum(scatter(g, "seq", 0), "ff").astype(F32)
        for g in (grad_qkv, grad_out_weight, grad_gain_one, grad_shift_one, grad_gain_two, grad_shift_two)
    ]
    return (layer_out, grad_tokens, shared[0], shared[1], grad_up, grad_down, *shared[2:])


MESH = pl.DeviceIdType.MESH
ROWS, PAD, D, FF, SHARD = 480, 512, 1024, 2048, 512
TILE = 240
WIDE = 256
STEP = 96
UP0, UP1, DN0, DN1, OUT, QS, KS, VS = range(8)
SUB = 2
OUT_AT = 1
LANES = WIDE // SUB
ORDER = (
    "lyhx", "yxlh", "xylh", "ylhx", "hyxl", "xylh", "yhlx", "lxyh",
    "hxly", "yxlh", "xyhl", "xylh", "xyhl", "xyhl", "ylhx", "lyxh",
)
EYES = "xhly"
M_UPC, M_DNC = 0, 1
M_W = 2
M_GBT, M_N2T, M_MXT, M_N1T, M_GA = 42, 43, 44, 45, 46
M_HID, M_GPR = 47, 49
M_PK = 51
M_VEC = 57
M_RED = 62
M_AGC = M_RED + 40 * SUB
M_AGX = M_AGC + 4 * SUB
M_AGF = M_AGX + 4 * SUB
N_MSG = M_AGF + 4 * SUB
WAYS = ("XYLPQ", "XYLPQ", "XYLD", "XYLD")
SCHED = {
    ("qkv", 3): (
        ("X", 0),
    ),
    ("att", 1): (
        ("X", 1),
    ),
    ("att", 3): (
        ("Y", 0), ("L", 0), ("X", 2),
    ),
    "ln2": (
        ("Y", 1), ("L", 1), ("X", 3),
    ),
    ("sh", 0): (
        ("P", 0), ("Q", 0),
    ),
    ("sh", 1): (
        ("D", 2), ("Y", 2), ("L", 2),
    ),
    ("sum", 1): (
        ("P", 1), ("Q", 1), ("D", 3),
    ),
    "weights": (
        ("Y", 3), ("L", 3),
    ),
    ("sh", 2): (
        ("R", 6, 0, 0),
    ),
    ("sum", 5): (
        ("R", 7, 0, 0), ("R", 1, 0, 0),
    ),
    ("sum", 6): (
        ("R", 4, 0, 0),
    ),
    ("bup", 0): (
        ("R", 0, 0, 0), ("R", 3, 0, 0),
    ),
    "ln2b": (
        ("R", 6, 0, 1),
    ),
    ("pr", 0): (
        ("R", 5, 0, 0), ("R", 7, 0, 1), ("R", 1, 0, 1), ("R", 4, 0, 1),
    ),
    ("pr", 1): (
        ("R", 0, 0, 1), ("R", 3, 0, 1),
    ),
    ("pr", 2): (
        ("R", 2, 0, 0), ("R", 5, 1, 0), ("R", 6, 1, 0),
    ),
    ("qs", 0): (
        ("R", 7, 1, 0), ("R", 3, 1, 0), ("R", 4, 1, 0),
    ),
    ("qs", 1): (
        ("R", 1, 1, 0), ("R", 0, 1, 0),
    ),
    ("dwn", 1): (
        ("R", 5, 2, 0),
    ),
    "fin": (
        ("R", 10, 0, 0), ("R", 6, 2, 0), ("R", 9, 0, 0),
    ),
    ("gn1", 0): (
        ("R", 8, 0, 0),
    ),
    ("gn1", 1): (
        ("R", 15, 0, 0), ("R", 2, 1, 0),
    ),
    "ln1b": (
        ("R", 3, 2, 0), ("R", 11, 0, 0), ("R", 14, 0, 0),
    ),
    "tail": (
        ("R", 15, 0, 1), ("R", 7, 2, 0), ("V", 0), ("R", 1, 2, 0), ("R", 14, 0, 1), ("R", 0, 2, 0), ("R", 12, 0, 0),
        ("R", 2, 2, 0), ("R", 5, 3, 0), ("R", 10, 1, 0), ("R", 7, 3, 0), ("R", 1, 3, 0), ("R", 11, 1, 0),
        ("R", 14, 1, 0), ("R", 13, 0, 0), ("R", 2, 3, 0), ("R", 4, 2, 0), ("R", 15, 1, 0), ("R", 6, 3, 0),
        ("R", 11, 2, 0), ("R", 10, 2, 0), ("R", 12, 1, 0), ("R", 9, 1, 0), ("R", 4, 3, 0), ("R", 14, 2, 0),
        ("R", 10, 3, 0), ("R", 13, 1, 0), ("R", 8, 1, 0), ("R", 11, 3, 0), ("R", 3, 3, 0), ("V", 1), ("R", 0, 3, 0),
        ("R", 9, 2, 0), ("R", 12, 2, 0), ("R", 15, 2, 0), ("R", 14, 3, 0), ("V", 2), ("G", 2), ("R", 8, 2, 0),
        ("G", 3), ("R", 13, 2, 0), ("R", 12, 3, 0), ("G", 6), ("R", 9, 3, 0), ("V", 3), ("R", 8, 3, 0),
        ("R", 15, 3, 0), ("R", 13, 3, 0), ("G", 4), ("G", 1), ("G", 0), ("G", 7), ("V", 4), ("G", 5),
    ),
}


def dot_nt(a, b):
    return lax.dot_general(a, b, (((1,), (1,)), ((), ())), preferred_element_type=F32)


def layer_kernel(
    tok_h, cot_h, live, wq_h, wo_h, up_h, dn_h, g1_h, s1_h, g2_h, s2_h,
    lo_h, gt_h, gq_h, gup_h, gdn_h, vec_h,
    g1, s1, g2, s2, gup_o, gdn_o, vec_o,
    wq, wo, upa, dna, tok, gb, nb, mx, pk, pks, xgb, xn2, xmx, xn1, probs, mask, mid, gm, facc,
    hids, gprs, ga, gas, gw, r0, r1, r2, r3, vsum, vbuf, vrecv, ssem, rsem, lsem,
):
    s, f = lax.axis_index("seq"), lax.axis_index("ff")
    bit = {"h": s // 4, "l": (s // 2) % 2, "y": s % 2, "x": f // 2, "c": f % 2}
    mate = {
        "h": (s + 4 - 8 * bit["h"], f), "l": (s + 2 - 4 * bit["l"], f), "y": (s + 1 - 2 * bit["y"], f),
        "x": (s, f + 2 - 4 * bit["x"]), "c": (s, f + 1 - 2 * bit["c"]),
    }
    x, c = bit["x"], bit["c"]

    def at(base, size, unit=128):
        return pl.ds(pl.multiple_of(base, unit), size)

    def local(i, src, dst):
        return pltpu.make_async_copy(src, dst, lsem.at[i])

    loads = {
        0: (tok_h, tok), 1: (cot_h, gb.at[0:ROWS]), 3: (wo_h, wo), 4: (up_h, upa.at[:, 0:SHARD]),
        5: (dn_h, dna.at[0:SHARD]), 6: (cot_h, nb.at[0:ROWS]), 7: (wq_h, wq),
        8: (nb.at[0:ROWS], lo_h), 9: (tok, gt_h), 10: (gup_o, gup_h), 15: (gdn_o, gdn_h), 16: (vec_o, vec_h),
        17: (g1_h, g1), 18: (s1_h, s1), 19: (g2_h, g2), 20: (s2_h, s2),
        **{21 + n: (xgb.at[n * 128:(n + 1) * 128], gq_h.at[n * 128:(n + 1) * 128]) for n in range(4)},
    }

    def load(i):
        local(i, *loads[i]).start()

    def loaded(i):
        local(i, *loads[i]).wait()

    def wq_chunk(n):
        cols = at(n * 768, 768)
        return local(11 + n, wq_h.at[:, cols], wq.at[:, cols])

    def remote(i, to, src, dst):
        return pltpu.make_async_remote_copy(
            src_ref=src, dst_ref=dst, send_sem=ssem.at[i], recv_sem=rsem.at[i], device_id=mate[to], device_id_type=MESH
        )

    def region(k, way, slot):
        yb = bit["y"] if way in ("X", "L") else 1 - bit["y"]
        lb = bit["l"] if way in ("X", "Y") else 1 - bit["l"]
        size = 128 if k < 2 else 64
        start = (2 * yb + lb) * (2 * size) + (k % 2) * size
        if way in ("P", "Q"):
            size //= 2
            start = start + (size if way == "Q" else 0)
        rows = at(start, size, 32)
        if slot is None:
            return up_h.at[rows, :] if k < 2 else dn_h.at[rows, :]
        if k < 2:
            return upa.at[rows, slot * SHARD:(slot + 1) * SHARD]
        return dna.at[at(slot * SHARD + start, size, 32), :]

    def onward(k, way):
        yb = bit["y"] if way == "Q" else 1 - bit["y"]
        lb = bit["l"] if way == "P" else 1 - bit["l"]
        size = 64 if k < 2 else 32
        start = (2 * yb + lb) * (4 * size) + (k % 2) * (2 * size) + (size if way == "Q" else 0)
        if k < 2:
            return upa.at[at(start, size, 32), 2 * SHARD:3 * SHARD]
        return dna.at[at(2 * SHARD + start, size, 32), :]

    def weight(k, way):
        i = M_W + k * 10 + WAYS[k].index(way)
        if way in ("X", "D"):
            return remote(i, "x", region(k, way, None), region(k, way, 2))
        if way in ("Y", "L"):
            return remote(i, way.lower(), region(k, "X", 2), region(k, "X", 2))
        return remote(i, "l" if way == "P" else "y", onward(k, way), onward(k, way))

    def weight_mate(k, way):
        return remote(M_W + k * 10 + 5 + WAYS[k].index(way), "c", region(k, way, 2), region(k, way, 3))

    def relay(way, k):
        weight(k, way).wait()
        if way == "X":
            weight(k, "Y").start()
            weight(k, "L").start()
        elif way == "Y" and k < 2:
            weight(k, "P").start()
        elif way == "L" and k < 2:
            weight(k, "Q").start()
        weight_mate(k, way).start()

    def weight_c(which):
        if which == 0:
            return remote(M_UPC, "c", up_h, upa.at[:, SHARD:2 * SHARD])
        return remote(M_DNC, "c", dn_h, dna.at[SHARD:2 * SHARD])

    def turned(i, ref):
        return remote(i, "c", ref.at[:, 0:PAD], ref.at[:, PAD:2 * PAD])

    def own_hid(slot):
        return wq.at[0:PAD, at(slot * SHARD, SHARD)]

    def own_gpr(slot):
        return wq.at[PAD:2 * PAD, at(slot * SHARD, SHARD)]

    def hid_copy(g):
        return remote(M_HID + g, "c", own_hid(2 * g + 1), hids.at[:, at(g * SHARD, SHARD)])

    def gpr_copy(g):
        return remote(M_GPR + g, "c", own_gpr(2 * g + 1), gprs.at[:, at(g * SHARD, SHARD)])

    def ga_copy():
        return remote(M_GA, "c", ga.at[:, at((1 - c) * 512, 512)], gas)

    def pk_copy(n, xb, part):
        return remote(
            M_PK + n * 3 + part, "c", pk.at[:, at(part * D + (1 - c) * 512 + xb * WIDE, WIDE)],
            pks.at[:, at(part * 512 + xb * WIDE, WIDE)],
        )

    landing = (r0, r1, r2, r3)

    def lanes_of(p):
        return slice((p % SUB) * LANES, (p % SUB + 1) * LANES)

    def bits_of(p):
        return {**bit, "x": 0} if p // SUB < OUT else bit

    def chosen(p, k, mine, xb=None):
        own, order, index = bits_of(p), ORDER[p], []
        for e in EYES:
            if e in order[:k]:
                index.append(own[e])
            elif e == order[k]:
                index.append(own[e] if mine else 1 - own[e])
            elif e == "x" and xb is not None:
                index.append(xb)
            else:
                index.append(slice(None))
        return index

    def red(p, k, xb=None, part=0):
        lead = (p // SUB,) if xb is None else (p // SUB, xb)
        rest = (slice(None), lanes_of(p))
        free = sum(isinstance(e, slice) for e in chosen(p, k, False, xb))
        return remote(
            M_RED + p * 5 + (k + 1 if k else part), ORDER[p][k],
            gw.at[(p // SUB, *chosen(p, k, False, xb), *rest)],
            landing[k].at[(*lead, *[slice(None)] * free, *rest)],
        )

    def add(p, k, xb=None):
        index = chosen(p, k, True, xb)
        free = [n for n, e in enumerate(index) if isinstance(e, slice)]
        count = len(free)
        rest = (slice(None), lanes_of(p))

        def body(i, _):
            place = [(i // (1 << (count - 1 - n))) % 2 for n in range(count)]
            full = list(index)
            for n, e in zip(free, place):
                full[n] = e
            own = (p // SUB, *full, *rest)
            lead = (p // SUB, *place) if xb is None else (p // SUB, xb, *place)
            gw[own] = (gw[own].astype(F32) + landing[k][(*lead, *rest)].astype(F32)).astype(BF)
            return 0

        lax.fori_loop(0, 1 << count, body, 0)

    parts_done = {}

    def first(n, xb, part):
        for p in range(n * SUB, (n + 1) * SUB):
            if n == OUT:
                red(p, 0).start()
            elif ORDER[p][0] != "x":
                red(p, 0, xb, part).start()
            elif (part == 1) == (n < OUT):
                red(p, 0).start()

    def reduced(p, k, part):
        n = p // SUB
        if k == 0 and ORDER[p][0] != "x" and n != OUT:
            xb = part if n < OUT else (1 - x if part == 0 else x)
            red(p, 0, xb, part).wait()
            add(p, 0, xb)
            parts_done[p] = parts_done.get(p, 0) + 1
            if parts_done[p] == 2:
                red(p, 1).start()
        elif k < 3:
            red(p, k).wait()
            add(p, k)
            red(p, k + 1).start()
        else:
            red(p, 3).wait()
            own, rest = bits_of(p), (slice(None), lanes_of(p))
            total = gw[(n, *(own[e] for e in EYES), *rest)].astype(F32) + r3[(n, *rest)].astype(F32)
            if n < OUT:
                cols = slice((n % 2) * WIDE + (p % SUB) * LANES, (n % 2) * WIDE + (p % SUB + 1) * LANES)
            if n in (UP0, UP1):
                gup_o[:, cols] = total
            elif n in (DN0, DN1):
                gdn_o[cols, :] = total.T
            else:
                q = p - OUT * SUB
                quarters(q, own_quarter)[...] = total.astype(BF)
                gather_c(q).start()
                gather_x(q).start()

    def quarters(q, n):
        row = (q // SUB) * 128
        return xgb.at[row:row + 128, at(n * WIDE + (q % SUB) * LANES, LANES)]

    own_quarter = 2 * c + x

    def gather_c(q):
        return remote(M_AGC + q, "c", quarters(q, own_quarter), quarters(q, own_quarter))

    def gather_x(q):
        return remote(M_AGX + q, "x", quarters(q, own_quarter), quarters(q, own_quarter))

    def gather_f(q):
        other = 2 * c + 1 - x
        return remote(M_AGF + q, "c", quarters(q, other), quarters(q, other))

    def vec(n):
        return remote(M_VEC + n, "cxylh"[n], vbuf.at[n], vrecv.at[n])

    def vec_step(n):
        vec(n).wait()
        vbuf[n + 1] = vbuf[n] + vrecv[n]
        if n < 4:
            vec(n + 1).start()

    def handle(event):
        kind = event[0]
        if kind == "R":
            reduced(*event[1:])
        elif kind == "G":
            gather_x(event[1]).wait()
            gather_f(event[1]).start()
        elif kind == "V":
            vec_step(event[1])
        else:
            relay(kind, event[1])

    def poll(name):
        for event in SCHED.get(name, ()):
            handle(event)

    def poll_at(name, i, count):
        for n in range(count):
            if (name, n) in SCHED:
                @pl.when(i == n)
                def _():
                    for event in SCHED[(name, n)]:
                        handle(event)

    limit = (live[0] - f * (ROWS // 15)) * 15

    def keep_of(r):
        rows = r * STEP + lax.broadcasted_iota(jnp.int32, (STEP, 1), 0)
        return jnp.where(rows < limit, 1.0, 0.0).astype(F32)

    def block(r):
        return pl.ds(pl.multiple_of(r * STEP, STEP), STEP)

    def centred(v):
        centre = v - jnp.mean(v, axis=-1, keepdims=True)
        rstd = lax.rsqrt(jnp.mean(centre * centre, axis=-1, keepdims=True) + 1e-05)
        return centre * rstd, rstd

    def turn(src, dst, j):
        cols = at(j * 128, 128)
        dst[cols, 0:PAD] = src[:, cols].T

    for i in (0, 17, 18):
        load(i)
    for n in range(4):
        wq_chunk(n).start()
    barrier = pltpu.get_barrier_semaphore()
    for e in "xylhc":
        pl.semaphore_signal(barrier, inc=1, device_id=mate[e], device_id_type=MESH)
    qi = lax.broadcasted_iota(jnp.int32, (TILE, TILE), 0)
    ki = lax.broadcasted_iota(jnp.int32, (TILE, TILE), 1)
    mask[...] = jnp.where((ki <= qi) & (ki >= qi - lax.rem(qi, 15)), 0.0, -1e30).astype(F32)
    nb[ROWS:PAD, :] = jnp.zeros((PAD - ROWS, D), BF)
    pl.semaphore_wait(barrier, 5)
    for k in range(4):
        weight(k, "X").start()
    for k in (2, 3):
        weight(k, "D").start()
    weight_c(0).start()
    weight_c(1).start()
    for ref in (gb, mx, ga):
        ref[ROWS:PAD, :] = jnp.zeros((PAD - ROWS, D), BF)
    pk[ROWS:PAD, :] = jnp.zeros((PAD - ROWS, 3 * D), BF)
    vsum[...] = jnp.zeros(vsum.shape, F32)
    for i in (0, 17, 18):
        loaded(i)

    def norm_one(r, _):
        xhat, _r = centred(tok[block(r), :].astype(F32))
        nb[block(r), :] = (xhat * g1[...] + s1[...]).astype(BF)
        return 0

    lax.fori_loop(0, ROWS // STEP, norm_one, 0)
    poll("ln1")
    for i in (1, 3, 4, 5, 19, 20):
        load(i)

    def qkv(n, _):
        wq_chunk(n).wait()
        cols = at(n * 768, 768)
        pk[0:ROWS, cols] = jnp.dot(nb[0:ROWS, :], wq[:, cols], preferred_element_type=F32).astype(BF)
        for m in range(2):
            turn(nb, xn1, n * 2 + m)
        poll_at("qkv", n, 4)
        return 0

    lax.fori_loop(0, 4, qkv, 0)
    turned(M_N1T, xn1).start()
    loaded(1)

    def mask_cot(r, _):
        gb[block(r), :] = (keep_of(r) * gb[block(r), :].astype(F32)).astype(BF)
        return 0

    lax.fori_loop(0, ROWS // STEP, mask_cot, 0)
    poll("msk")

    def attend(i, _):
        for h, t in ((i * 2 + n, t) for n in range(2) for t in range(2)):
            cols = [at(part * D + h * 128, 128) for part in range(3)]
            rows = slice(t * TILE, (t + 1) * TILE)
            sc = dot_nt(pk[rows, cols[0]], pk[rows, cols[1]]) * (128 ** -0.5) + mask[...]
            w = jnp.exp(sc - jnp.max(sc, axis=-1, keepdims=True))
            p = (w * (1.0 / jnp.sum(w, axis=-1, keepdims=True))).astype(BF)
            probs[h * 2 + t] = p
            mx[rows, at(h * 128, 128)] = jnp.dot(p, pk[rows, cols[2]], preferred_element_type=F32).astype(BF)
        poll_at("att", i, 4)
        return 0

    lax.fori_loop(0, 4, attend, 0)
    loaded(3)

    def project(n, _):
        cols = at(n * 512, 512)
        facc[:, cols] = jnp.dot(mx[0:ROWS, :], wo[:, cols], preferred_element_type=F32)
        for m in range(4):
            turn(gb, xgb, n * 4 + m)
            turn(mx, xmx, n * 4 + m)
        poll_at("prj", n, 2)
        return 0

    lax.fori_loop(0, 2, project, 0)
    turned(M_GBT, xgb).start()

    loaded(19)
    loaded(20)

    def norm_two(r, _):
        m = tok[block(r), :].astype(F32) + keep_of(r) * facc[block(r), :]
        mid[block(r), :] = m
        xhat, _r = centred(m)
        nb[block(r), :] = (xhat * g2[...] + s2[...]).astype(BF)
        return 0

    lax.fori_loop(0, ROWS // STEP, norm_two, 0)
    poll("ln2")

    def turn_two(j, _):
        turn(nb, xn2, j)
        return 0

    lax.fori_loop(0, D // 128, turn_two, 0)
    turned(M_N2T, xn2).start()
    poll("n2t")

    loaded(4)
    loaded(5)
    wq[ROWS:PAD, 0:FF] = jnp.zeros((PAD - ROWS, FF), BF)
    wq[PAD + ROWS:2 * PAD, 0:FF] = jnp.zeros((PAD - ROWS, FF), BF)

    def shard(j):
        cols = at(j * SHARD, SHARD)
        pre = jnp.dot(nb[0:ROWS, :], upa[:, cols], preferred_element_type=F32)
        sq = pre * pre
        t = jnp.tanh(0.7978845608028654 * pre * (1.0 + 0.044715 * sq))
        half = 0.5 * (1.0 + t)
        wq[0:ROWS, cols] = (pre * half).astype(BF)
        slope = half + 0.5 * pre * (1.0 - t * t) * (0.7978845608028654 * (1.0 + 0.134145 * sq))
        gh = dot_nt(gb[0:ROWS, :], dna[cols, :])
        wq[PAD:PAD + ROWS, cols] = (gh * slope).astype(BF)

    def group(g, _):
        @pl.when(g == 0)
        def _():
            weight_c(0).wait()
            weight_c(1).wait()

        @pl.when(g == 1)
        def _():
            poll("weights")
            for k in range(4):
                for way in WAYS[k]:
                    weight_mate(k, way).wait()

        def one(n, _):
            shard(2 * g + 1 - n)

            @pl.when(n == 0)
            def _():
                hid_copy(g).start()
                gpr_copy(g).start()

            poll_at("sh", 2 * g + n, 4)
            return 0

        lax.fori_loop(0, 2, one, 0)

        mine, theirs = at(2 * g * SHARD, SHARD), at(g * SHARD, SHARD)

        def sums(i, _):
            n = lax.rem(i, 2)
            rows = at(n * 512, 512)
            for m, lhs, top, low, p in ((0, xgb, 0, hids, DN0), (1, xn2, PAD, gprs, UP0)):
                @pl.when(i == 2 * m)
                def _():
                    (gpr_copy if m else hid_copy)(g).wait()

                    @pl.when(g == 0)
                    def _():
                        turned((M_GBT, M_N2T)[m], lhs).wait()

                @pl.when(i // 2 == m)
                def _():
                    rhs = jnp.concatenate([wq[top:top + PAD, mine], low[:, theirs]], axis=0)
                    total = jnp.dot(lhs[rows, :], rhs, preferred_element_type=F32).astype(BF)
                    for half in range(2):
                        gw[p + half, g, n] = total[:, half * WIDE:(half + 1) * WIDE].reshape(2, 2, 128, WIDE)

                    for part in range(2):
                        @pl.when((n == 1) & (g == part))
                        def _():
                            for half in range(2):
                                first(p + half, part, part)

            poll_at("sum", 4 * g + i, 8)
            return 0

        lax.fori_loop(0, 4, sums, 0)
        return 0

    lax.fori_loop(0, 2, group, 0)
    turned(M_MXT, xmx).start()
    load(6)

    def back_up(n, _):
        cols = at(n * 512, 512)
        facc[:, cols] = dot_nt(wq[PAD:PAD + ROWS, 0:FF], upa[cols, :])
        poll_at("bup", n, 2)
        return 0

    lax.fori_loop(0, 2, back_up, 0)
    loaded(6)

    def row_sum(v):
        total = v[0:8]
        for n in range(1, STEP // 8):
            total = total + v[n * 8:(n + 1) * 8]
        return total

    def norm_back(v, gn, gain, n):
        xhat, rstd = centred(v)
        vsum[n] += row_sum(gn * xhat)
        vsum[n + 1] += row_sum(gn)
        e = gn * gain
        return rstd * (e - jnp.mean(e, axis=-1, keepdims=True) - xhat * jnp.mean(e * xhat, axis=-1, keepdims=True))

    def norm_two_back(r, _):
        total = nb[block(r), :].astype(F32) + norm_back(mid[block(r), :], facc[block(r), :], g2[...], 2)
        gm[block(r), :] = total
        ga[block(r), :] = (keep_of(r) * total).astype(BF)
        return 0

    lax.fori_loop(0, ROWS // STEP, norm_two_back, 0)
    ga_copy().start()
    poll("ln2b")

    def back_out(n, _):
        cols = at(n * 512, 512)
        mx[0:ROWS, cols] = dot_nt(ga[0:ROWS, :], wo[cols, :]).astype(BF)
        return 0

    lax.fori_loop(0, 2, back_out, 0)
    poll("bout")

    def out_sums(n, _):
        rows = at(n * 512, 512)
        rhs = jnp.concatenate([ga[:, at(c * 512, 512)], gas[...]], axis=0)
        total = jnp.dot(xmx[rows, :], rhs, preferred_element_type=F32).astype(BF)
        for half in range(2):
            gw[OUT, half, n] = total[:, half * WIDE:(half + 1) * WIDE].reshape(2, 2, 128, WIDE)
        return 0

    def heads_back(h0):
        for h, t in ((h0 + n, t) for n in range(2) for t in range(2)):
            cols = [at(part * D + h * 128, 128) for part in range(3)]
            rows = slice(t * TILE, (t + 1) * TILE)
            q, k, v = (pk[rows, col] for col in cols)
            o = mx[rows, at(h * 128, 128)]
            pb = probs[h * 2 + t]
            p = pb.astype(F32)
            dp = dot_nt(o, v)
            gs = (p * (dp - jnp.sum(p * dp, axis=-1, keepdims=True))).astype(BF)
            gv = lax.dot_general(pb, o, (((0,), (0,)), ((), ())), preferred_element_type=F32)
            gq = jnp.dot(gs, k, preferred_element_type=F32) * (128 ** -0.5)
            gk = lax.dot_general(gs, q, (((0,), (0,)), ((), ())), preferred_element_type=F32) * (128 ** -0.5)
            for col, g in zip(cols, (gq, gk, gv)):
                pk[rows, col] = g.astype(BF)

    def pair(i, _):
        later = lax.rem(i, 2)
        cb = c + (1 - i // 2) * (1 - 2 * c)
        xb = x + (1 - later) * (1 - 2 * x)
        heads_back(cb * 4 + xb * 2)
        for n in range(2):
            @pl.when(i == n)
            def _():
                for part in range(3):
                    pk_copy(n, 1 - x if n == 0 else x, part).start()

        poll_at("pr", i, 4)

        @pl.when(i == OUT_AT)
        def _():
            turned(M_MXT, xmx).wait()
            ga_copy().wait()
            lax.fori_loop(0, 2, out_sums, 0)
            first(OUT, None, 0)
            poll("osum")

        @pl.when(i >= 2)
        def _():
            @pl.when(i == 2)
            def _():
                turned(M_N1T, xn1).wait()

            for n in range(2):
                @pl.when(later == n)
                def _():
                    for part in range(3):
                        pk_copy(n, 1 - x if n == 0 else x, part).wait()

            def body(n, _):
                rows = at(n * 512, 512)
                rhs = jnp.concatenate(
                    [
                        jnp.concatenate([pk[:, at(part * D + c * 512 + xb * WIDE, WIDE)] for part in range(3)], axis=1),
                        jnp.concatenate([pks[:, at(part * 512 + xb * WIDE, WIDE)] for part in range(3)], axis=1),
                    ],
                    axis=0,
                )
                total = jnp.dot(xn1[rows, :], rhs, preferred_element_type=F32).astype(BF)
                for part in range(3):
                    gw[QS + part, xb, n] = total[:, part * WIDE:(part + 1) * WIDE].reshape(2, 2, 128, WIDE)
                return 0

            lax.fori_loop(0, 2, body, 0)
            for n in range(2):
                @pl.when(later == n)
                def _():
                    for p in (QS, KS, VS):
                        first(p, 1 - x if n == 0 else x, n)
                    poll(("qs", n))

        return 0

    lax.fori_loop(0, 4, pair, 0)

    def down(n, _):
        cols = at(n * 512, 512)
        facc[:, cols] = jnp.dot(wq[0:ROWS, 0:FF], dna[:, cols], preferred_element_type=F32)
        poll_at("dwn", n, 2)
        return 0

    lax.fori_loop(0, 2, down, 0)
    load(7)

    def finish_out(r, _):
        nb[block(r), :] = (mid[block(r), :] + keep_of(r) * facc[block(r), :]).astype(BF)
        return 0

    lax.fori_loop(0, ROWS // STEP, finish_out, 0)
    load(8)
    poll("fin")
    loaded(7)

    def back_qkv(n, _):
        cols = at(n * 512, 512)
        facc[:, cols] = dot_nt(pk[0:ROWS, :], wq[cols, :])
        poll_at("gn1", n, 2)
        return 0

    lax.fori_loop(0, 2, back_qkv, 0)

    def norm_one_back(r, _):
        total = gm[block(r), :] + norm_back(tok[block(r), :].astype(F32), facc[block(r), :], g1[...], 0)
        tok[block(r), :] = total.astype(BF)
        return 0

    lax.fori_loop(0, ROWS // STEP, norm_one_back, 0)
    load(9)
    vbuf[0] = jnp.concatenate(
        [jnp.sum(vsum[n], axis=0, keepdims=True) for n in range(4)] + [jnp.zeros((4, D), F32)], axis=0
    )
    vec(0).start()
    poll("ln1b")
    poll("tail")
    vec_o[...] = vbuf[5, :, at(s * 128, 128)]
    for i in (10, 15, 16):
        load(i)
    for n in range(4):
        for q in range(n * SUB, (n + 1) * SUB):
            gather_c(q).wait()
            gather_f(q).wait()
        load(21 + n)
    for i in (8, 9, 10, 15, 16, 21, 22, 23, 24):
        loaded(i)


def result_kernel(*refs):
    lo, gt, gq, gup, gdn, vec = refs[:6]
    lo_o, gt_o, gqkv_o, gout_o, gup_o, gdn_o = refs[6:12]
    lov, gtv, gqv, gupv, gdnv, vecv, gqkv, gout, sem = refs[16:]
    pairs = [(gq, gqv), (lo, lov), (gt, gtv), (gup, gupv), (gdn, gdnv), (vec, vecv)]
    pairs += [(lov, lo_o), (gtv, gt_o), (gupv, gup_o), (gdnv, gdn_o), (gout, gout_o)]
    pairs += [(vecv.at[n], refs[12 + n]) for n in range(4)]
    pairs += [(gqkv.at[:, n * D:(n + 1) * D], gqkv_o.at[:, n * D:(n + 1) * D]) for n in range(3)]
    copies = [pltpu.make_async_copy(a, b, sem.at[n]) for n, (a, b) in enumerate(pairs)]
    for n in range(6):
        copies[n].start()
    copies[0].wait()
    for n in range(3):
        gqkv[:, n * D:(n + 1) * D] = gqv[(n + 1) * 128:(n + 2) * 128, :].astype(F32)
        copies[15 + n].start()
    gout[...] = gqv[0:128, :].astype(F32)
    copies[10].start()
    for n in range(1, 6):
        copies[n].wait()
        for m in ((n + 5,) if n < 5 else range(11, 15)):
            copies[m].start()
    for n in range(6, 18):
        copies[n].wait()


def fused(
    tokens, cotangent, live_items, qkv_weight, out_weight, up_weight, down_weight,
    gain_one, shift_one, gain_two, shift_two,
):
    rows_of = [v.reshape(1, D) for v in (gain_one, shift_one, gain_two, shift_two)]
    hbm = pl.BlockSpec(memory_space=pl.ANY)
    shape = jax.ShapeDtypeStruct
    outs = pl.pallas_call(
        layer_kernel,
        name="layer",
        out_shape=(
            shape((ROWS, D), BF), shape((ROWS, D), BF), shape((512, D), BF),
            shape((128, SHARD), F32), shape((SHARD, 128), F32), shape((8, 128), F32),
        ),
        in_specs=[hbm, hbm, pl.BlockSpec(memory_space=pltpu.SMEM)] + [hbm] * 8,
        out_specs=[hbm] * 6,
        scratch_shapes=[
            *[pltpu.VMEM((1, D), F32)] * 4,
            pltpu.VMEM((128, SHARD), F32), pltpu.VMEM((SHARD, 128), F32), pltpu.VMEM((8, 128), F32),
            pltpu.VMEM((D, 3 * D), BF), pltpu.VMEM((D, D), BF), pltpu.VMEM((D, FF), BF), pltpu.VMEM((FF, D), BF),
            pltpu.VMEM((ROWS, D), BF), pltpu.VMEM((PAD, D), BF), pltpu.VMEM((PAD, D), BF), pltpu.VMEM((PAD, D), BF),
            pltpu.VMEM((PAD, 3 * D), BF), pltpu.VMEM((PAD, 3 * 512), BF),
            pltpu.VMEM((D, 2 * PAD), BF), pltpu.VMEM((D, 2 * PAD), BF), pltpu.VMEM((D, 2 * PAD), BF),
            pltpu.VMEM((D, 2 * PAD), BF),
            pltpu.VMEM((16, TILE, TILE), BF), pltpu.VMEM((TILE, TILE), F32),
            pltpu.VMEM((ROWS, D), F32), pltpu.VMEM((ROWS, D), F32), pltpu.VMEM((ROWS, D), F32),
            pltpu.VMEM((PAD, 2 * SHARD), BF), pltpu.VMEM((PAD, 2 * SHARD), BF),
            pltpu.VMEM((PAD, D), BF), pltpu.VMEM((PAD, 512), BF),
            pltpu.VMEM((8, 2, 2, 2, 2, 128, WIDE), BF),
            pltpu.VMEM((8, 2, 2, 2, 128, WIDE), BF), pltpu.VMEM((8, 2, 2, 128, WIDE), BF),
            pltpu.VMEM((8, 2, 128, WIDE), BF), pltpu.VMEM((8, 128, WIDE), BF),
            pltpu.VMEM((4, 8, D), F32), pltpu.VMEM((6, 8, D), F32), pltpu.VMEM((5, 8, D), F32),
            pltpu.SemaphoreType.DMA((N_MSG,)), pltpu.SemaphoreType.DMA((N_MSG,)), pltpu.SemaphoreType.DMA((25,)),
        ],
        compiler_params=pltpu.CompilerParams(
            collective_id=0, has_side_effects=True, vmem_limit_bytes=67_043_328
        ),
    )(tokens, cotangent, live_items, qkv_weight, out_weight, up_weight, down_weight, *rows_of)
    return pl.pallas_call(
        result_kernel,
        name="results",
        out_shape=(
            shape((ROWS, D), BF), shape((ROWS, D), BF), shape((128, 3 * D), F32), shape((128, D), F32),
            shape((128, SHARD), F32), shape((SHARD, 128), F32),
            shape((128,), F32), shape((128,), F32), shape((128,), F32), shape((128,), F32),
        ),
        in_specs=[hbm] * 6,
        out_specs=[hbm] * 10,
        scratch_shapes=[
            pltpu.VMEM((ROWS, D), BF), pltpu.VMEM((ROWS, D), BF), pltpu.VMEM((512, D), BF),
            pltpu.VMEM((128, SHARD), F32), pltpu.VMEM((SHARD, 128), F32), pltpu.VMEM((8, 128), F32),
            pltpu.VMEM((128, 3 * D), F32), pltpu.VMEM((128, D), F32), pltpu.SemaphoreType.DMA((18,)),
        ],
    )(*outs)


IN_SPECS = (
    P(("seq", "ff"), None), P(("seq", "ff"), None), P("seq"), P(), P(), P(None, "ff"), P("ff", None),
    P(), P(), P(), P(),
)
OUT_SPECS = (
    P(("seq", "ff"), None), P(("seq", "ff"), None), P("seq", None), P("seq", None), P("seq", "ff"),
    P("ff", "seq"), P("seq"), P("seq"), P("seq"), P("seq"),
)


def solution(mesh):
    body = fused if (mesh.shape["seq"], mesh.shape["ff"]) == (8, 4) else general
    return jax.shard_map(body, mesh=mesh, in_specs=IN_SPECS, out_specs=OUT_SPECS, check_vma=False)
```

```python
import jax
import jax.numpy as jnp
from jax import lax
from jax.experimental import pallas as pl
from jax.experimental.pallas import tpu as pltpu
from jax.sharding import PartitionSpec as P

HEADS = 8
HEAD_DIM = 128
ITEM_LEN = 15
BF = jnp.bfloat16
F32 = jnp.float32


def layer_norm(content_matrix, gain, shift):
    centre = content_matrix - jnp.mean(content_matrix, axis=-1, keepdims=True)
    spread = jnp.mean(centre * centre, axis=-1, keepdims=True)
    return centre * lax.rsqrt(spread + 1e-05) * gain + shift


def tile_allowed(tile_rows):
    position = jnp.arange(tile_rows, dtype=jnp.int32)
    same_item = position[:, None] // ITEM_LEN == position[None, :] // ITEM_LEN
    return same_item & (position[None, :] <= position[:, None])


def dot(a, b):
    return jnp.dot(a, b, preferred_element_type=F32)


def tiles_of(x, tile):
    return x.reshape(-1, tile, HEAD_DIM)


def scores_of(q, k, allowed):
    s = jnp.einsum("tqd,tkd->tqk", q, k, preferred_element_type=F32) * HEAD_DIM ** (-0.5)
    return jnp.where(allowed, s, -1e30)


def attend_forward(packed, tile):
    allowed = tile_allowed(tile)
    width = HEADS * HEAD_DIM
    mixed, saved = [], []
    for h in range(HEADS):
        q, k, v = (tiles_of(packed[:, p * width + h * HEAD_DIM:][:, :HEAD_DIM], tile) for p in range(3))
        probs = jax.nn.softmax(scores_of(q, k, allowed), axis=-1)
        o = jnp.einsum("tqk,tkd->tqd", probs.astype(BF), v, preferred_element_type=F32)
        mixed.append(o.astype(BF).reshape(-1, HEAD_DIM))
        saved.append(probs)
    return jnp.concatenate(mixed, axis=1), saved


def attend_backward(packed, saved, grad_mixed, tile):
    width = HEADS * HEAD_DIM
    scale = HEAD_DIM ** (-0.5)
    parts = ([], [], [])
    for h in range(HEADS):
        q, k, v = (tiles_of(packed[:, p * width + h * HEAD_DIM:][:, :HEAD_DIM], tile) for p in range(3))
        o = tiles_of(grad_mixed[:, h * HEAD_DIM:][:, :HEAD_DIM], tile)
        probs = saved[h]
        dp = jnp.einsum("tqd,tkd->tqk", o, v, preferred_element_type=F32)
        gv = jnp.einsum("tqk,tqd->tkd", probs.astype(BF), o, preferred_element_type=F32)
        gs = (probs * (dp - jnp.sum(probs * dp, axis=-1, keepdims=True))).astype(BF)
        gq = jnp.einsum("tqk,tkd->tqd", gs, k, preferred_element_type=F32) * scale
        gk = jnp.einsum("tqk,tqd->tkd", gs, q, preferred_element_type=F32) * scale
        for part, g in zip(parts, (gq, gk, gv)):
            part.append(g.astype(BF).reshape(-1, HEAD_DIM))
    return jnp.concatenate(parts[0] + parts[1] + parts[2], axis=1)


def general(
    tokens, cotangent, live_items, qkv_weight, out_weight, up_weight, down_weight,
    gain_one, shift_one, gain_two, shift_two,
):
    rows = tokens.shape[0]
    items = rows // ITEM_LEN
    tile = ITEM_LEN * (16 if items % 16 == 0 else 1)
    place = lax.axis_index("ff") * items + jnp.arange(rows, dtype=jnp.int32) // ITEM_LEN
    keep = (place < live_items[0]).astype(F32)[:, None]
    up_all = lax.all_gather(up_weight, "ff", axis=1, tiled=True)
    down_all = lax.all_gather(down_weight, "ff", axis=0, tiled=True)
    inputs = tokens.astype(F32)
    normed, norm_one_pull = jax.vjp(layer_norm, inputs, gain_one, shift_one)
    normed = normed.astype(BF)
    packed = dot(normed, qkv_weight).astype(BF)
    mixed, saved = attend_forward(packed, tile)
    middle = inputs + keep * dot(mixed, out_weight)
    normed_two, norm_two_pull = jax.vjp(layer_norm, middle, gain_two, shift_two)
    normed_two = normed_two.astype(BF)
    grad_out = cotangent.astype(F32)
    grad_branch = (keep * grad_out).astype(BF)
    pre = dot(normed_two, up_all)
    hidden = jax.nn.gelu(pre).astype(BF)
    layer_out = (middle + keep * dot(hidden, down_all)).astype(BF)
    grad_hidden = dot(grad_branch, down_all.T)
    grad_pre = jax.vjp(jax.nn.gelu, pre)[1](grad_hidden)[0].astype(BF)
    grad_down = dot(hidden.T, grad_branch).astype(BF)
    grad_up = dot(normed_two.T, grad_pre).astype(BF)
    grad_middle_norm, grad_gain_two, grad_shift_two = norm_two_pull(dot(grad_pre, up_all.T))
    grad_middle = grad_out + grad_middle_norm
    grad_attended = (keep * grad_middle).astype(BF)
    grad_out_weight = dot(mixed.T, grad_attended).astype(BF)
    grad_mixed = dot(grad_attended, out_weight.T).astype(BF)
    grad_packed = attend_backward(packed, saved, grad_mixed, tile)
    grad_qkv = dot(normed.T, grad_packed).astype(BF)
    grad_inputs, grad_gain_one, grad_shift_one = norm_one_pull(dot(grad_packed, qkv_weight.T))
    grad_tokens = (grad_middle + grad_inputs).astype(BF)

    def scatter(x, axis, dim):
        return lax.psum_scatter(x, axis, scatter_dimension=dim, tiled=True)

    grad_up = scatter(scatter(grad_up, "ff", 1), "seq", 0).astype(F32)
    grad_down = scatter(scatter(grad_down, "ff", 0), "seq", 1).astype(F32)
    shared = [
        lax.psum(scatter(g, "seq", 0), "ff").astype(F32)
        for g in (grad_qkv, grad_out_weight, grad_gain_one, grad_shift_one, grad_gain_two, grad_shift_two)
    ]
    return (layer_out, grad_tokens, shared[0], shared[1], grad_up, grad_down, *shared[2:])


MESH = pl.DeviceIdType.MESH
ROWS, PAD, D, FF, SHARD = 480, 512, 1024, 2048, 512
TILE = 240
WIDE = 256
STEP = 240
UP0, UP1, DN0, DN1, OUT, QS, KS, VS = range(8)
SUB = 2
OUT_AT = 0
LANES = WIDE // SUB
ORDER = (
    "xylh", "lyhx", "lxhy", "lxhy", "ylxh", "xlhy", "yxhl", "ylxh",
    "xlyh", "yxlh", "yxlh", "lyxh", "xlhy", "yxlh", "yxlh", "yxlh",
)
EYES = "xhly"
M_UPC, M_DNC = 0, 1
M_W = 2
M_MATE = 22
M_GBT, M_N2T, M_MXT, M_N1T, M_GA = 24, 25, 26, 27, 28
M_HID, M_GPR = 29, 31
M_PK = 33
M_VEC = 35
M_RED = 40
M_AGX = M_RED + 48 * SUB
M_AG = M_AGX + 4 * SUB
N_MSG = M_AG + 4
WAYS = ("XYLPQ", "XYLD", "XYLPQ", "XYLD")
SCHED = {
    ("att", 0): (
        ("X", 0),
    ),
    ("att", 1): (
        ("X", 1),
    ),
    "n2t": (
        ("X", 2),
    ),
    ("sh", 0): (
        ("Y", 0), ("L", 0),
    ),
    ("bk", 1): (
        ("X", 3),
    ),
    ("sum", 0): (
        ("Y", 1), ("L", 1),
    ),
    ("sum", 1): (
        ("Y", 2), ("L", 2),
    ),
    "wup": (
        ("D", 1), ("P", 0), ("Q", 0), ("D", 3),
    ),
    ("sh", 3): (
        ("Y", 3), ("L", 3),
    ),
    "wdn": (
        ("P", 2), ("Q", 2),
    ),
    ("sum", 2): (
        ("R", 4, 0, 0), ("R", 1, 0, 0),
    ),
    "bup": (
        ("R", 6, 0, 0), ("R", 2, 0, 0),
    ),
    "ln2b": (
        ("R", 7, 0, 0), ("R", 3, 0, 0),
    ),
    ("pr", 0): (
        ("R", 4, 0, 1), ("R", 1, 0, 1), ("R", 5, 0, 0),
    ),
    "osum": (
        ("R", 6, 0, 1), ("R", 2, 0, 1),
    ),
    ("pr", 1): (
        ("R", 7, 0, 1), ("R", 3, 0, 1), ("R", 0, 0, 0),
    ),
    ("qs", 0): (
        ("R", 4, 1, 0), ("R", 1, 1, 0),
    ),
    ("qs", 1): (
        ("R", 5, 1, 0),
    ),
    "dwn": (
        ("R", 8, 0, 0),
    ),
    "fin": (
        ("R", 9, 0, 0), ("R", 7, 1, 0), ("R", 6, 1, 0),
    ),
    "gn1": (
        ("R", 0, 1, 0), ("R", 11, 0, 0), ("R", 2, 1, 0),
    ),
    "ln1b": (
        ("R", 1, 2, 0), ("R", 10, 0, 0), ("R", 3, 1, 0), ("R", 11, 0, 1),
    ),
    "tail": (
        ("R", 13, 0, 0), ("V", 0), ("R", 5, 2, 0), ("R", 14, 0, 0), ("R", 8, 1, 0), ("R", 12, 0, 0), ("R", 4, 2, 0),
        ("R", 6, 2, 0), ("R", 15, 0, 0), ("R", 0, 2, 0), ("R", 9, 1, 0), ("R", 2, 2, 0), ("R", 10, 0, 1),
        ("R", 7, 2, 0), ("R", 1, 3, 0), ("V", 1), ("R", 3, 2, 0), ("R", 13, 0, 1), ("R", 12, 1, 0), ("R", 6, 3, 0),
        ("R", 4, 3, 0), ("R", 10, 1, 0), ("R", 14, 0, 1), ("R", 0, 3, 0), ("R", 9, 2, 0), ("R", 7, 3, 0),
        ("R", 13, 1, 0), ("R", 15, 0, 1), ("R", 10, 2, 0), ("R", 12, 2, 0), ("R", 14, 1, 0), ("R", 11, 1, 0),
        ("R", 5, 3, 0), ("R", 13, 2, 0), ("R", 9, 3, 0), ("R", 8, 2, 0), ("R", 15, 1, 0), ("R", 2, 3, 0),
        ("R", 10, 3, 0), ("R", 14, 2, 0), ("V", 2), ("R", 11, 2, 0), ("R", 3, 3, 0), ("G", 1), ("R", 12, 3, 0),
        ("R", 13, 3, 0), ("G", 2), ("R", 15, 2, 0), ("R", 8, 3, 0), ("G", 4), ("V", 3), ("R", 14, 3, 0), ("G", 5),
        ("R", 11, 3, 0), ("G", 0), ("R", 15, 3, 0), ("G", 6), ("V", 4), ("G", 3), ("G", 7),
    ),
}


def dot_nt(a, b):
    return lax.dot_general(a, b, (((1,), (1,)), ((), ())), preferred_element_type=F32)


def dot_tn(a, b):
    return lax.dot_general(a, b, (((0,), (0,)), ((), ())), preferred_element_type=F32)


def layer_kernel(
    tok_h, cot_h, live, wq_h, wo_h, up_h, dn_h, g1_h, s1_h, g2_h, s2_h,
    lo_h, gt_h, gq_h, gup_h, gdn_h, vec_h,
    g1, s1, g2, s2, gup_o, gdn_o, vec_o,
    wq, wo, upa, dna, tok, gb, nb, mx, pk, pks, xgb, xn2, xmx, xn1, probs, mask, mid, gm, facc,
    hids, gprs, gas, gw, r0, r1, r2, r3, vsum, vbuf, vrecv, ssem, rsem, lsem,
):
    s, f = lax.axis_index("seq"), lax.axis_index("ff")
    bit = {"h": s // 4, "l": (s // 2) % 2, "y": s % 2, "x": f // 2, "c": f % 2}
    mate = {
        "h": (s + 4 - 8 * bit["h"], f), "l": (s + 2 - 4 * bit["l"], f), "y": (s + 1 - 2 * bit["y"], f),
        "x": (s, f + 2 - 4 * bit["x"]), "c": (s, f + 1 - 2 * bit["c"]),
        "lh": (s + 6 - 4 * bit["l"] - 8 * bit["h"], f),
    }
    x, c = bit["x"], bit["c"]

    def at(base, size, unit=128):
        return pl.ds(pl.multiple_of(base, unit), size)

    ga = xn2.at[0:PAD]

    def local(i, src, dst):
        return pltpu.make_async_copy(src, dst, lsem.at[i])

    loads = {
        0: (tok_h, tok), 1: (cot_h, gb.at[0:ROWS]), 3: (wo_h, wo), 4: (up_h, upa.at[:, 0:SHARD]),
        5: (dn_h, dna.at[0:SHARD]), 6: (cot_h, nb.at[0:ROWS]), 7: (wq_h, wq),
        8: (nb.at[0:ROWS], lo_h), 9: (tok, gt_h), 10: (gup_o, gup_h), 15: (gdn_o, gdn_h), 16: (vec_o, vec_h),
        17: (g1_h, g1), 18: (s1_h, s1), 19: (g2_h, g2), 20: (s2_h, s2),
        **{21 + n: (xgb.at[n * 128:(n + 1) * 128], gq_h.at[n * 128:(n + 1) * 128]) for n in range(4)},
    }

    def load(i):
        local(i, *loads[i]).start()

    def loaded(i):
        local(i, *loads[i]).wait()

    def wq_chunk(n):
        cols = at(n * 768, 768)
        return local(11 + n, wq_h.at[:, cols], wq.at[:, cols])

    def remote(i, to, src, dst):
        return pltpu.make_async_remote_copy(
            src_ref=src, dst_ref=dst, send_sem=ssem.at[i], recv_sem=rsem.at[i], device_id=mate[to], device_id_type=MESH
        )

    def region(k, way, slot):
        yb = bit["y"] if way in ("X", "L") else 1 - bit["y"]
        lb = bit["l"] if way in ("X", "Y") else 1 - bit["l"]
        size = 128 if k < 2 else 64
        start = (2 * yb + lb) * (2 * size) + (k % 2) * size
        if way in ("P", "Q"):
            size //= 2
            start = start + (size if way == "Q" else 0)
        rows = at(start, size, 32)
        if slot is None:
            return up_h.at[rows, :] if k < 2 else dn_h.at[rows, :]
        if k < 2:
            return upa.at[rows, slot * SHARD:(slot + 1) * SHARD]
        return dna.at[at(slot * SHARD + start, size, 32), :]

    def onward(k, way):
        yb = bit["y"] if way == "Q" else 1 - bit["y"]
        lb = bit["l"] if way == "P" else 1 - bit["l"]
        size = 64 if k < 2 else 32
        start = (2 * yb + lb) * (4 * size) + (k % 2) * (2 * size) + (size if way == "Q" else 0)
        if k < 2:
            return upa.at[at(start, size, 32), 2 * SHARD:3 * SHARD]
        return dna.at[at(2 * SHARD + start, size, 32), :]

    def weight(k, way):
        i = M_W + k * 5 + WAYS[k].index(way)
        if way in ("X", "D"):
            return remote(i, "x", region(k, way, None), region(k, way, 2))
        if way in ("Y", "L"):
            return remote(i, way.lower(), region(k, "X", 2), region(k, "X", 2))
        return remote(i, "l" if way == "P" else "y", onward(k, way), onward(k, way))

    def weight_mate(k, way):
        return remote(M_MATE + k // 2, "c", region(k, way, 2), region(k, way, 3))

    def weight_mates(m):
        if m == 0:
            return remote(M_MATE, "c", upa.at[:, 2 * SHARD:3 * SHARD], upa.at[:, 3 * SHARD:4 * SHARD])
        return remote(M_MATE + 1, "c", dna.at[2 * SHARD:3 * SHARD], dna.at[3 * SHARD:4 * SHARD])

    def relay(way, k):
        weight(k, way).wait()
        if way == "X":
            weight(k, "Y").start()
            weight(k, "L").start()
        elif way == "Y" and k % 2 == 0:
            weight(k, "P").start()
        elif way == "L" and k % 2 == 0:
            weight(k, "Q").start()
        weight_mate(k, way).start()

    def weight_c(which):
        if which == 0:
            return remote(M_UPC, "c", up_h, upa.at[:, SHARD:2 * SHARD])
        return remote(M_DNC, "c", dn_h, dna.at[SHARD:2 * SHARD])

    def turned(i, ref):
        return remote(i, "c", ref.at[:, 0:PAD], ref.at[:, PAD:2 * PAD])

    def own_hid(slot):
        return wq.at[0:PAD, at(slot * SHARD, SHARD)]

    def own_gpr(slot):
        return wq.at[PAD:2 * PAD, at(slot * SHARD, SHARD)]

    def hid_copy(g):
        return remote(M_HID + g, "c", own_hid(2 * g + 1), hids)

    def gpr_copy(g):
        return remote(M_GPR + g, "c", own_gpr(2 * g + 1), gprs)

    def ga_copy():
        return remote(M_GA, "c", ga.at[:, at((1 - c) * 512, 512)], gas)

    def pk_copy(n, xb, part):
        return remote(
            M_PK + n, "c", pk.at[:, at(part * D + (1 - c) * 512 + xb * WIDE, WIDE)],
            pks.at[:, at(part * 512 + xb * WIDE, WIDE)],
        )

    def pk_copies(n):
        return remote(M_PK + n, "c", pks.at[:, 0:3 * WIDE], pks.at[:, 0:3 * WIDE])

    landing = (r0, r1, r2, r3)

    def lanes_of(p):
        return slice((p % SUB) * LANES, (p % SUB + 1) * LANES)

    def bits_of(p):
        return {**bit, "x": 0} if p // SUB < OUT else bit

    def chosen(p, k, mine, xb=None):
        own, order, index = bits_of(p), ORDER[p], []
        for e in EYES:
            if e in order[:k]:
                index.append(own[e])
            elif e == order[k]:
                index.append(own[e] if mine else 1 - own[e])
            elif e == "x" and xb is not None:
                index.append(xb)
            else:
                index.append(slice(None))
        return index

    def red(p, k, xb=None, part=0):
        lead = (p // SUB,) if xb is None else (p // SUB, xb)
        rest = (slice(None), lanes_of(p))
        free = sum(isinstance(e, slice) for e in chosen(p, k, False, xb))
        return remote(
            M_RED + p * 6 + (k + 1 if k else part), ORDER[p][k],
            gw.at[(p // SUB, *chosen(p, k, False, xb), *rest)],
            landing[k].at[(*lead, *[slice(None)] * free, *rest)],
        )

    def add(p, k, xb=None):
        index = chosen(p, k, True, xb)
        free = [n for n, e in enumerate(index) if isinstance(e, slice)]
        count = len(free)
        rest = (slice(None), lanes_of(p))

        def body(i, _):
            place = [(i // (1 << (count - 1 - n))) % 2 for n in range(count)]
            full = list(index)
            for n, e in zip(free, place):
                full[n] = e
            own = (p // SUB, *full, *rest)
            lead = (p // SUB, *place) if xb is None else (p // SUB, xb, *place)
            gw[own] = (gw[own].astype(F32) + landing[k][(*lead, *rest)].astype(F32)).astype(BF)
            return 0

        lax.fori_loop(0, 1 << count, body, 0)

    def line(p):
        own, rest, copies = bits_of(p), (slice(None), lanes_of(p)), []
        for n, to in enumerate(("l", "h", "lh")):
            block = {e: 1 - own[e] if e in to else own[e] for e in EYES}
            copies.append(remote(
                M_RED + p * 6 + 3 + n, to, gw.at[(p // SUB, *(block[e] for e in EYES), *rest)], lands(p)[n].at[rest]
            ))
        return copies

    def lands(p):
        n = p // SUB
        return (r2.at[n, 0], r2.at[n, 1], r3.at[n])

    def go(p, k):
        for copy in line(p) if ORDER[p][k] == "z" else (red(p, k),):
            copy.start()

    parts_done = {}

    def first(n, xb, part):
        for p in range(n * SUB, (n + 1) * SUB):
            if n == OUT:
                red(p, 0).start()
            elif ORDER[p][0] != "x":
                red(p, 0, xb, part).start()
            elif (part == 1) == (n < OUT):
                red(p, 0).start()

    def reduced(p, k, part):
        n = p // SUB
        if k == 0 and ORDER[p][0] != "x" and n != OUT:
            xb = part if n < OUT else (1 - x if part == 0 else x)
            red(p, 0, xb, part).wait()
            add(p, 0, xb)
            parts_done[p] = parts_done.get(p, 0) + 1
            if parts_done[p] == 2:
                go(p, 1)
        elif k < len(ORDER[p]) - 1:
            red(p, k).wait()
            add(p, k)
            go(p, k + 1)
        else:
            own, rest = bits_of(p), (slice(None), lanes_of(p))
            total = gw[(n, *(own[e] for e in EYES), *rest)].astype(F32)
            if k == 2:
                for copy, land in zip(line(p), lands(p)):
                    copy.wait()
                    total = total + land[rest].astype(F32)
            else:
                red(p, 3).wait()
                total = total + r3[(n, *rest)].astype(F32)
            if n < OUT:
                cols = slice((n % 2) * WIDE + (p % SUB) * LANES, (n % 2) * WIDE + (p % SUB + 1) * LANES)
            if n in (UP0, UP1):
                gup_o[:, cols] = total
            elif n in (DN0, DN1):
                gdn_o[cols, :] = total.T
            else:
                q = p - OUT * SUB
                quarters(q, own_quarter)[...] = total.astype(BF)
                gather_c(q).start()
                gather_x(q).start()

    def quarters(q, n):
        row = (q // SUB) * 128
        return xgb.at[row:row + 128, at(n * WIDE + (q % SUB) * LANES, LANES)]

    own_quarter = 2 * c + x

    def gather_c(q):
        return remote(M_AG + q // SUB, "c", quarters(q, own_quarter), quarters(q, own_quarter))

    def gather_x(q):
        return remote(M_AGX + q, "x", quarters(q, own_quarter), quarters(q, own_quarter))

    def gather_f(q):
        other = 2 * c + 1 - x
        return remote(M_AG + q // SUB, "c", quarters(q, other), quarters(q, other))

    def gathered(n):
        half = xgb.at[n * 128:(n + 1) * 128, 0:2 * WIDE]
        return remote(M_AG + n, "c", half, half)

    def vec(n):
        return remote(M_VEC + n, "cxylh"[n], vbuf.at[n], vrecv.at[n])

    def vec_step(n):
        vec(n).wait()
        vbuf[n + 1] = vbuf[n] + vrecv[n]
        if n < 4:
            vec(n + 1).start()

    def handle(event):
        kind = event[0]
        if kind == "R":
            reduced(*event[1:])
        elif kind == "G":
            gather_x(event[1]).wait()
            gather_f(event[1]).start()
        elif kind == "V":
            vec_step(event[1])
        else:
            relay(kind, event[1])

    def poll(name):
        for event in SCHED.get(name, ()):
            handle(event)

    def poll_at(name, i, places):
        for n in places:
            if (name, n) in SCHED:
                @pl.when(i == n)
                def _():
                    for event in SCHED[(name, n)]:
                        handle(event)

    limit = (live[0] - f * (ROWS // 15)) * 15

    def keep_of(r):
        rows = r * STEP + lax.broadcasted_iota(jnp.int32, (STEP, 1), 0)
        return jnp.where(rows < limit, 1.0, 0.0).astype(F32)

    def block(r):
        return pl.ds(pl.multiple_of(r * STEP, STEP), STEP)

    def centred(v):
        centre = v - jnp.mean(v, axis=-1, keepdims=True)
        rstd = lax.rsqrt(jnp.mean(centre * centre, axis=-1, keepdims=True) + 1e-05)
        return centre * rstd, rstd

    def turn(src, dst, j):
        cols = at(j * 128, 128)
        dst[cols, 0:PAD] = src[:, cols].T

    for i in (0, 17, 18):
        load(i)
    for n in range(4):
        wq_chunk(n).start()
    barrier = pltpu.get_barrier_semaphore()
    for e in "xylhc":
        pl.semaphore_signal(barrier, inc=1, device_id=mate[e], device_id_type=MESH)
    ki = lax.broadcasted_iota(jnp.int32, (TILE, TILE), 0)
    qi = lax.broadcasted_iota(jnp.int32, (TILE, TILE), 1)
    mask[...] = jnp.where((ki <= qi) & (ki >= qi - lax.rem(qi, 15)), 0.0, -1e30).astype(F32)
    nb[ROWS:PAD, :] = jnp.zeros((PAD - ROWS, D), BF)
    pl.semaphore_wait(barrier, 5)
    for k in range(4):
        weight(k, "X").start()
    for k in (1, 3):
        weight(k, "D").start()
    weight_c(0).start()
    weight_c(1).start()
    for ref in (gb, mx):
        ref[ROWS:PAD, :] = jnp.zeros((PAD - ROWS, D), BF)
    pk[ROWS:PAD, :] = jnp.zeros((PAD - ROWS, 3 * D), BF)
    vsum[...] = jnp.zeros(vsum.shape, F32)
    for i in (0, 17, 18):
        loaded(i)

    def norm_one(r, _):
        xhat, _r = centred(tok[block(r), :].astype(F32))
        nb[block(r), :] = (xhat * g1[...] + s1[...]).astype(BF)
        return 0

    lax.fori_loop(0, ROWS // STEP, norm_one, 0)
    poll("ln1")
    for i in (1, 3, 4, 5, 19, 20):
        load(i)

    def qkv(n, _):
        wq_chunk(n).wait()
        cols = at(n * 768, 768)
        pk[0:ROWS, cols] = jnp.dot(nb[0:ROWS, :], wq[:, cols], preferred_element_type=F32).astype(BF)
        for m in range(2):
            turn(nb, xn1, n * 2 + m)
        poll_at("qkv", n, range(4))
        return 0

    lax.fori_loop(0, 4, qkv, 0)
    turned(M_N1T, xn1).start()
    loaded(1)

    def mask_cot(r, _):
        gb[block(r), :] = (keep_of(r) * gb[block(r), :].astype(F32)).astype(BF)
        return 0

    lax.fori_loop(0, ROWS // STEP, mask_cot, 0)
    poll("msk")

    def attend(i, _):
        for h, t in ((i * 4 + n, t) for n in range(4) for t in range(2)):
            cols = [at(part * D + h * 128, 128) for part in range(3)]
            rows = slice(t * TILE, (t + 1) * TILE)
            sc = dot_nt(pk[rows, cols[1]], pk[rows, cols[0]]) * (128 ** -0.5) + mask[...]
            w = jnp.exp(sc - jnp.max(sc, axis=0, keepdims=True))
            p = (w * (1.0 / jnp.sum(w, axis=0, keepdims=True))).astype(BF)
            probs[h * 2 + t] = p
            mx[rows, at(h * 128, 128)] = dot_tn(p, pk[rows, cols[2]]).astype(BF)
        poll_at("att", i, range(2))
        return 0

    lax.fori_loop(0, 2, attend, 0)
    loaded(3)

    facc[...] = jnp.dot(mx[0:ROWS, :], wo[...], preferred_element_type=F32)
    for m in range(8):
        turn(gb, xgb, m)
        turn(mx, xmx, m)
    poll("prj")
    turned(M_GBT, xgb).start()

    loaded(19)
    loaded(20)

    def norm_two(r, _):
        m = tok[block(r), :].astype(F32) + keep_of(r) * facc[block(r), :]
        mid[block(r), :] = m
        xhat, _r = centred(m)
        nb[block(r), :] = (xhat * g2[...] + s2[...]).astype(BF)
        return 0

    lax.fori_loop(0, ROWS // STEP, norm_two, 0)
    poll("ln2")

    def turn_two(j, _):
        turn(nb, xn2, j)
        return 0

    lax.fori_loop(0, D // 128, turn_two, 0)
    poll("n2t")

    loaded(4)
    loaded(5)
    wq[ROWS:PAD, 0:FF] = jnp.zeros((PAD - ROWS, FF), BF)
    wq[PAD + ROWS:2 * PAD, 0:FF] = jnp.zeros((PAD - ROWS, FF), BF)

    def widen(j):
        cols = at(j * SHARD, SHARD)
        pre = jnp.dot(nb[0:ROWS, :], upa[:, cols], preferred_element_type=F32)
        sq = pre * pre
        t = jnp.tanh(0.7978845608028654 * pre * (1.0 + 0.044715 * sq))
        half = 0.5 * (1.0 + t)
        wq[0:ROWS, cols] = (pre * half).astype(BF)
        slope = half + 0.5 * pre * (1.0 - t * t) * (0.7978845608028654 * (1.0 + 0.134145 * sq))
        facc[:, at(lax.rem(j, 2) * SHARD, SHARD)] = slope

    def narrow_back(j):
        cols = at(j * SHARD, SHARD)
        gh = dot_nt(gb[0:ROWS, :], dna[cols, :])
        wq[PAD:PAD + ROWS, cols] = (gh * facc[:, at(lax.rem(j, 2) * SHARD, SHARD)]).astype(BF)

    def group(g, _):
        mine = at(2 * g * SHARD, SHARD)
        for m, work, copy in ((0, widen, hid_copy), (1, narrow_back, gpr_copy)):
            @pl.when(g == 0)
            def _():
                weight_c(m).wait()

            @pl.when(g == 1)
            def _():
                poll("wdn" if m else "wup")
                weight_mates(m).wait()
                if m == 0:
                    for p in (DN0, DN1, UP0, UP1):
                        first(p, 0, 0)

            def one(n, _):
                work(2 * g + 1 - n)

                @pl.when(n == 0)
                def _():
                    copy(g).start()

                poll_at("bk" if m else "sh", 2 * g + n, range(4))
                return 0

            lax.fori_loop(0, 2, one, 0)
            if m == 0:
                @pl.when(g == 0)
                def _():
                    turned(M_N2T, xn2).start()

        for m, copy, lhs, top, low, p in ((0, hid_copy, xgb, 0, hids, DN0), (1, gpr_copy, xn2, PAD, gprs, UP0)):
            copy(g).wait()

            @pl.when(g == 0)
            def _():
                turned((M_GBT, M_N2T)[m], lhs).wait()

            rhs = jnp.concatenate([wq[top:top + PAD, mine], low[...]], axis=0)
            total = jnp.dot(lhs[...], rhs, preferred_element_type=F32).astype(BF)
            for half in range(2):
                gw[p + half, g] = total[:, half * WIDE:(half + 1) * WIDE].reshape(2, 2, 2, 128, WIDE)

            @pl.when(g == 1)
            def _():
                for half in range(2):
                    first(p + half, 1, 1)

            poll_at("sum", 2 * g + m, (m, 2 + m))

        return 0

    lax.fori_loop(0, 2, group, 0)
    turned(M_MXT, xmx).start()
    load(6)

    facc[...] = dot_nt(wq[PAD:PAD + ROWS, 0:FF], upa[...])
    poll("bup")
    loaded(6)

    def row_sum(v):
        total = v[0:8]
        for n in range(1, STEP // 8):
            total = total + v[n * 8:(n + 1) * 8]
        return total

    def norm_back(v, gn, gain, n):
        xhat, rstd = centred(v)
        vsum[n] += row_sum(gn * xhat)
        vsum[n + 1] += row_sum(gn)
        e = gn * gain
        return rstd * (e - jnp.mean(e, axis=-1, keepdims=True) - xhat * jnp.mean(e * xhat, axis=-1, keepdims=True))

    def norm_two_back(r, _):
        total = nb[block(r), :].astype(F32) + norm_back(mid[block(r), :], facc[block(r), :], g2[...], 2)
        gm[block(r), :] = total
        ga[block(r), :] = (keep_of(r) * total).astype(BF)
        return 0

    ga[ROWS:PAD, :] = jnp.zeros((PAD - ROWS, D), BF)
    lax.fori_loop(0, ROWS // STEP, norm_two_back, 0)
    ga_copy().start()
    poll("ln2b")

    mx[0:ROWS, :] = dot_nt(ga[0:ROWS, :], wo[...]).astype(BF)
    poll("bout")

    def out_sums():
        rhs = jnp.concatenate([ga[:, at(c * 512, 512)], gas[...]], axis=0)
        total = jnp.dot(xmx[...], rhs, preferred_element_type=F32).astype(BF)
        for half in range(2):
            gw[OUT, half] = total[:, half * WIDE:(half + 1) * WIDE].reshape(2, 2, 2, 128, WIDE)

    def heads_back(i, _):
        h0 = 4 * (c + (1 - i) * (1 - 2 * c))
        for h, t in ((h0 + n, t) for n in range(4) for t in range(2)):
            cols = [at(part * D + h * 128, 128) for part in range(3)]
            rows = slice(t * TILE, (t + 1) * TILE)
            q, k, v = (pk[rows, col] for col in cols)
            o = mx[rows, at(h * 128, 128)]
            pb = probs[h * 2 + t]
            p = pb.astype(F32)
            dp = dot_nt(v, o)
            gs = (p * (dp - jnp.sum(p * dp, axis=0, keepdims=True))).astype(BF)
            gv = jnp.dot(pb, o, preferred_element_type=F32)
            gq = dot_tn(gs, k) * (128 ** -0.5)
            gk = jnp.dot(gs, q, preferred_element_type=F32) * (128 ** -0.5)
            for col, g in zip(cols, (gq, gk, gv)):
                pk[rows, col] = g.astype(BF)

        @pl.when(i == 0)
        def _():
            for n in range(2):
                for part in range(3):
                    pk_copy(n, 1 - x if n == 0 else x, part).start()

        poll_at("pr", i, range(2))

        @pl.when(i == OUT_AT)
        def _():
            turned(M_MXT, xmx).wait()
            ga_copy().wait()
            out_sums()
            first(OUT, None, 0)
            poll("osum")

        return 0

    lax.fori_loop(0, 2, heads_back, 0)
    turned(M_N1T, xn1).wait()

    def qkv_sums(later, _):
        xb = x + (1 - later) * (1 - 2 * x)
        for n in range(2):
            @pl.when(later == n)
            def _():
                pk_copies(n).wait()

        rhs = jnp.concatenate(
            [
                jnp.concatenate([pk[:, at(part * D + c * 512 + xb * WIDE, WIDE)] for part in range(3)], axis=1),
                jnp.concatenate([pks[:, at(part * 512 + xb * WIDE, WIDE)] for part in range(3)], axis=1),
            ],
            axis=0,
        )
        for m in range(2):
            total = jnp.dot(xn1[m * 512:(m + 1) * 512, :], rhs, preferred_element_type=F32).astype(BF)
            for part in range(3):
                gw[QS + part, xb, m] = total[:, part * WIDE:(part + 1) * WIDE].reshape(2, 2, 128, WIDE)
        for n in range(2):
            @pl.when(later == n)
            def _():
                for p in (QS, KS, VS):
                    first(p, 1 - x if n == 0 else x, n)
                poll(("qs", n))

        return 0

    lax.fori_loop(0, 2, qkv_sums, 0)

    facc[...] = jnp.dot(wq[0:ROWS, 0:FF], dna[...], preferred_element_type=F32)
    poll("dwn")
    load(7)

    def finish_out(r, _):
        nb[block(r), :] = (mid[block(r), :] + keep_of(r) * facc[block(r), :]).astype(BF)
        return 0

    lax.fori_loop(0, ROWS // STEP, finish_out, 0)
    load(8)
    poll("fin")
    loaded(7)

    facc[...] = dot_nt(pk[0:ROWS, :], wq[...])
    poll("gn1")

    def norm_one_back(r, _):
        total = gm[block(r), :] + norm_back(tok[block(r), :].astype(F32), facc[block(r), :], g1[...], 0)
        tok[block(r), :] = total.astype(BF)
        return 0

    lax.fori_loop(0, ROWS // STEP, norm_one_back, 0)
    load(9)
    vbuf[0] = jnp.concatenate(
        [jnp.sum(vsum[n], axis=0, keepdims=True) for n in range(4)] + [jnp.zeros((4, D), F32)], axis=0
    )
    vec(0).start()
    poll("ln1b")
    poll("tail")
    vec_o[...] = vbuf[5, :, at(s * 128, 128)]
    for i in (10, 15, 16):
        load(i)
    for n in range(4):
        gathered(n).wait()
        load(21 + n)
    for i in (8, 9, 10, 15, 16, 21, 22, 23, 24):
        loaded(i)


def result_kernel(*refs):
    lo, gt, gq, gup, gdn, vec = refs[:6]
    lo_o, gt_o, gqkv_o, gout_o, gup_o, gdn_o = refs[6:12]
    lov, gtv, gqv, gupv, gdnv, vecv, gqkv, gout, sem = refs[16:]
    pairs = [(gq, gqv), (lo, lov), (gt, gtv), (gup, gupv), (gdn, gdnv), (vec, vecv)]
    pairs += [(lov, lo_o), (gtv, gt_o), (gupv, gup_o), (gdnv, gdn_o), (gout, gout_o)]
    pairs += [(vecv.at[n], refs[12 + n]) for n in range(4)]
    pairs += [(gqkv.at[:, n * D:(n + 1) * D], gqkv_o.at[:, n * D:(n + 1) * D]) for n in range(3)]
    copies = [pltpu.make_async_copy(a, b, sem.at[n]) for n, (a, b) in enumerate(pairs)]
    for n in range(6):
        copies[n].start()
    copies[0].wait()
    for n in range(3):
        gqkv[:, n * D:(n + 1) * D] = gqv[(n + 1) * 128:(n + 2) * 128, :].astype(F32)
        copies[15 + n].start()
    gout[...] = gqv[0:128, :].astype(F32)
    copies[10].start()
    for n in range(1, 6):
        copies[n].wait()
        for m in ((n + 5,) if n < 5 else range(11, 15)):
            copies[m].start()
    for n in range(6, 18):
        copies[n].wait()


def fused(
    tokens, cotangent, live_items, qkv_weight, out_weight, up_weight, down_weight,
    gain_one, shift_one, gain_two, shift_two,
):
    rows_of = [v.reshape(1, D) for v in (gain_one, shift_one, gain_two, shift_two)]
    hbm = pl.BlockSpec(memory_space=pl.ANY)
    shape = jax.ShapeDtypeStruct
    outs = pl.pallas_call(
        layer_kernel,
        name="layer",
        out_shape=(
            shape((ROWS, D), BF), shape((ROWS, D), BF), shape((512, D), BF),
            shape((128, SHARD), F32), shape((SHARD, 128), F32), shape((8, 128), F32),
        ),
        in_specs=[hbm, hbm, pl.BlockSpec(memory_space=pltpu.SMEM)] + [hbm] * 8,
        out_specs=[hbm] * 6,
        scratch_shapes=[
            *[pltpu.VMEM((1, D), F32)] * 4,
            pltpu.VMEM((128, SHARD), F32), pltpu.VMEM((SHARD, 128), F32), pltpu.VMEM((8, 128), F32),
            pltpu.VMEM((D, 3 * D), BF), pltpu.VMEM((D, D), BF), pltpu.VMEM((D, FF), BF), pltpu.VMEM((FF, D), BF),
            pltpu.VMEM((ROWS, D), BF), pltpu.VMEM((PAD, D), BF), pltpu.VMEM((PAD, D), BF), pltpu.VMEM((PAD, D), BF),
            pltpu.VMEM((PAD, 3 * D), BF), pltpu.VMEM((PAD, 3 * 512), BF),
            pltpu.VMEM((D, 2 * PAD), BF), pltpu.VMEM((D, 2 * PAD), BF), pltpu.VMEM((D, 2 * PAD), BF),
            pltpu.VMEM((D, 2 * PAD), BF),
            pltpu.VMEM((16, TILE, TILE), BF), pltpu.VMEM((TILE, TILE), F32),
            pltpu.VMEM((ROWS, D), F32), pltpu.VMEM((ROWS, D), F32), pltpu.VMEM((ROWS, D), F32),
            pltpu.VMEM((PAD, SHARD), BF), pltpu.VMEM((PAD, SHARD), BF), pltpu.VMEM((PAD, 512), BF),
            pltpu.VMEM((8, 2, 2, 2, 2, 128, WIDE), BF),
            pltpu.VMEM((8, 2, 2, 2, 128, WIDE), BF), pltpu.VMEM((8, 2, 2, 128, WIDE), BF),
            pltpu.VMEM((8, 2, 128, WIDE), BF), pltpu.VMEM((8, 128, WIDE), BF),
            pltpu.VMEM((4, 8, D), F32), pltpu.VMEM((6, 8, D), F32), pltpu.VMEM((5, 8, D), F32),
            pltpu.SemaphoreType.DMA((N_MSG,)), pltpu.SemaphoreType.DMA((N_MSG,)), pltpu.SemaphoreType.DMA((25,)),
        ],
        compiler_params=pltpu.CompilerParams(
            collective_id=0, has_side_effects=True, vmem_limit_bytes=67_043_328
        ),
    )(tokens, cotangent, live_items, qkv_weight, out_weight, up_weight, down_weight, *rows_of)
    return pl.pallas_call(
        result_kernel,
        name="results",
        out_shape=(
            shape((ROWS, D), BF), shape((ROWS, D), BF), shape((128, 3 * D), F32), shape((128, D), F32),
            shape((128, SHARD), F32), shape((SHARD, 128), F32),
            shape((128,), F32), shape((128,), F32), shape((128,), F32), shape((128,), F32),
        ),
        in_specs=[hbm] * 6,
        out_specs=[hbm] * 10,
        scratch_shapes=[
            pltpu.VMEM((ROWS, D), BF), pltpu.VMEM((ROWS, D), BF), pltpu.VMEM((512, D), BF),
            pltpu.VMEM((128, SHARD), F32), pltpu.VMEM((SHARD, 128), F32), pltpu.VMEM((8, 128), F32),
            pltpu.VMEM((128, 3 * D), F32), pltpu.VMEM((128, D), F32), pltpu.SemaphoreType.DMA((18,)),
        ],
    )(*outs)


IN_SPECS = (
    P(("seq", "ff"), None), P(("seq", "ff"), None), P("seq"), P(), P(), P(None, "ff"), P("ff", None),
    P(), P(), P(), P(),
)
OUT_SPECS = (
    P(("seq", "ff"), None), P(("seq", "ff"), None), P("seq", None), P("seq", None), P("seq", "ff"),
    P("ff", "seq"), P("seq"), P("seq"), P("seq"), P("seq"),
)


def solution(mesh):
    body = fused if (mesh.shape["seq"], mesh.shape["ff"]) == (8, 4) else general
    return jax.shard_map(body, mesh=mesh, in_specs=IN_SPECS, out_specs=OUT_SPECS, check_vma=False)
```

```python
import jax
import jax.numpy as jnp
from jax import lax
from jax.experimental import pallas as pl
from jax.experimental.pallas import tpu as pltpu
from jax.sharding import PartitionSpec as P

HEADS = 8
HEAD_DIM = 128
ITEM_LEN = 15
BF = jnp.bfloat16
F32 = jnp.float32


def layer_norm(content_matrix, gain, shift):
    centre = content_matrix - jnp.mean(content_matrix, axis=-1, keepdims=True)
    spread = jnp.mean(centre * centre, axis=-1, keepdims=True)
    return centre * lax.rsqrt(spread + 1e-05) * gain + shift


def tile_allowed(tile_rows):
    position = jnp.arange(tile_rows, dtype=jnp.int32)
    same_item = position[:, None] // ITEM_LEN == position[None, :] // ITEM_LEN
    return same_item & (position[None, :] <= position[:, None])


def dot(a, b):
    return jnp.dot(a, b, preferred_element_type=F32)


def tiles_of(x, tile):
    return x.reshape(-1, tile, HEAD_DIM)


def scores_of(q, k, allowed):
    s = jnp.einsum("tqd,tkd->tqk", q, k, preferred_element_type=F32) * HEAD_DIM ** (-0.5)
    return jnp.where(allowed, s, -1e30)


def attend_forward(packed, tile):
    allowed = tile_allowed(tile)
    width = HEADS * HEAD_DIM
    mixed, saved = [], []
    for h in range(HEADS):
        q, k, v = (tiles_of(packed[:, p * width + h * HEAD_DIM:][:, :HEAD_DIM], tile) for p in range(3))
        probs = jax.nn.softmax(scores_of(q, k, allowed), axis=-1)
        o = jnp.einsum("tqk,tkd->tqd", probs.astype(BF), v, preferred_element_type=F32)
        mixed.append(o.astype(BF).reshape(-1, HEAD_DIM))
        saved.append(probs)
    return jnp.concatenate(mixed, axis=1), saved


def attend_backward(packed, saved, grad_mixed, tile):
    width = HEADS * HEAD_DIM
    scale = HEAD_DIM ** (-0.5)
    parts = ([], [], [])
    for h in range(HEADS):
        q, k, v = (tiles_of(packed[:, p * width + h * HEAD_DIM:][:, :HEAD_DIM], tile) for p in range(3))
        o = tiles_of(grad_mixed[:, h * HEAD_DIM:][:, :HEAD_DIM], tile)
        probs = saved[h]
        dp = jnp.einsum("tqd,tkd->tqk", o, v, preferred_element_type=F32)
        gv = jnp.einsum("tqk,tqd->tkd", probs.astype(BF), o, preferred_element_type=F32)
        gs = (probs * (dp - jnp.sum(probs * dp, axis=-1, keepdims=True))).astype(BF)
        gq = jnp.einsum("tqk,tkd->tqd", gs, k, preferred_element_type=F32) * scale
        gk = jnp.einsum("tqk,tqd->tkd", gs, q, preferred_element_type=F32) * scale
        for part, g in zip(parts, (gq, gk, gv)):
            part.append(g.astype(BF).reshape(-1, HEAD_DIM))
    return jnp.concatenate(parts[0] + parts[1] + parts[2], axis=1)


def general(
    tokens, cotangent, live_items, qkv_weight, out_weight, up_weight, down_weight,
    gain_one, shift_one, gain_two, shift_two,
):
    rows = tokens.shape[0]
    items = rows // ITEM_LEN
    tile = ITEM_LEN * (16 if items % 16 == 0 else 1)
    place = lax.axis_index("ff") * items + jnp.arange(rows, dtype=jnp.int32) // ITEM_LEN
    keep = (place < live_items[0]).astype(F32)[:, None]
    up_all = lax.all_gather(up_weight, "ff", axis=1, tiled=True)
    down_all = lax.all_gather(down_weight, "ff", axis=0, tiled=True)
    inputs = tokens.astype(F32)
    normed, norm_one_pull = jax.vjp(layer_norm, inputs, gain_one, shift_one)
    normed = normed.astype(BF)
    packed = dot(normed, qkv_weight).astype(BF)
    mixed, saved = attend_forward(packed, tile)
    middle = inputs + keep * dot(mixed, out_weight)
    normed_two, norm_two_pull = jax.vjp(layer_norm, middle, gain_two, shift_two)
    normed_two = normed_two.astype(BF)
    grad_out = cotangent.astype(F32)
    grad_branch = (keep * grad_out).astype(BF)
    pre = dot(normed_two, up_all)
    hidden = jax.nn.gelu(pre).astype(BF)
    layer_out = (middle + keep * dot(hidden, down_all)).astype(BF)
    grad_hidden = dot(grad_branch, down_all.T)
    grad_pre = jax.vjp(jax.nn.gelu, pre)[1](grad_hidden)[0].astype(BF)
    grad_down = dot(hidden.T, grad_branch).astype(BF)
    grad_up = dot(normed_two.T, grad_pre).astype(BF)
    grad_middle_norm, grad_gain_two, grad_shift_two = norm_two_pull(dot(grad_pre, up_all.T))
    grad_middle = grad_out + grad_middle_norm
    grad_attended = (keep * grad_middle).astype(BF)
    grad_out_weight = dot(mixed.T, grad_attended).astype(BF)
    grad_mixed = dot(grad_attended, out_weight.T).astype(BF)
    grad_packed = attend_backward(packed, saved, grad_mixed, tile)
    grad_qkv = dot(normed.T, grad_packed).astype(BF)
    grad_inputs, grad_gain_one, grad_shift_one = norm_one_pull(dot(grad_packed, qkv_weight.T))
    grad_tokens = (grad_middle + grad_inputs).astype(BF)

    def scatter(x, axis, dim):
        return lax.psum_scatter(x, axis, scatter_dimension=dim, tiled=True)

    grad_up = scatter(scatter(grad_up, "ff", 1), "seq", 0).astype(F32)
    grad_down = scatter(scatter(grad_down, "ff", 0), "seq", 1).astype(F32)
    shared = [
        lax.psum(scatter(g, "seq", 0), "ff").astype(F32)
        for g in (grad_qkv, grad_out_weight, grad_gain_one, grad_shift_one, grad_gain_two, grad_shift_two)
    ]
    return (layer_out, grad_tokens, shared[0], shared[1], grad_up, grad_down, *shared[2:])


MESH = pl.DeviceIdType.MESH
ROWS, PAD, D, FF, SHARD = 480, 512, 1024, 2048, 512
TILE = 240
WIDE = 256
STEP = 240
UP0, UP1, DN0, DN1, OUT, QS, KS, VS = range(8)
SUB = 2
OUT_AT = 0
LANES = WIDE // SUB
ORDER = (
    "xylh", "lyhx", "lxhy", "lxhy", "ylxh", "xlhy", "yxhl", "ylxh",
    "xlyh", "yxlh", "yxlh", "lyxh", "xlhy", "yxlh", "yxlh", "yxlh",
)
EYES = "xhly"
M_UPC, M_DNC = 0, 1
M_W = 2
M_MATE = 22
M_GBT, M_N2T, M_MXT, M_N1T, M_GA = 24, 25, 26, 27, 28
M_HID, M_GPR = 29, 31
M_PK = 33
M_VEC = 35
M_RED = 40
M_AGX = M_RED + 40 * SUB
M_AG = M_AGX + 4 * SUB
N_MSG = M_AG + 4
N_SENT = M_RED + 16 * SUB
WAYS = ("XYLPQ", "XYLD", "XYLPQ", "XYLD")
SCHED = {
    ("att", 0): (
        ("X", 0),
    ),
    ("att", 1): (
        ("X", 1),
    ),
    "n2t": (
        ("X", 2),
    ),
    ("sh", 0): (
        ("Y", 0), ("L", 0),
    ),
    ("bk", 1): (
        ("X", 3),
    ),
    ("sum", 0): (
        ("Y", 1), ("L", 1),
    ),
    ("sum", 1): (
        ("Y", 2), ("L", 2),
    ),
    "wup": (
        ("D", 1), ("P", 0), ("Q", 0), ("D", 3),
    ),
    ("sh", 3): (
        ("Y", 3), ("L", 3),
    ),
    "wdn": (
        ("P", 2), ("Q", 2),
    ),
    ("sum", 2): (
        ("R", 4, 0, 0), ("R", 1, 0, 0),
    ),
    "bup": (
        ("R", 6, 0, 0), ("R", 2, 0, 0),
    ),
    "ln2b": (
        ("R", 7, 0, 0), ("R", 3, 0, 0),
    ),
    ("pr", 0): (
        ("R", 4, 0, 1), ("R", 1, 0, 1), ("R", 5, 0, 0),
    ),
    "osum": (
        ("R", 6, 0, 1), ("R", 2, 0, 1),
    ),
    ("pr", 1): (
        ("R", 7, 0, 1), ("R", 3, 0, 1), ("R", 0, 0, 0),
    ),
    ("qs", 0): (
        ("R", 4, 1, 0), ("R", 1, 1, 0),
    ),
    ("qs", 1): (
        ("R", 5, 1, 0),
    ),
    "dwn": (
        ("R", 8, 0, 0),
    ),
    "fin": (
        ("R", 9, 0, 0), ("R", 7, 1, 0), ("R", 6, 1, 0),
    ),
    "gn1": (
        ("R", 0, 1, 0), ("R", 11, 0, 0), ("R", 2, 1, 0),
    ),
    "ln1b": (
        ("R", 1, 2, 0), ("R", 10, 0, 0), ("R", 3, 1, 0), ("R", 11, 0, 1),
    ),
    "tail": (
        ("R", 13, 0, 0), ("V", 0), ("R", 5, 2, 0), ("R", 14, 0, 0), ("R", 8, 1, 0), ("R", 12, 0, 0), ("R", 4, 2, 0),
        ("R", 6, 2, 0), ("R", 15, 0, 0), ("R", 0, 2, 0), ("R", 9, 1, 0), ("R", 2, 2, 0), ("R", 10, 0, 1),
        ("R", 7, 2, 0), ("R", 1, 3, 0), ("V", 1), ("R", 3, 2, 0), ("R", 13, 0, 1), ("R", 12, 1, 0), ("R", 6, 3, 0),
        ("R", 4, 3, 0), ("R", 10, 1, 0), ("R", 14, 0, 1), ("R", 0, 3, 0), ("R", 9, 2, 0), ("R", 7, 3, 0),
        ("R", 13, 1, 0), ("R", 15, 0, 1), ("R", 10, 2, 0), ("R", 12, 2, 0), ("R", 14, 1, 0), ("R", 11, 1, 0),
        ("R", 5, 3, 0), ("R", 13, 2, 0), ("R", 9, 3, 0), ("R", 8, 2, 0), ("R", 15, 1, 0), ("R", 2, 3, 0),
        ("R", 10, 3, 0), ("R", 14, 2, 0), ("V", 2), ("R", 11, 2, 0), ("R", 3, 3, 0), ("G", 1), ("R", 12, 3, 0),
        ("R", 13, 3, 0), ("G", 2), ("R", 15, 2, 0), ("R", 8, 3, 0), ("G", 4), ("V", 3), ("R", 14, 3, 0), ("G", 5),
        ("R", 11, 3, 0), ("G", 0), ("R", 15, 3, 0), ("G", 6), ("V", 4), ("G", 3), ("G", 7),
    ),
}


def dot_nt(a, b):
    return lax.dot_general(a, b, (((1,), (1,)), ((), ())), preferred_element_type=F32)


def dot_tn(a, b):
    return lax.dot_general(a, b, (((0,), (0,)), ((), ())), preferred_element_type=F32)


def layer_kernel(
    tok_h, cot_h, live, wq_h, wo_h, up_h, dn_h, g1_h, s1_h, g2_h, s2_h,
    lo_h, gt_h, gq_h, gup_h, gdn_h, vec_h,
    g1, s1, g2, s2, gup_o, gdn_o, vec_o,
    wq, wo, upa, dna, tok, gb, nb, mx, pk, pks, xgb, xn2, xmx, xn1, probs, mask, mid, gm, facc,
    hids, gprs, gas, gw, r0, r1, r2, r3, vsum, vbuf, vrecv, ssem, rsem, lsem,
):
    s, f = lax.axis_index("seq"), lax.axis_index("ff")
    bit = {"h": s // 4, "l": (s // 2) % 2, "y": s % 2, "x": f // 2, "c": f % 2}
    mate = {
        "h": (s + 4 - 8 * bit["h"], f), "l": (s + 2 - 4 * bit["l"], f), "y": (s + 1 - 2 * bit["y"], f),
        "x": (s, f + 2 - 4 * bit["x"]), "c": (s, f + 1 - 2 * bit["c"]),
        "lh": (s + 6 - 4 * bit["l"] - 8 * bit["h"], f),
    }
    x, c = bit["x"], bit["c"]

    def at(base, size, unit=128):
        return pl.ds(pl.multiple_of(base, unit), size)

    ga = xn2.at[0:PAD]

    def local(i, src, dst):
        return pltpu.make_async_copy(src, dst, lsem.at[i])

    loads = {
        0: (tok_h, tok), 1: (cot_h, gb.at[0:ROWS]), 3: (wo_h, wo), 4: (up_h, upa.at[:, 0:SHARD]),
        5: (dn_h, dna.at[0:SHARD]), 6: (cot_h, nb.at[0:ROWS]), 7: (wq_h, wq),
        8: (nb.at[0:ROWS], lo_h), 9: (tok, gt_h), 10: (gup_o, gup_h), 15: (gdn_o, gdn_h), 16: (vec_o, vec_h),
        17: (g1_h, g1), 18: (s1_h, s1), 19: (g2_h, g2), 20: (s2_h, s2),
        **{21 + n: (xgb.at[n * 128:(n + 1) * 128], gq_h.at[n * 128:(n + 1) * 128]) for n in range(4)},
    }

    def load(i):
        local(i, *loads[i]).start()

    def loaded(i):
        local(i, *loads[i]).wait()

    def wq_chunk(n):
        cols = at(n * 768, 768)
        return local(11 + n, wq_h.at[:, cols], wq.at[:, cols])

    def remote(i, to, src, dst, sent=None):
        return pltpu.make_async_remote_copy(
            src_ref=src, dst_ref=dst, send_sem=ssem.at[i if sent is None else sent], recv_sem=rsem.at[i],
            device_id=mate[to], device_id_type=MESH,
        )

    def region(k, way, slot):
        yb = bit["y"] if way in ("X", "L") else 1 - bit["y"]
        lb = bit["l"] if way in ("X", "Y") else 1 - bit["l"]
        size = 128 if k < 2 else 64
        start = (2 * yb + lb) * (2 * size) + (k % 2) * size
        if way in ("P", "Q"):
            size //= 2
            start = start + (size if way == "Q" else 0)
        rows = at(start, size, 32)
        if slot is None:
            return up_h.at[rows, :] if k < 2 else dn_h.at[rows, :]
        if k < 2:
            return upa.at[rows, slot * SHARD:(slot + 1) * SHARD]
        return dna.at[at(slot * SHARD + start, size, 32), :]

    def onward(k, way):
        yb = bit["y"] if way == "Q" else 1 - bit["y"]
        lb = bit["l"] if way == "P" else 1 - bit["l"]
        size = 64 if k < 2 else 32
        start = (2 * yb + lb) * (4 * size) + (k % 2) * (2 * size) + (size if way == "Q" else 0)
        if k < 2:
            return upa.at[at(start, size, 32), 2 * SHARD:3 * SHARD]
        return dna.at[at(2 * SHARD + start, size, 32), :]

    def weight(k, way):
        i = M_W + k * 5 + WAYS[k].index(way)
        if way in ("X", "D"):
            return remote(i, "x", region(k, way, None), region(k, way, 2))
        if way in ("Y", "L"):
            return remote(i, way.lower(), region(k, "X", 2), region(k, "X", 2))
        return remote(i, "l" if way == "P" else "y", onward(k, way), onward(k, way))

    def weight_mate(k, way):
        return remote(M_MATE + k // 2, "c", region(k, way, 2), region(k, way, 3))

    def weight_mates(m):
        if m == 0:
            return remote(M_MATE, "c", upa.at[:, 2 * SHARD:3 * SHARD], upa.at[:, 3 * SHARD:4 * SHARD])
        return remote(M_MATE + 1, "c", dna.at[2 * SHARD:3 * SHARD], dna.at[3 * SHARD:4 * SHARD])

    def relay(way, k):
        weight(k, way).wait()
        if way == "X":
            weight(k, "Y").start()
            weight(k, "L").start()
        elif way == "Y" and k % 2 == 0:
            weight(k, "P").start()
        elif way == "L" and k % 2 == 0:
            weight(k, "Q").start()
        weight_mate(k, way).start()

    def weight_c(which):
        if which == 0:
            return remote(M_UPC, "c", up_h, upa.at[:, SHARD:2 * SHARD])
        return remote(M_DNC, "c", dn_h, dna.at[SHARD:2 * SHARD])

    def turned(i, ref):
        return remote(i, "c", ref.at[:, 0:PAD], ref.at[:, PAD:2 * PAD])

    def own_hid(slot):
        return wq.at[0:PAD, at(slot * SHARD, SHARD)]

    def own_gpr(slot):
        return wq.at[PAD:2 * PAD, at(slot * SHARD, SHARD)]

    def hid_copy(g):
        return remote(M_HID + g, "c", own_hid(2 * g + 1), hids)

    def gpr_copy(g):
        return remote(M_GPR + g, "c", own_gpr(2 * g + 1), gprs)

    def ga_copy():
        return remote(M_GA, "c", ga.at[:, at((1 - c) * 512, 512)], gas)

    def pk_copy(n, xb, part):
        return remote(
            M_PK + n, "c", pk.at[:, at(part * D + (1 - c) * 512 + xb * WIDE, WIDE)],
            pks.at[:, at(part * 512 + xb * WIDE, WIDE)],
        )

    def pk_copies(n):
        return remote(M_PK + n, "c", pks.at[:, 0:3 * WIDE], pks.at[:, 0:3 * WIDE])

    landing = (r0, r1, r2, r3)

    def lanes_of(p):
        return slice((p % SUB) * LANES, (p % SUB + 1) * LANES)

    def bits_of(p):
        return {**bit, "x": 0} if p // SUB < OUT else bit

    def chosen(p, k, mine, xb=None):
        own, order, index = bits_of(p), ORDER[p], []
        for e in EYES:
            if e in order[:k]:
                index.append(own[e])
            elif e == order[k]:
                index.append(own[e] if mine else 1 - own[e])
            elif e == "x" and xb is not None:
                index.append(xb)
            else:
                index.append(slice(None))
        return index

    def red(p, k, xb=None, part=0):
        lead = (p // SUB,) if xb is None else (p // SUB, xb)
        rest = (slice(None), lanes_of(p))
        free = sum(isinstance(e, slice) for e in chosen(p, k, False, xb))
        return remote(
            M_RED + p * 5 + (k + 1 if k else part), ORDER[p][k],
            gw.at[(p // SUB, *chosen(p, k, False, xb), *rest)],
            landing[k].at[(*lead, *[slice(None)] * free, *rest)], M_RED + p * 2 + part,
        )

    def add(p, k, xb=None):
        index = chosen(p, k, True, xb)
        free = [n for n, e in enumerate(index) if isinstance(e, slice)]
        count = len(free)
        rest = (slice(None), lanes_of(p))

        def body(i, _):
            place = [(i // (1 << (count - 1 - n))) % 2 for n in range(count)]
            full = list(index)
            for n, e in zip(free, place):
                full[n] = e
            own = (p // SUB, *full, *rest)
            lead = (p // SUB, *place) if xb is None else (p // SUB, xb, *place)
            gw[own] = (gw[own].astype(F32) + landing[k][(*lead, *rest)].astype(F32)).astype(BF)
            return 0

        lax.fori_loop(0, 1 << count, body, 0)

    parts_done = {}

    def first(n, xb, part):
        for p in range(n * SUB, (n + 1) * SUB):
            if n == OUT:
                red(p, 0).start()
            elif ORDER[p][0] != "x":
                red(p, 0, xb, part).start()
            elif (part == 1) == (n < OUT):
                red(p, 0).start()

    def reduced(p, k, part):
        n = p // SUB
        if k == 0 and ORDER[p][0] != "x" and n != OUT:
            xb = part if n < OUT else (1 - x if part == 0 else x)
            red(p, 0, xb, part).wait()
            add(p, 0, xb)
            parts_done[p] = parts_done.get(p, 0) + 1
            if parts_done[p] == 2:
                red(p, 1).start()
        elif k < 3:
            red(p, k).wait()
            add(p, k)
            red(p, k + 1).start()
        else:
            own, rest = bits_of(p), (slice(None), lanes_of(p))
            total = gw[(n, *(own[e] for e in EYES), *rest)].astype(F32)
            red(p, 3).wait()
            total = total + r3[(n, *rest)].astype(F32)
            if n < OUT:
                cols = slice((n % 2) * WIDE + (p % SUB) * LANES, (n % 2) * WIDE + (p % SUB + 1) * LANES)
            if n in (UP0, UP1):
                gup_o[:, cols] = total
            elif n in (DN0, DN1):
                gdn_o[cols, :] = total.T
            else:
                q = p - OUT * SUB
                quarters(q, own_quarter)[...] = total.astype(BF)
                gather_c(q).start()
                gather_x(q).start()

    def quarters(q, n):
        row = (q // SUB) * 128
        return xgb.at[row:row + 128, at(n * WIDE + (q % SUB) * LANES, LANES)]

    own_quarter = 2 * c + x

    def gather_c(q):
        sent = M_W + q // SUB
        return remote(M_AG + q // SUB, "c", quarters(q, own_quarter), quarters(q, own_quarter), sent)

    def gather_x(q):
        sent = M_RED + (OUT * SUB + q) * 2
        return remote(M_AGX + q, "x", quarters(q, own_quarter), quarters(q, own_quarter), sent)

    def gather_f(q):
        other = 2 * c + 1 - x
        sent = M_W + q // SUB
        return remote(M_AG + q // SUB, "c", quarters(q, other), quarters(q, other), sent)

    def gathered(n):
        half = xgb.at[n * 128:(n + 1) * 128, 0:2 * WIDE]
        return remote(M_AG + n, "c", half, half, M_W + n)

    def vec(n):
        return remote(M_VEC + n, "cxylh"[n], vbuf.at[n], vrecv.at[n])

    def vec_step(n):
        vec(n).wait()
        vbuf[n + 1] = vbuf[n] + vrecv[n]
        if n < 4:
            vec(n + 1).start()

    def handle(event):
        kind = event[0]
        if kind == "R":
            reduced(*event[1:])
        elif kind == "G":
            gather_x(event[1]).wait()
            gather_f(event[1]).start()
        elif kind == "V":
            vec_step(event[1])
        else:
            relay(kind, event[1])

    def poll(name):
        for event in SCHED.get(name, ()):
            handle(event)

    def poll_at(name, i, places):
        for n in places:
            if (name, n) in SCHED:
                @pl.when(i == n)
                def _():
                    for event in SCHED[(name, n)]:
                        handle(event)

    limit = (live[0] - f * (ROWS // 15)) * 15

    def keep_of(r):
        rows = r * STEP + lax.broadcasted_iota(jnp.int32, (STEP, 1), 0)
        return jnp.where(rows < limit, 1.0, 0.0).astype(F32)

    def block(r):
        return pl.ds(pl.multiple_of(r * STEP, STEP), STEP)

    def centred(v):
        centre = v - jnp.mean(v, axis=-1, keepdims=True)
        rstd = lax.rsqrt(jnp.mean(centre * centre, axis=-1, keepdims=True) + 1e-05)
        return centre * rstd, rstd

    def turn(src, dst, j):
        cols = at(j * 128, 128)
        dst[cols, 0:PAD] = src[:, cols].T

    for i in (0, 17, 18):
        load(i)
    for n in range(4):
        wq_chunk(n).start()
    barrier = pltpu.get_barrier_semaphore()
    for e in "xylhc":
        pl.semaphore_signal(barrier, inc=1, device_id=mate[e], device_id_type=MESH)
    ki = lax.broadcasted_iota(jnp.int32, (TILE, TILE), 0)
    qi = lax.broadcasted_iota(jnp.int32, (TILE, TILE), 1)
    mask[...] = jnp.where((ki <= qi) & (ki >= qi - lax.rem(qi, 15)), 0.0, -1e30).astype(F32)
    nb[ROWS:PAD, :] = jnp.zeros((PAD - ROWS, D), BF)
    pl.semaphore_wait(barrier, 5)
    for k in range(4):
        weight(k, "X").start()
    for k in (1, 3):
        weight(k, "D").start()
    weight_c(0).start()
    weight_c(1).start()
    for ref in (gb, mx):
        ref[ROWS:PAD, :] = jnp.zeros((PAD - ROWS, D), BF)
    pk[ROWS:PAD, :] = jnp.zeros((PAD - ROWS, 3 * D), BF)
    vsum[...] = jnp.zeros(vsum.shape, F32)
    for i in (0, 17, 18):
        loaded(i)

    def norm_one(r, _):
        xhat, _r = centred(tok[block(r), :].astype(F32))
        nb[block(r), :] = (xhat * g1[...] + s1[...]).astype(BF)
        return 0

    lax.fori_loop(0, ROWS // STEP, norm_one, 0)
    poll("ln1")
    for i in (1, 3, 4, 5, 19, 20):
        load(i)

    def qkv(n, _):
        wq_chunk(n).wait()
        cols = at(n * 768, 768)
        pk[0:ROWS, cols] = jnp.dot(nb[0:ROWS, :], wq[:, cols], preferred_element_type=F32).astype(BF)
        for m in range(2):
            turn(nb, xn1, n * 2 + m)
        poll_at("qkv", n, range(4))
        return 0

    lax.fori_loop(0, 4, qkv, 0)
    turned(M_N1T, xn1).start()
    loaded(1)

    def mask_cot(r, _):
        gb[block(r), :] = (keep_of(r) * gb[block(r), :].astype(F32)).astype(BF)
        return 0

    lax.fori_loop(0, ROWS // STEP, mask_cot, 0)
    poll("msk")

    def attend(i, _):
        for h, t in ((i * 4 + n, t) for n in range(4) for t in range(2)):
            cols = [at(part * D + h * 128, 128) for part in range(3)]
            rows = slice(t * TILE, (t + 1) * TILE)
            sc = dot_nt(pk[rows, cols[1]], pk[rows, cols[0]]) * (128 ** -0.5) + mask[...]
            w = jnp.exp(sc - jnp.max(sc, axis=0, keepdims=True))
            p = (w * (1.0 / jnp.sum(w, axis=0, keepdims=True))).astype(BF)
            probs[h * 2 + t] = p
            mx[rows, at(h * 128, 128)] = dot_tn(p, pk[rows, cols[2]]).astype(BF)
        poll_at("att", i, range(2))
        return 0

    lax.fori_loop(0, 2, attend, 0)
    loaded(3)

    facc[...] = jnp.dot(mx[0:ROWS, :], wo[...], preferred_element_type=F32)
    for m in range(8):
        turn(gb, xgb, m)
        turn(mx, xmx, m)
    poll("prj")
    turned(M_GBT, xgb).start()

    loaded(19)
    loaded(20)

    def norm_two(r, _):
        m = tok[block(r), :].astype(F32) + keep_of(r) * facc[block(r), :]
        mid[block(r), :] = m
        xhat, _r = centred(m)
        nb[block(r), :] = (xhat * g2[...] + s2[...]).astype(BF)
        return 0

    lax.fori_loop(0, ROWS // STEP, norm_two, 0)
    poll("ln2")

    def turn_two(j, _):
        turn(nb, xn2, j)
        return 0

    lax.fori_loop(0, D // 128, turn_two, 0)
    poll("n2t")

    loaded(4)
    loaded(5)
    wq[ROWS:PAD, 0:FF] = jnp.zeros((PAD - ROWS, FF), BF)
    wq[PAD + ROWS:2 * PAD, 0:FF] = jnp.zeros((PAD - ROWS, FF), BF)

    def widen(j):
        cols = at(j * SHARD, SHARD)
        pre = jnp.dot(nb[0:ROWS, :], upa[:, cols], preferred_element_type=F32)
        sq = pre * pre
        t = jnp.tanh(0.7978845608028654 * pre * (1.0 + 0.044715 * sq))
        half = 0.5 * (1.0 + t)
        wq[0:ROWS, cols] = (pre * half).astype(BF)
        slope = half + 0.5 * pre * (1.0 - t * t) * (0.7978845608028654 * (1.0 + 0.134145 * sq))
        facc[:, at(lax.rem(j, 2) * SHARD, SHARD)] = slope

    def narrow_back(j):
        cols = at(j * SHARD, SHARD)
        gh = dot_nt(gb[0:ROWS, :], dna[cols, :])
        wq[PAD:PAD + ROWS, cols] = (gh * facc[:, at(lax.rem(j, 2) * SHARD, SHARD)]).astype(BF)

    def group(g, _):
        mine = at(2 * g * SHARD, SHARD)
        for m, work, copy in ((0, widen, hid_copy), (1, narrow_back, gpr_copy)):
            @pl.when(g == 0)
            def _():
                weight_c(m).wait()

            @pl.when(g == 1)
            def _():
                poll("wdn" if m else "wup")
                weight_mates(m).wait()
                if m == 0:
                    for p in (DN0, DN1, UP0, UP1):
                        first(p, 0, 0)

            def one(n, _):
                work(2 * g + 1 - n)

                @pl.when(n == 0)
                def _():
                    copy(g).start()

                poll_at("bk" if m else "sh", 2 * g + n, range(4))
                return 0

            lax.fori_loop(0, 2, one, 0)
            if m == 0:
                @pl.when(g == 0)
                def _():
                    turned(M_N2T, xn2).start()

        for m, copy, lhs, top, low, p in ((0, hid_copy, xgb, 0, hids, DN0), (1, gpr_copy, xn2, PAD, gprs, UP0)):
            copy(g).wait()

            @pl.when(g == 0)
            def _():
                turned((M_GBT, M_N2T)[m], lhs).wait()

            rhs = jnp.concatenate([wq[top:top + PAD, mine], low[...]], axis=0)
            total = jnp.dot(lhs[...], rhs, preferred_element_type=F32).astype(BF)
            for half in range(2):
                gw[p + half, g] = total[:, half * WIDE:(half + 1) * WIDE].reshape(2, 2, 2, 128, WIDE)

            @pl.when(g == 1)
            def _():
                for half in range(2):
                    first(p + half, 1, 1)

            poll_at("sum", 2 * g + m, (m, 2 + m))

        return 0

    lax.fori_loop(0, 2, group, 0)
    turned(M_MXT, xmx).start()
    load(6)

    facc[...] = dot_nt(wq[PAD:PAD + ROWS, 0:FF], upa[...])
    poll("bup")
    loaded(6)

    def row_sum(v):
        total = v[0:8]
        for n in range(1, STEP // 8):
            total = total + v[n * 8:(n + 1) * 8]
        return total

    def norm_back(v, gn, gain, n):
        xhat, rstd = centred(v)
        vsum[n] += row_sum(gn * xhat)
        vsum[n + 1] += row_sum(gn)
        e = gn * gain
        return rstd * (e - jnp.mean(e, axis=-1, keepdims=True) - xhat * jnp.mean(e * xhat, axis=-1, keepdims=True))

    def norm_two_back(r, _):
        total = nb[block(r), :].astype(F32) + norm_back(mid[block(r), :], facc[block(r), :], g2[...], 2)
        gm[block(r), :] = total
        ga[block(r), :] = (keep_of(r) * total).astype(BF)
        return 0

    ga[ROWS:PAD, :] = jnp.zeros((PAD - ROWS, D), BF)
    lax.fori_loop(0, ROWS // STEP, norm_two_back, 0)
    ga_copy().start()
    poll("ln2b")

    mx[0:ROWS, :] = dot_nt(ga[0:ROWS, :], wo[...]).astype(BF)
    poll("bout")

    def out_sums():
        rhs = jnp.concatenate([ga[:, at(c * 512, 512)], gas[...]], axis=0)
        total = jnp.dot(xmx[...], rhs, preferred_element_type=F32).astype(BF)
        for half in range(2):
            gw[OUT, half] = total[:, half * WIDE:(half + 1) * WIDE].reshape(2, 2, 2, 128, WIDE)

    def heads_back(i, _):
        h0 = 4 * (c + (1 - i) * (1 - 2 * c))
        for h, t in ((h0 + n, t) for n in range(4) for t in range(2)):
            cols = [at(part * D + h * 128, 128) for part in range(3)]
            rows = slice(t * TILE, (t + 1) * TILE)
            q, k, v = (pk[rows, col] for col in cols)
            o = mx[rows, at(h * 128, 128)]
            pb = probs[h * 2 + t]
            p = pb.astype(F32)
            dp = dot_nt(v, o)
            gs = (p * (dp - jnp.sum(p * dp, axis=0, keepdims=True))).astype(BF)
            gv = jnp.dot(pb, o, preferred_element_type=F32)
            gq = dot_tn(gs, k) * (128 ** -0.5)
            gk = jnp.dot(gs, q, preferred_element_type=F32) * (128 ** -0.5)
            for col, g in zip(cols, (gq, gk, gv)):
                pk[rows, col] = g.astype(BF)

        @pl.when(i == 0)
        def _():
            for n in range(2):
                for part in range(3):
                    pk_copy(n, 1 - x if n == 0 else x, part).start()

        poll_at("pr", i, range(2))

        @pl.when(i == OUT_AT)
        def _():
            turned(M_MXT, xmx).wait()
            ga_copy().wait()
            out_sums()
            first(OUT, None, 0)
            poll("osum")

        return 0

    lax.fori_loop(0, 2, heads_back, 0)
    turned(M_N1T, xn1).wait()

    def qkv_sums(later, _):
        xb = x + (1 - later) * (1 - 2 * x)
        for n in range(2):
            @pl.when(later == n)
            def _():
                pk_copies(n).wait()

        rhs = jnp.concatenate(
            [
                jnp.concatenate([pk[:, at(part * D + c * 512 + xb * WIDE, WIDE)] for part in range(3)], axis=1),
                jnp.concatenate([pks[:, at(part * 512 + xb * WIDE, WIDE)] for part in range(3)], axis=1),
            ],
            axis=0,
        )
        for m in range(2):
            total = jnp.dot(xn1[m * 512:(m + 1) * 512, :], rhs, preferred_element_type=F32).astype(BF)
            for part in range(3):
                gw[QS + part, xb, m] = total[:, part * WIDE:(part + 1) * WIDE].reshape(2, 2, 128, WIDE)
        for n in range(2):
            @pl.when(later == n)
            def _():
                for p in (QS, KS, VS):
                    first(p, 1 - x if n == 0 else x, n)
                poll(("qs", n))

        return 0

    lax.fori_loop(0, 2, qkv_sums, 0)

    facc[...] = jnp.dot(wq[0:ROWS, 0:FF], dna[...], preferred_element_type=F32)
    poll("dwn")
    load(7)

    def finish_out(r, _):
        nb[block(r), :] = (mid[block(r), :] + keep_of(r) * facc[block(r), :]).astype(BF)
        return 0

    lax.fori_loop(0, ROWS // STEP, finish_out, 0)
    load(8)
    poll("fin")
    loaded(7)

    facc[...] = dot_nt(pk[0:ROWS, :], wq[...])
    poll("gn1")

    def norm_one_back(r, _):
        total = gm[block(r), :] + norm_back(tok[block(r), :].astype(F32), facc[block(r), :], g1[...], 0)
        tok[block(r), :] = total.astype(BF)
        return 0

    lax.fori_loop(0, ROWS // STEP, norm_one_back, 0)
    load(9)
    vbuf[0] = jnp.concatenate(
        [jnp.sum(vsum[n], axis=0, keepdims=True) for n in range(4)] + [jnp.zeros((4, D), F32)], axis=0
    )
    vec(0).start()
    poll("ln1b")
    poll("tail")
    vec_o[...] = vbuf[5, :, at(s * 128, 128)]
    for i in (10, 15, 16):
        load(i)
    for n in range(4):
        gathered(n).wait()
        load(21 + n)
    for i in (8, 9, 10, 15, 16, 21, 22, 23, 24):
        loaded(i)


def result_kernel(*refs):
    lo, gt, gq, gup, gdn, vec = refs[:6]
    lo_o, gt_o, gqkv_o, gout_o, gup_o, gdn_o = refs[6:12]
    lov, gtv, gqv, gupv, gdnv, vecv, gqkv, gout, sem = refs[16:]
    pairs = [(gq, gqv), (lo, lov), (gt, gtv), (gup, gupv), (gdn, gdnv), (vec, vecv)]
    pairs += [(lov, lo_o), (gtv, gt_o), (gupv, gup_o), (gdnv, gdn_o), (gout, gout_o)]
    pairs += [(vecv.at[n], refs[12 + n]) for n in range(4)]
    pairs += [(gqkv.at[:, n * D:(n + 1) * D], gqkv_o.at[:, n * D:(n + 1) * D]) for n in range(3)]
    copies = [pltpu.make_async_copy(a, b, sem.at[n]) for n, (a, b) in enumerate(pairs)]
    for n in range(6):
        copies[n].start()
    copies[0].wait()
    for n in range(3):
        gqkv[:, n * D:(n + 1) * D] = gqv[(n + 1) * 128:(n + 2) * 128, :].astype(F32)
        copies[15 + n].start()
    gout[...] = gqv[0:128, :].astype(F32)
    copies[10].start()
    for n in range(1, 6):
        copies[n].wait()
        for m in ((n + 5,) if n < 5 else range(11, 15)):
            copies[m].start()
    for n in range(6, 18):
        copies[n].wait()


def fused(
    tokens, cotangent, live_items, qkv_weight, out_weight, up_weight, down_weight,
    gain_one, shift_one, gain_two, shift_two,
):
    rows_of = [v.reshape(1, D) for v in (gain_one, shift_one, gain_two, shift_two)]
    hbm = pl.BlockSpec(memory_space=pl.ANY)
    shape = jax.ShapeDtypeStruct
    outs = pl.pallas_call(
        layer_kernel,
        name="layer",
        out_shape=(
            shape((ROWS, D), BF), shape((ROWS, D), BF), shape((512, D), BF),
            shape((128, SHARD), F32), shape((SHARD, 128), F32), shape((8, 128), F32),
        ),
        in_specs=[hbm, hbm, pl.BlockSpec(memory_space=pltpu.SMEM)] + [hbm] * 8,
        out_specs=[hbm] * 6,
        scratch_shapes=[
            *[pltpu.VMEM((1, D), F32)] * 4,
            pltpu.VMEM((128, SHARD), F32), pltpu.VMEM((SHARD, 128), F32), pltpu.VMEM((8, 128), F32),
            pltpu.VMEM((D, 3 * D), BF), pltpu.VMEM((D, D), BF), pltpu.VMEM((D, FF), BF), pltpu.VMEM((FF, D), BF),
            pltpu.VMEM((ROWS, D), BF), pltpu.VMEM((PAD, D), BF), pltpu.VMEM((PAD, D), BF), pltpu.VMEM((PAD, D), BF),
            pltpu.VMEM((PAD, 3 * D), BF), pltpu.VMEM((PAD, 3 * 512), BF),
            pltpu.VMEM((D, 2 * PAD), BF), pltpu.VMEM((D, 2 * PAD), BF), pltpu.VMEM((D, 2 * PAD), BF),
            pltpu.VMEM((D, 2 * PAD), BF),
            pltpu.VMEM((16, TILE, TILE), BF), pltpu.VMEM((TILE, TILE), F32),
            pltpu.VMEM((ROWS, D), F32), pltpu.VMEM((ROWS, D), F32), pltpu.VMEM((ROWS, D), F32),
            pltpu.VMEM((PAD, SHARD), BF), pltpu.VMEM((PAD, SHARD), BF), pltpu.VMEM((PAD, 512), BF),
            pltpu.VMEM((8, 2, 2, 2, 2, 128, WIDE), BF),
            pltpu.VMEM((8, 2, 2, 2, 128, WIDE), BF), pltpu.VMEM((8, 2, 2, 128, WIDE), BF),
            pltpu.VMEM((8, 2, 128, WIDE), BF), pltpu.VMEM((8, 128, WIDE), BF),
            pltpu.VMEM((4, 8, D), F32), pltpu.VMEM((6, 8, D), F32), pltpu.VMEM((5, 8, D), F32),
            pltpu.SemaphoreType.DMA((N_SENT,)), pltpu.SemaphoreType.DMA((N_MSG,)), pltpu.SemaphoreType.DMA((25,)),
        ],
        compiler_params=pltpu.CompilerParams(
            collective_id=0, has_side_effects=True, vmem_limit_bytes=67_043_328
        ),
    )(tokens, cotangent, live_items, qkv_weight, out_weight, up_weight, down_weight, *rows_of)
    return pl.pallas_call(
        result_kernel,
        name="results",
        out_shape=(
            shape((ROWS, D), BF), shape((ROWS, D), BF), shape((128, 3 * D), F32), shape((128, D), F32),
            shape((128, SHARD), F32), shape((SHARD, 128), F32),
            shape((128,), F32), shape((128,), F32), shape((128,), F32), shape((128,), F32),
        ),
        in_specs=[hbm] * 6,
        out_specs=[hbm] * 10,
        scratch_shapes=[
            pltpu.VMEM((ROWS, D), BF), pltpu.VMEM((ROWS, D), BF), pltpu.VMEM((512, D), BF),
            pltpu.VMEM((128, SHARD), F32), pltpu.VMEM((SHARD, 128), F32), pltpu.VMEM((8, 128), F32),
            pltpu.VMEM((128, 3 * D), F32), pltpu.VMEM((128, D), F32), pltpu.SemaphoreType.DMA((18,)),
        ],
    )(*outs)


IN_SPECS = (
    P(("seq", "ff"), None), P(("seq", "ff"), None), P("seq"), P(), P(), P(None, "ff"), P("ff", None),
    P(), P(), P(), P(),
)
OUT_SPECS = (
    P(("seq", "ff"), None), P(("seq", "ff"), None), P("seq", None), P("seq", None), P("seq", "ff"),
    P("ff", "seq"), P("seq"), P("seq"), P("seq"), P("seq"),
)


def solution(mesh):
    body = fused if (mesh.shape["seq"], mesh.shape["ff"]) == (8, 4) else general
    return jax.shard_map(body, mesh=mesh, in_specs=IN_SPECS, out_specs=OUT_SPECS, check_vma=False)
```

```python
import jax
import jax.numpy as jnp
from jax import lax
from jax.experimental import pallas as pl
from jax.experimental.pallas import tpu as pltpu
from jax.sharding import PartitionSpec as P

HEADS = 8
HEAD_DIM = 128
ITEM_LEN = 15
BF = jnp.bfloat16
F32 = jnp.float32


def layer_norm(content_matrix, gain, shift):
    centre = content_matrix - jnp.mean(content_matrix, axis=-1, keepdims=True)
    spread = jnp.mean(centre * centre, axis=-1, keepdims=True)
    return centre * lax.rsqrt(spread + 1e-05) * gain + shift


def tile_allowed(tile_rows):
    position = jnp.arange(tile_rows, dtype=jnp.int32)
    same_item = position[:, None] // ITEM_LEN == position[None, :] // ITEM_LEN
    return same_item & (position[None, :] <= position[:, None])


def dot(a, b):
    return jnp.dot(a, b, preferred_element_type=F32)


def tiles_of(x, tile):
    return x.reshape(-1, tile, HEAD_DIM)


def scores_of(q, k, allowed):
    s = jnp.einsum("tqd,tkd->tqk", q, k, preferred_element_type=F32) * HEAD_DIM ** (-0.5)
    return jnp.where(allowed, s, -1e30)


def attend_forward(packed, tile):
    allowed = tile_allowed(tile)
    width = HEADS * HEAD_DIM
    mixed, saved = [], []
    for h in range(HEADS):
        q, k, v = (tiles_of(packed[:, p * width + h * HEAD_DIM:][:, :HEAD_DIM], tile) for p in range(3))
        probs = jax.nn.softmax(scores_of(q, k, allowed), axis=-1)
        o = jnp.einsum("tqk,tkd->tqd", probs.astype(BF), v, preferred_element_type=F32)
        mixed.append(o.astype(BF).reshape(-1, HEAD_DIM))
        saved.append(probs)
    return jnp.concatenate(mixed, axis=1), saved


def attend_backward(packed, saved, grad_mixed, tile):
    width = HEADS * HEAD_DIM
    scale = HEAD_DIM ** (-0.5)
    parts = ([], [], [])
    for h in range(HEADS):
        q, k, v = (tiles_of(packed[:, p * width + h * HEAD_DIM:][:, :HEAD_DIM], tile) for p in range(3))
        o = tiles_of(grad_mixed[:, h * HEAD_DIM:][:, :HEAD_DIM], tile)
        probs = saved[h]
        dp = jnp.einsum("tqd,tkd->tqk", o, v, preferred_element_type=F32)
        gv = jnp.einsum("tqk,tqd->tkd", probs.astype(BF), o, preferred_element_type=F32)
        gs = (probs * (dp - jnp.sum(probs * dp, axis=-1, keepdims=True))).astype(BF)
        gq = jnp.einsum("tqk,tkd->tqd", gs, k, preferred_element_type=F32) * scale
        gk = jnp.einsum("tqk,tqd->tkd", gs, q, preferred_element_type=F32) * scale
        for part, g in zip(parts, (gq, gk, gv)):
            part.append(g.astype(BF).reshape(-1, HEAD_DIM))
    return jnp.concatenate(parts[0] + parts[1] + parts[2], axis=1)


def general(
    tokens, cotangent, live_items, qkv_weight, out_weight, up_weight, down_weight,
    gain_one, shift_one, gain_two, shift_two,
):
    rows = tokens.shape[0]
    items = rows // ITEM_LEN
    tile = ITEM_LEN * (16 if items % 16 == 0 else 1)
    place = lax.axis_index("ff") * items + jnp.arange(rows, dtype=jnp.int32) // ITEM_LEN
    keep = (place < live_items[0]).astype(F32)[:, None]
    up_all = lax.all_gather(up_weight, "ff", axis=1, tiled=True)
    down_all = lax.all_gather(down_weight, "ff", axis=0, tiled=True)
    inputs = tokens.astype(F32)
    normed, norm_one_pull = jax.vjp(layer_norm, inputs, gain_one, shift_one)
    normed = normed.astype(BF)
    packed = dot(normed, qkv_weight).astype(BF)
    mixed, saved = attend_forward(packed, tile)
    middle = inputs + keep * dot(mixed, out_weight)
    normed_two, norm_two_pull = jax.vjp(layer_norm, middle, gain_two, shift_two)
    normed_two = normed_two.astype(BF)
    grad_out = cotangent.astype(F32)
    grad_branch = (keep * grad_out).astype(BF)
    pre = dot(normed_two, up_all)
    hidden = jax.nn.gelu(pre).astype(BF)
    layer_out = (middle + keep * dot(hidden, down_all)).astype(BF)
    grad_hidden = dot(grad_branch, down_all.T)
    grad_pre = jax.vjp(jax.nn.gelu, pre)[1](grad_hidden)[0].astype(BF)
    grad_down = dot(hidden.T, grad_branch).astype(BF)
    grad_up = dot(normed_two.T, grad_pre).astype(BF)
    grad_middle_norm, grad_gain_two, grad_shift_two = norm_two_pull(dot(grad_pre, up_all.T))
    grad_middle = grad_out + grad_middle_norm
    grad_attended = (keep * grad_middle).astype(BF)
    grad_out_weight = dot(mixed.T, grad_attended).astype(BF)
    grad_mixed = dot(grad_attended, out_weight.T).astype(BF)
    grad_packed = attend_backward(packed, saved, grad_mixed, tile)
    grad_qkv = dot(normed.T, grad_packed).astype(BF)
    grad_inputs, grad_gain_one, grad_shift_one = norm_one_pull(dot(grad_packed, qkv_weight.T))
    grad_tokens = (grad_middle + grad_inputs).astype(BF)

    def scatter(x, axis, dim):
        return lax.psum_scatter(x, axis, scatter_dimension=dim, tiled=True)

    grad_up = scatter(scatter(grad_up, "ff", 1), "seq", 0).astype(F32)
    grad_down = scatter(scatter(grad_down, "ff", 0), "seq", 1).astype(F32)
    shared = [
        lax.psum(scatter(g, "seq", 0), "ff").astype(F32)
        for g in (grad_qkv, grad_out_weight, grad_gain_one, grad_shift_one, grad_gain_two, grad_shift_two)
    ]
    return (layer_out, grad_tokens, shared[0], shared[1], grad_up, grad_down, *shared[2:])


MESH = pl.DeviceIdType.MESH
ROWS, PAD, D, FF, SHARD = 480, 512, 1024, 2048, 512
TILE = 240
WIDE = 256
STEP = 240
UP0, UP1, DN0, DN1, OUT, QS, KS, VS = range(8)
SUB = 2
OUT_AT = 0
LANES = WIDE // SUB
ORDER = (
    "xylh", "lyhx", "lxhy", "lxhy", "ylxh", "xlhy", "yxhl", "ylxh",
    "xlyh", "yxlh", "yxlh", "lyxh", "xlhy", "yxlh", "yxlh", "yxlh",
)
EYES = "xhly"
M_UPC, M_DNC = 0, 1
M_W = 2
M_MATE = 22
M_GBT, M_N2T, M_MXT, M_N1T, M_GA = 24, 25, 26, 27, 28
M_HID, M_GPR = 29, 31
M_PK = 33
M_VEC = 35
M_RED = 40
M_AGX = M_RED + 40 * SUB
M_AG = M_AGX + 4 * SUB
N_MSG = M_AG + 4
N_SENT = M_RED + 16 * SUB
WAYS = ("XYLPQ", "XYLD", "XYLPQ", "XYLD")
SCHED = {
    ("att", 0): (
        ("X", 0),
    ),
    ("att", 1): (
        ("X", 1),
    ),
    "n2t": (
        ("X", 2),
    ),
    ("sh", 0): (
        ("Y", 0), ("L", 0),
    ),
    ("bk", 1): (
        ("X", 3),
    ),
    ("sum", 0): (
        ("Y", 1), ("L", 1),
    ),
    ("sum", 1): (
        ("Y", 2), ("L", 2),
    ),
    "wup": (
        ("D", 1), ("P", 0), ("Q", 0), ("D", 3),
    ),
    ("sh", 3): (
        ("Y", 3), ("L", 3),
    ),
    "wdn": (
        ("P", 2), ("Q", 2),
    ),
    ("sum", 2): (
        ("R", 4, 0, 0), ("R", 1, 0, 0),
    ),
    "bup": (
        ("R", 6, 0, 0), ("R", 2, 0, 0),
    ),
    "ln2b": (
        ("R", 7, 0, 0), ("R", 3, 0, 0),
    ),
    ("pr", 0): (
        ("R", 4, 0, 1), ("R", 1, 0, 1), ("R", 5, 0, 0),
    ),
    "osum": (
        ("R", 6, 0, 1), ("R", 2, 0, 1),
    ),
    ("pr", 1): (
        ("R", 7, 0, 1), ("R", 3, 0, 1), ("R", 0, 0, 0),
    ),
    ("qs", 0): (
        ("R", 4, 1, 0), ("R", 1, 1, 0),
    ),
    ("qs", 1): (
        ("R", 5, 1, 0),
    ),
    "dwn": (
        ("R", 8, 0, 0),
    ),
    "fin": (
        ("R", 9, 0, 0), ("R", 7, 1, 0), ("R", 6, 1, 0),
    ),
    "gn1": (
        ("R", 0, 1, 0), ("R", 11, 0, 0), ("R", 2, 1, 0),
    ),
    "ln1b": (
        ("R", 1, 2, 0), ("R", 10, 0, 0), ("R", 3, 1, 0), ("R", 11, 0, 1),
    ),
    "tail": (
        ("R", 13, 0, 0), ("V", 0), ("R", 5, 2, 0), ("R", 14, 0, 0), ("R", 8, 1, 0), ("R", 12, 0, 0), ("R", 4, 2, 0),
        ("R", 6, 2, 0), ("R", 15, 0, 0), ("R", 0, 2, 0), ("R", 9, 1, 0), ("R", 2, 2, 0), ("R", 10, 0, 1),
        ("R", 7, 2, 0), ("R", 1, 3, 0), ("V", 1), ("R", 3, 2, 0), ("R", 13, 0, 1), ("R", 12, 1, 0), ("R", 6, 3, 0),
        ("R", 4, 3, 0), ("R", 10, 1, 0), ("R", 14, 0, 1), ("R", 0, 3, 0), ("R", 9, 2, 0), ("R", 7, 3, 0),
        ("R", 13, 1, 0), ("R", 15, 0, 1), ("R", 10, 2, 0), ("R", 12, 2, 0), ("R", 14, 1, 0), ("R", 11, 1, 0),
        ("R", 5, 3, 0), ("R", 13, 2, 0), ("R", 9, 3, 0), ("R", 8, 2, 0), ("R", 15, 1, 0), ("R", 2, 3, 0),
        ("R", 10, 3, 0), ("R", 14, 2, 0), ("V", 2), ("R", 11, 2, 0), ("R", 3, 3, 0), ("G", 1), ("R", 12, 3, 0),
        ("R", 13, 3, 0), ("G", 2), ("R", 15, 2, 0), ("R", 8, 3, 0), ("G", 4), ("V", 3), ("R", 14, 3, 0), ("G", 5),
        ("R", 11, 3, 0), ("G", 0), ("R", 15, 3, 0), ("G", 6), ("V", 4), ("G", 3), ("G", 7),
    ),
}


def dot_nt(a, b):
    return lax.dot_general(a, b, (((1,), (1,)), ((), ())), preferred_element_type=F32)


def dot_tn(a, b):
    return lax.dot_general(a, b, (((0,), (0,)), ((), ())), preferred_element_type=F32)


def layer_kernel(
    tok_h, cot_h, live, wq_h, wo_h, up_h, dn_h, g1_h, s1_h, g2_h, s2_h,
    lo_h, gt_h, gq_h, gup_h, gdn_h, vec_h,
    g1, s1, g2, s2, gup_o, gdn_o, vec_o,
    wq, wo, upa, dna, tok, gb, nb, mx, pk, pks, xgb, xn2, xmx, xn1, probs, mask, mid, gm, facc,
    hids, gprs, gas, gw, r0, r1, r2, r3, vsum, vbuf, vrecv, ssem, rsem, lsem,
):
    s, f = lax.axis_index("seq"), lax.axis_index("ff")
    bit = {"h": s // 4, "l": (s // 2) % 2, "y": s % 2, "x": f // 2, "c": f % 2}
    mate = {
        "h": (s + 4 - 8 * bit["h"], f), "l": (s + 2 - 4 * bit["l"], f), "y": (s + 1 - 2 * bit["y"], f),
        "x": (s, f + 2 - 4 * bit["x"]), "c": (s, f + 1 - 2 * bit["c"]),
        "lh": (s + 6 - 4 * bit["l"] - 8 * bit["h"], f),
    }
    x, c = bit["x"], bit["c"]

    def at(base, size, unit=128):
        return pl.ds(pl.multiple_of(base, unit), size)

    ga = xn2.at[0:PAD]

    def local(i, src, dst):
        return pltpu.make_async_copy(src, dst, lsem.at[i])

    loads = {
        0: (tok_h, tok), 1: (cot_h, gb.at[0:ROWS]), 3: (wo_h, wo), 4: (up_h, upa.at[:, 0:SHARD]),
        5: (dn_h, dna.at[0:SHARD]), 6: (cot_h, nb.at[0:ROWS]), 7: (wq_h, wq),
        8: (nb.at[0:ROWS], lo_h), 9: (tok, gt_h), 10: (gup_o, gup_h), 15: (gdn_o, gdn_h), 16: (vec_o, vec_h),
        17: (g1_h, g1), 18: (s1_h, s1), 19: (g2_h, g2), 20: (s2_h, s2),
        **{21 + n: (xgb.at[n * 128:(n + 1) * 128], gq_h.at[n * 128:(n + 1) * 128]) for n in range(4)},
    }

    def load(i):
        local(i, *loads[i]).start()

    def loaded(i):
        local(i, *loads[i]).wait()

    def wq_chunk(n):
        cols = at(n * 768, 768)
        return local(11 + n, wq_h.at[:, cols], wq.at[:, cols])

    def remote(i, to, src, dst, sent=None):
        return pltpu.make_async_remote_copy(
            src_ref=src, dst_ref=dst, send_sem=ssem.at[i if sent is None else sent], recv_sem=rsem.at[i],
            device_id=mate[to], device_id_type=MESH,
        )

    def region(k, way, slot):
        yb = bit["y"] if way in ("X", "L") else 1 - bit["y"]
        lb = bit["l"] if way in ("X", "Y") else 1 - bit["l"]
        size = 128 if k < 2 else 64
        start = (2 * yb + lb) * (2 * size) + (k % 2) * size
        if way in ("P", "Q"):
            size //= 2
            start = start + (size if way == "Q" else 0)
        rows = at(start, size, 32)
        if slot is None:
            return up_h.at[rows, :] if k < 2 else dn_h.at[rows, :]
        if k < 2:
            return upa.at[rows, slot * SHARD:(slot + 1) * SHARD]
        return dna.at[at(slot * SHARD + start, size, 32), :]

    def onward(k, way):
        yb = bit["y"] if way == "Q" else 1 - bit["y"]
        lb = bit["l"] if way == "P" else 1 - bit["l"]
        size = 64 if k < 2 else 32
        start = (2 * yb + lb) * (4 * size) + (k % 2) * (2 * size) + (size if way == "Q" else 0)
        if k < 2:
            return upa.at[at(start, size, 32), 2 * SHARD:3 * SHARD]
        return dna.at[at(2 * SHARD + start, size, 32), :]

    def weight(k, way):
        i = M_W + k * 5 + WAYS[k].index(way)
        if way in ("X", "D"):
            return remote(i, "x", region(k, way, None), region(k, way, 2))
        if way in ("Y", "L"):
            return remote(i, way.lower(), region(k, "X", 2), region(k, "X", 2))
        return remote(i, "l" if way == "P" else "y", onward(k, way), onward(k, way))

    def weight_mate(k, way):
        return remote(M_MATE + k // 2, "c", region(k, way, 2), region(k, way, 3))

    def weight_mates(m):
        if m == 0:
            return remote(M_MATE, "c", upa.at[:, 2 * SHARD:3 * SHARD], upa.at[:, 3 * SHARD:4 * SHARD])
        return remote(M_MATE + 1, "c", dna.at[2 * SHARD:3 * SHARD], dna.at[3 * SHARD:4 * SHARD])

    def relay(way, k):
        weight(k, way).wait()
        if way == "X":
            weight(k, "Y").start()
            weight(k, "L").start()
        elif way == "Y" and k % 2 == 0:
            weight(k, "P").start()
        elif way == "L" and k % 2 == 0:
            weight(k, "Q").start()
        weight_mate(k, way).start()

    def weight_c(which):
        if which == 0:
            return remote(M_UPC, "c", up_h, upa.at[:, SHARD:2 * SHARD])
        return remote(M_DNC, "c", dn_h, dna.at[SHARD:2 * SHARD])

    def turned(i, ref):
        return remote(i, "c", ref.at[:, 0:PAD], ref.at[:, PAD:2 * PAD])

    def own_hid(slot):
        return wq.at[0:PAD, at(slot * SHARD, SHARD)]

    def own_gpr(slot):
        return wq.at[PAD:2 * PAD, at(slot * SHARD, SHARD)]

    def hid_copy(g):
        return remote(M_HID + g, "c", own_hid(2 * g + 1), hids)

    def gpr_copy(g):
        return remote(M_GPR + g, "c", own_gpr(2 * g + 1), gprs)

    def ga_copy():
        return remote(M_GA, "c", ga.at[:, at((1 - c) * 512, 512)], gas)

    def pk_copy(n, xb, part):
        return remote(
            M_PK + n, "c", pk.at[:, at(part * D + (1 - c) * 512 + xb * WIDE, WIDE)],
            pks.at[:, at(part * 512 + xb * WIDE, WIDE)],
        )

    def pk_copies(n):
        return remote(M_PK + n, "c", pks.at[:, 0:3 * WIDE], pks.at[:, 0:3 * WIDE])

    landing = (r0, r1, r2, r3)

    def lanes_of(p):
        return slice((p % SUB) * LANES, (p % SUB + 1) * LANES)

    def bits_of(p):
        return {**bit, "x": 0} if p // SUB < OUT else bit

    def chosen(p, k, mine, xb=None):
        own, order, index = bits_of(p), ORDER[p], []
        for e in EYES:
            if e in order[:k]:
                index.append(own[e])
            elif e == order[k]:
                index.append(own[e] if mine else 1 - own[e])
            elif e == "x" and xb is not None:
                index.append(xb)
            else:
                index.append(slice(None))
        return index

    def red(p, k, xb=None, part=0):
        lead = (p // SUB,) if xb is None else (p // SUB, xb)
        rest = (slice(None), lanes_of(p))
        free = sum(isinstance(e, slice) for e in chosen(p, k, False, xb))
        return remote(
            M_RED + p * 5 + (k + 1 if k else part), ORDER[p][k],
            gw.at[(p // SUB, *chosen(p, k, False, xb), *rest)],
            landing[k].at[(*lead, *[slice(None)] * free, *rest)], M_RED + p * 2 + part,
        )

    def add(p, k, xb=None):
        index = chosen(p, k, True, xb)
        free = [n for n, e in enumerate(index) if isinstance(e, slice)]
        count = len(free)
        rest = (slice(None), lanes_of(p))

        def body(i, _):
            place = [(i // (1 << (count - 1 - n))) % 2 for n in range(count)]
            full = list(index)
            for n, e in zip(free, place):
                full[n] = e
            own = (p // SUB, *full, *rest)
            lead = (p // SUB, *place) if xb is None else (p // SUB, xb, *place)
            gw[own] = (gw[own].astype(F32) + landing[k][(*lead, *rest)].astype(F32)).astype(BF)
            return 0

        lax.fori_loop(0, 1 << count, body, 0)

    parts_done = {}

    def first(n, xb, part):
        for p in range(n * SUB, (n + 1) * SUB):
            if n == OUT:
                red(p, 0).start()
            elif ORDER[p][0] != "x":
                red(p, 0, xb, part).start()
            elif (part == 1) == (n < OUT):
                red(p, 0).start()

    def reduced(p, k, part):
        n = p // SUB
        if k == 0 and ORDER[p][0] != "x" and n != OUT:
            xb = part if n < OUT else (1 - x if part == 0 else x)
            red(p, 0, xb, part).wait()
            add(p, 0, xb)
            parts_done[p] = parts_done.get(p, 0) + 1
            if parts_done[p] == 2:
                red(p, 1).start()
        elif k < 3:
            red(p, k).wait()
            add(p, k)
            red(p, k + 1).start()
        else:
            own, rest = bits_of(p), (slice(None), lanes_of(p))
            total = gw[(n, *(own[e] for e in EYES), *rest)].astype(F32)
            red(p, 3).wait()
            total = total + r3[(n, *rest)].astype(F32)
            if n < OUT:
                cols = slice((n % 2) * WIDE + (p % SUB) * LANES, (n % 2) * WIDE + (p % SUB + 1) * LANES)
            if n in (UP0, UP1):
                gup_o[:, cols] = total
            elif n in (DN0, DN1):
                gdn_o[cols, :] = total.T
            else:
                q = p - OUT * SUB
                quarters(q, own_quarter)[...] = total.astype(BF)
                gather_c(q).start()
                gather_x(q).start()

    def quarters(q, n):
        row = (q // SUB) * 128
        return xgb.at[row:row + 128, at(n * WIDE + (q % SUB) * LANES, LANES)]

    own_quarter = 2 * c + x

    def gather_c(q):
        sent = M_W + q // SUB
        return remote(M_AG + q // SUB, "c", quarters(q, own_quarter), quarters(q, own_quarter), sent)

    def gather_x(q):
        sent = M_RED + (OUT * SUB + q) * 2
        return remote(M_AGX + q, "x", quarters(q, own_quarter), quarters(q, own_quarter), sent)

    def gather_f(q):
        other = 2 * c + 1 - x
        sent = M_W + q // SUB
        return remote(M_AG + q // SUB, "c", quarters(q, other), quarters(q, other), sent)

    def gathered(n):
        half = xgb.at[n * 128:(n + 1) * 128, 0:2 * WIDE]
        return remote(M_AG + n, "c", half, half, M_W + n)

    def vec(n):
        return remote(M_VEC + n, "cxylh"[n], vbuf.at[n], vrecv.at[n])

    def vec_step(n):
        vec(n).wait()
        vbuf[n + 1] = vbuf[n] + vrecv[n]
        if n < 4:
            vec(n + 1).start()

    def handle(event):
        kind = event[0]
        if kind == "R":
            reduced(*event[1:])
        elif kind == "G":
            gather_x(event[1]).wait()
            gather_f(event[1]).start()
        elif kind == "V":
            vec_step(event[1])
        else:
            relay(kind, event[1])

    def poll(name):
        for event in SCHED.get(name, ()):
            handle(event)

    def poll_at(name, i, places):
        for n in places:
            if (name, n) in SCHED:
                @pl.when(i == n)
                def _():
                    for event in SCHED[(name, n)]:
                        handle(event)

    limit = (live[0] - f * (ROWS // 15)) * 15

    def keep_of(r):
        rows = r * STEP + lax.broadcasted_iota(jnp.int32, (STEP, 1), 0)
        return jnp.where(rows < limit, 1.0, 0.0).astype(F32)

    def block(r):
        return pl.ds(pl.multiple_of(r * STEP, STEP), STEP)

    def centred(v):
        centre = v - jnp.mean(v, axis=-1, keepdims=True)
        rstd = lax.rsqrt(jnp.mean(centre * centre, axis=-1, keepdims=True) + 1e-05)
        return centre * rstd, rstd

    def turn(src, dst, j):
        cols = at(j * 128, 128)
        dst[cols, 0:PAD] = src[:, cols].T

    for i in (0, 17, 18):
        load(i)
    for n in range(4):
        wq_chunk(n).start()
    barrier = pltpu.get_barrier_semaphore()
    for e in "xylhc":
        pl.semaphore_signal(barrier, inc=1, device_id=mate[e], device_id_type=MESH)
    ki = lax.broadcasted_iota(jnp.int32, (TILE, TILE), 0)
    qi = lax.broadcasted_iota(jnp.int32, (TILE, TILE), 1)
    mask[...] = jnp.where((ki <= qi) & (ki >= qi - lax.rem(qi, 15)), 0.0, -1e30).astype(F32)
    nb[ROWS:PAD, :] = jnp.zeros((PAD - ROWS, D), BF)
    pl.semaphore_wait(barrier, 5)
    for k in range(4):
        weight(k, "X").start()
    for k in (1, 3):
        weight(k, "D").start()
    weight_c(0).start()
    weight_c(1).start()
    for ref in (gb, mx):
        ref[ROWS:PAD, :] = jnp.zeros((PAD - ROWS, D), BF)
    pk[ROWS:PAD, :] = jnp.zeros((PAD - ROWS, 3 * D), BF)
    vsum[...] = jnp.zeros(vsum.shape, F32)
    for i in (0, 17, 18):
        loaded(i)

    def norm_one(r, _):
        xhat, _r = centred(tok[block(r), :].astype(F32))
        nb[block(r), :] = (xhat * g1[...] + s1[...]).astype(BF)
        return 0

    lax.fori_loop(0, ROWS // STEP, norm_one, 0)
    poll("ln1")
    for i in (1, 3, 4, 5, 19, 20):
        load(i)

    def qkv(n, _):
        wq_chunk(n).wait()
        cols = at(n * 768, 768)
        pk[0:ROWS, cols] = jnp.dot(nb[0:ROWS, :], wq[:, cols], preferred_element_type=F32).astype(BF)
        for m in range(2):
            turn(nb, xn1, n * 2 + m)
        poll_at("qkv", n, range(4))
        return 0

    lax.fori_loop(0, 4, qkv, 0)
    turned(M_N1T, xn1).start()
    loaded(1)

    def mask_cot(r, _):
        gb[block(r), :] = (keep_of(r) * gb[block(r), :].astype(F32)).astype(BF)
        return 0

    lax.fori_loop(0, ROWS // STEP, mask_cot, 0)
    poll("msk")

    def attend(i, _):
        for h, t in ((i * 4 + n, t) for n in range(4) for t in range(2)):
            cols = [at(part * D + h * 128, 128) for part in range(3)]
            rows = slice(t * TILE, (t + 1) * TILE)
            sc = dot_nt(pk[rows, cols[1]], pk[rows, cols[0]]) * (128 ** -0.5) + mask[...]
            w = jnp.exp(sc - jnp.max(sc, axis=0, keepdims=True))
            p = (w * (1.0 / jnp.sum(w, axis=0, keepdims=True))).astype(BF)
            probs[h * 2 + t] = p
            mx[rows, at(h * 128, 128)] = dot_tn(p, pk[rows, cols[2]]).astype(BF)
        poll_at("att", i, range(2))
        return 0

    lax.fori_loop(0, 2, attend, 0)
    loaded(3)

    facc[...] = jnp.dot(mx[0:ROWS, :], wo[...], preferred_element_type=F32)
    for m in range(8):
        turn(gb, xgb, m)
        turn(mx, xmx, m)
    poll("prj")
    turned(M_GBT, xgb).start()

    loaded(19)
    loaded(20)

    def norm_two(r, _):
        m = tok[block(r), :].astype(F32) + keep_of(r) * facc[block(r), :]
        mid[block(r), :] = m
        xhat, _r = centred(m)
        nb[block(r), :] = (xhat * g2[...] + s2[...]).astype(BF)
        return 0

    lax.fori_loop(0, ROWS // STEP, norm_two, 0)
    poll("ln2")

    def turn_two(j, _):
        turn(nb, xn2, j)
        return 0

    lax.fori_loop(0, D // 128, turn_two, 0)
    poll("n2t")

    loaded(4)
    loaded(5)
    wq[ROWS:PAD, 0:FF] = jnp.zeros((PAD - ROWS, FF), BF)
    wq[PAD + ROWS:2 * PAD, 0:FF] = jnp.zeros((PAD - ROWS, FF), BF)

    def widen(j):
        cols = at(j * SHARD, SHARD)
        pre = jnp.dot(nb[0:ROWS, :], upa[:, cols], preferred_element_type=F32)
        sq = pre * pre
        t = jnp.tanh(0.7978845608028654 * pre * (1.0 + 0.044715 * sq))
        half = 0.5 * (1.0 + t)
        wq[0:ROWS, cols] = (pre * half).astype(BF)
        slope = half + 0.5 * pre * (1.0 - t * t) * (0.7978845608028654 * (1.0 + 0.134145 * sq))
        facc[:, at(lax.rem(j, 2) * SHARD, SHARD)] = slope

    def narrow_back(j):
        cols = at(j * SHARD, SHARD)
        gh = dot_nt(gb[0:ROWS, :], dna[cols, :])
        wq[PAD:PAD + ROWS, cols] = (gh * facc[:, at(lax.rem(j, 2) * SHARD, SHARD)]).astype(BF)

    def group(g, _):
        mine = at(2 * g * SHARD, SHARD)
        for m, work, copy in ((0, widen, hid_copy), (1, narrow_back, gpr_copy)):
            @pl.when(g == 0)
            def _():
                weight_c(m).wait()

            @pl.when(g == 1)
            def _():
                poll("wdn" if m else "wup")
                weight_mates(m).wait()
                if m == 0:
                    for p in (DN0, DN1, UP0, UP1):
                        first(p, 0, 0)

            def one(n, _):
                work(2 * g + 1 - n)

                @pl.when(n == 0)
                def _():
                    copy(g).start()

                poll_at("bk" if m else "sh", 2 * g + n, range(4))
                return 0

            lax.fori_loop(0, 2, one, 0)
            if m == 0:
                @pl.when(g == 0)
                def _():
                    turned(M_N2T, xn2).start()

        for m, copy, lhs, top, low, p in ((0, hid_copy, xgb, 0, hids, DN0), (1, gpr_copy, xn2, PAD, gprs, UP0)):
            copy(g).wait()

            @pl.when(g == 0)
            def _():
                turned((M_GBT, M_N2T)[m], lhs).wait()

            rhs = jnp.concatenate([wq[top:top + PAD, mine], low[...]], axis=0)
            total = jnp.dot(lhs[...], rhs, preferred_element_type=F32).astype(BF)
            for half in range(2):
                gw[p + half, g] = total[:, half * WIDE:(half + 1) * WIDE].reshape(2, 2, 2, 128, WIDE)

            @pl.when(g == 1)
            def _():
                for half in range(2):
                    first(p + half, 1, 1)

            poll_at("sum", 2 * g + m, (m, 2 + m))

        return 0

    lax.fori_loop(0, 2, group, 0)
    turned(M_MXT, xmx).start()
    load(6)

    facc[...] = dot_nt(wq[PAD:PAD + ROWS, 0:FF], upa[...])
    poll("bup")
    loaded(6)

    def row_sum(v):
        total = v[0:8]
        for n in range(1, STEP // 8):
            total = total + v[n * 8:(n + 1) * 8]
        return total

    def norm_back(v, gn, gain, n):
        xhat, rstd = centred(v)
        vsum[n] += row_sum(gn * xhat)
        vsum[n + 1] += row_sum(gn)
        e = gn * gain
        return rstd * (e - jnp.mean(e, axis=-1, keepdims=True) - xhat * jnp.mean(e * xhat, axis=-1, keepdims=True))

    def norm_two_back(r, _):
        total = nb[block(r), :].astype(F32) + norm_back(mid[block(r), :], facc[block(r), :], g2[...], 2)
        gm[block(r), :] = total
        ga[block(r), :] = (keep_of(r) * total).astype(BF)
        return 0

    ga[ROWS:PAD, :] = jnp.zeros((PAD - ROWS, D), BF)
    lax.fori_loop(0, ROWS // STEP, norm_two_back, 0)
    ga_copy().start()
    poll("ln2b")

    mx[0:ROWS, :] = dot_nt(ga[0:ROWS, :], wo[...]).astype(BF)
    poll("bout")

    def out_sums():
        rhs = jnp.concatenate([ga[:, at(c * 512, 512)], gas[...]], axis=0)
        total = jnp.dot(xmx[...], rhs, preferred_element_type=F32).astype(BF)
        for half in range(2):
            gw[OUT, half] = total[:, half * WIDE:(half + 1) * WIDE].reshape(2, 2, 2, 128, WIDE)

    def heads_back(i, _):
        h0 = 4 * (c + (1 - i) * (1 - 2 * c))
        for h, t in ((h0 + n, t) for n in range(4) for t in range(2)):
            cols = [at(part * D + h * 128, 128) for part in range(3)]
            rows = slice(t * TILE, (t + 1) * TILE)
            q, k, v = (pk[rows, col] for col in cols)
            o = mx[rows, at(h * 128, 128)]
            pb = probs[h * 2 + t]
            p = pb.astype(F32)
            dp = dot_nt(v, o)
            gs = (p * (dp - jnp.sum(p * dp, axis=0, keepdims=True))).astype(BF)
            gv = jnp.dot(pb, o, preferred_element_type=F32)
            gq = dot_tn(gs, k) * (128 ** -0.5)
            gk = jnp.dot(gs, q, preferred_element_type=F32) * (128 ** -0.5)
            for col, g in zip(cols, (gq, gk, gv)):
                pk[rows, col] = g.astype(BF)

        @pl.when(i == 0)
        def _():
            for n in range(2):
                for part in range(3):
                    pk_copy(n, 1 - x if n == 0 else x, part).start()

        poll_at("pr", i, range(2))

        @pl.when(i == OUT_AT)
        def _():
            turned(M_MXT, xmx).wait()
            ga_copy().wait()
            out_sums()
            first(OUT, None, 0)
            poll("osum")

        return 0

    lax.fori_loop(0, 2, heads_back, 0)
    turned(M_N1T, xn1).wait()

    def qkv_sums(later, _):
        xb = x + (1 - later) * (1 - 2 * x)
        for n in range(2):
            @pl.when(later == n)
            def _():
                pk_copies(n).wait()

        rhs = jnp.concatenate(
            [
                jnp.concatenate([pk[:, at(part * D + c * 512 + xb * WIDE, WIDE)] for part in range(3)], axis=1),
                jnp.concatenate([pks[:, at(part * 512 + xb * WIDE, WIDE)] for part in range(3)], axis=1),
            ],
            axis=0,
        )
        for m in range(2):
            total = jnp.dot(xn1[m * 512:(m + 1) * 512, :], rhs, preferred_element_type=F32).astype(BF)
            for part in range(3):
                gw[QS + part, xb, m] = total[:, part * WIDE:(part + 1) * WIDE].reshape(2, 2, 128, WIDE)
        for n in range(2):
            @pl.when(later == n)
            def _():
                for p in (QS, KS, VS):
                    first(p, 1 - x if n == 0 else x, n)
                poll(("qs", n))

        return 0

    lax.fori_loop(0, 2, qkv_sums, 0)

    facc[...] = jnp.dot(wq[0:ROWS, 0:FF], dna[...], preferred_element_type=F32)
    poll("dwn")
    load(7)

    def finish_out(r, _):
        nb[block(r), :] = (mid[block(r), :] + keep_of(r) * facc[block(r), :]).astype(BF)
        return 0

    lax.fori_loop(0, ROWS // STEP, finish_out, 0)
    load(8)
    poll("fin")
    loaded(7)

    facc[...] = dot_nt(pk[0:ROWS, :], wq[...])
    poll("gn1")

    def norm_one_back(r, _):
        total = gm[block(r), :] + norm_back(tok[block(r), :].astype(F32), facc[block(r), :], g1[...], 0)
        tok[block(r), :] = total.astype(BF)
        return 0

    lax.fori_loop(0, ROWS // STEP, norm_one_back, 0)
    load(9)
    vbuf[0] = jnp.concatenate(
        [jnp.sum(vsum[n], axis=0, keepdims=True) for n in range(4)] + [jnp.zeros((4, D), F32)], axis=0
    )
    vec(0).start()
    poll("ln1b")
    poll("tail")
    vec_o[...] = vbuf[5, :, at(s * 128, 128)]
    for i in (10, 15, 16):
        load(i)
    for n in range(4):
        gathered(n).wait()
        load(21 + n)
    for i in (8, 9, 10, 15, 16, 21, 22, 23, 24):
        loaded(i)


def result_kernel(*refs):
    lo, gt, gq, gup, gdn, vec = refs[:6]
    lo_o, gt_o, gqkv_o, gout_o, gup_o, gdn_o = refs[6:12]
    lov, gtv, gqv, gupv, gdnv, vecv, gqkv, gout, sem = refs[16:]
    halves = [slice(0, ROWS // 2), slice(ROWS // 2, ROWS)]
    moved = [(lo, lov, lo_o), (gt, gtv, gt_o)]
    pairs = [(gq, gqv)]
    pairs += [(src.at[h], mid.at[h]) for src, mid, _ in moved for h in halves]
    pairs += [(gup, gupv), (gdn, gdnv), (vec, vecv)]
    pairs += [(mid.at[h], dst.at[h]) for _, mid, dst in moved for h in halves]
    pairs += [(gupv, gup_o), (gdnv, gdn_o)]
    pairs += [(vecv.at[n], refs[12 + n]) for n in range(4)]
    pairs += [(gqkv.at[:, n * D:(n + 1) * D], gqkv_o.at[:, n * D:(n + 1) * D]) for n in range(3)]
    pairs += [(gout, gout_o)]
    copies = [pltpu.make_async_copy(a, b, sem.at[n]) for n, (a, b) in enumerate(pairs)]
    for n in range(8):
        copies[n].start()
    copies[0].wait()
    for n in range(3):
        gqkv[:, n * D:(n + 1) * D] = gqv[(n + 1) * 128:(n + 2) * 128, :].astype(F32)
        copies[18 + n].start()
    gout[...] = gqv[0:128, :].astype(F32)
    copies[21].start()
    for n in range(1, 8):
        copies[n].wait()
        for m in ((n + 7,) if n < 7 else range(14, 18)):
            copies[m].start()
    for n in range(8, 22):
        copies[n].wait()


def fused(
    tokens, cotangent, live_items, qkv_weight, out_weight, up_weight, down_weight,
    gain_one, shift_one, gain_two, shift_two,
):
    rows_of = [v.reshape(1, D) for v in (gain_one, shift_one, gain_two, shift_two)]
    hbm = pl.BlockSpec(memory_space=pl.ANY)
    shape = jax.ShapeDtypeStruct
    outs = pl.pallas_call(
        layer_kernel,
        name="layer",
        out_shape=(
            shape((ROWS, D), BF), shape((ROWS, D), BF), shape((512, D), BF),
            shape((128, SHARD), F32), shape((SHARD, 128), F32), shape((8, 128), F32),
        ),
        in_specs=[hbm, hbm, pl.BlockSpec(memory_space=pltpu.SMEM)] + [hbm] * 8,
        out_specs=[hbm] * 6,
        scratch_shapes=[
            *[pltpu.VMEM((1, D), F32)] * 4,
            pltpu.VMEM((128, SHARD), F32), pltpu.VMEM((SHARD, 128), F32), pltpu.VMEM((8, 128), F32),
            pltpu.VMEM((D, 3 * D), BF), pltpu.VMEM((D, D), BF), pltpu.VMEM((D, FF), BF), pltpu.VMEM((FF, D), BF),
            pltpu.VMEM((ROWS, D), BF), pltpu.VMEM((PAD, D), BF), pltpu.VMEM((PAD, D), BF), pltpu.VMEM((PAD, D), BF),
            pltpu.VMEM((PAD, 3 * D), BF), pltpu.VMEM((PAD, 3 * 512), BF),
            pltpu.VMEM((D, 2 * PAD), BF), pltpu.VMEM((D, 2 * PAD), BF), pltpu.VMEM((D, 2 * PAD), BF),
            pltpu.VMEM((D, 2 * PAD), BF),
            pltpu.VMEM((16, TILE, TILE), BF), pltpu.VMEM((TILE, TILE), F32),
            pltpu.VMEM((ROWS, D), F32), pltpu.VMEM((ROWS, D), F32), pltpu.VMEM((ROWS, D), F32),
            pltpu.VMEM((PAD, SHARD), BF), pltpu.VMEM((PAD, SHARD), BF), pltpu.VMEM((PAD, 512), BF),
            pltpu.VMEM((8, 2, 2, 2, 2, 128, WIDE), BF),
            pltpu.VMEM((8, 2, 2, 2, 128, WIDE), BF), pltpu.VMEM((8, 2, 2, 128, WIDE), BF),
            pltpu.VMEM((8, 2, 128, WIDE), BF), pltpu.VMEM((8, 128, WIDE), BF),
            pltpu.VMEM((4, 8, D), F32), pltpu.VMEM((6, 8, D), F32), pltpu.VMEM((5, 8, D), F32),
            pltpu.SemaphoreType.DMA((N_SENT,)), pltpu.SemaphoreType.DMA((N_MSG,)), pltpu.SemaphoreType.DMA((25,)),
        ],
        compiler_params=pltpu.CompilerParams(
            collective_id=0, has_side_effects=True, vmem_limit_bytes=67_043_328
        ),
    )(tokens, cotangent, live_items, qkv_weight, out_weight, up_weight, down_weight, *rows_of)
    return pl.pallas_call(
        result_kernel,
        name="results",
        out_shape=(
            shape((ROWS, D), BF), shape((ROWS, D), BF), shape((128, 3 * D), F32), shape((128, D), F32),
            shape((128, SHARD), F32), shape((SHARD, 128), F32),
            shape((128,), F32), shape((128,), F32), shape((128,), F32), shape((128,), F32),
        ),
        in_specs=[hbm] * 6,
        out_specs=[hbm] * 10,
        scratch_shapes=[
            pltpu.VMEM((ROWS, D), BF), pltpu.VMEM((ROWS, D), BF), pltpu.VMEM((512, D), BF),
            pltpu.VMEM((128, SHARD), F32), pltpu.VMEM((SHARD, 128), F32), pltpu.VMEM((8, 128), F32),
            pltpu.VMEM((128, 3 * D), F32), pltpu.VMEM((128, D), F32), pltpu.SemaphoreType.DMA((22,)),
        ],
    )(*outs)


IN_SPECS = (
    P(("seq", "ff"), None), P(("seq", "ff"), None), P("seq"), P(), P(), P(None, "ff"), P("ff", None),
    P(), P(), P(), P(),
)
OUT_SPECS = (
    P(("seq", "ff"), None), P(("seq", "ff"), None), P("seq", None), P("seq", None), P("seq", "ff"),
    P("ff", "seq"), P("seq"), P("seq"), P("seq"), P("seq"),
)


def solution(mesh):
    body = fused if (mesh.shape["seq"], mesh.shape["ff"]) == (8, 4) else general
    return jax.shard_map(body, mesh=mesh, in_specs=IN_SPECS, out_specs=OUT_SPECS, check_vma=False)
```
